32 devices in a mesh: dp: 16 (over z, y, x), tensor: 2 (over core).
Axes of the slice: x: 2, y: 2, z: 4, core: 2. Of those that a mesh axis runs over, the one named last changes fastest.
Arguments:
- activations: bfloat16 [24576, 768], P('dp'), may hold values from -6 to 6
- cotangent: bfloat16 [24576, 768], P('dp'), may hold values from -6 to 6
- token_weight: int32 [24576], P('dp'), may hold values from 1 to 4
- lengths: int32 [48], P('dp'), may hold values from 64 to 512, as said below
- step_count: int32 [1], replicated, may hold values from 1 to 20
- inward_weight: float32 [3, 768, 768], P(None, 'dp', 'tensor'), may hold values from -0.21875 to 0.21875
- output_weight: float32 [768, 768], P('tensor', 'dp'), may hold values from -2 to 2
- up_weight: float32 [768, 3072], P('dp', 'tensor'), may hold values from -0.21875 to 0.21875
- down_weight: float32 [3072, 768], P('tensor', 'dp'), may hold values from -0.109375 to 0.109375
- heads_bias: float32 [2, 48, 16], P(None, 'tensor', 'dp'), may hold values from -3 to 3
- hidden_bias: float32 [192, 16], P('tensor', 'dp'), may hold values from -3 to 3
- norm_vectors: float32 [6, 768], P(None, 'dp'), may hold values from -0.9 to 1.6
- inward_first: float32 [3, 768, 768], P(None, 'dp', 'tensor'), may hold values from -1792 to 1792
- output_first: float32 [768, 768], P('tensor', 'dp'), may hold values from -192 to 192
- up_first: float32 [768, 3072], P('dp', 'tensor'), may hold values from -512 to 512
- down_first: float32 [3072, 768], P('tensor', 'dp'), may hold values from -1024 to 1024
- heads_first: float32 [2, 48, 16], P(None, 'tensor', 'dp'), may hold values from -1792 to 1792
- hidden_first: float32 [192, 16], P('tensor', 'dp'), may hold values from -512 to 512
- norm_first: float32 [6, 768], P(None, 'dp'), may hold values from -1280 to 1280
- inward_second: float32 [3, 768, 768], P(None, 'dp', 'tensor'), may hold values from 98304 to 393216
- output_second: float32 [768, 768], P('tensor', 'dp'), may hold values from 1152 to 4608
- up_second: float32 [768, 3072], P('dp', 'tensor'), may hold values from 8847.36 to 35389.44
- down_second: float32 [3072, 768], P('tensor', 'dp'), may hold values from 29491.2 to 117964.8
- heads_second: float32 [2, 48, 16], P(None, 'tensor', 'dp'), may hold values from 98304 to 393216
- hidden_second: float32 [192, 16], P('tensor', 'dp'), may hold values from 8847.36 to 35389.44
- norm_second: float32 [6, 768], P(None, 'dp'), may hold values from 55296 to 221184
Outputs:
- layer_output: bfloat16 [24576, 768], P('dp')
- input_grad: float32 [24576, 768], P('dp')
- new_inward: float32 [3, 768, 768], P(None, 'dp', 'tensor')
- new_inward_first: float32 [3, 768, 768], P(None, 'dp', 'tensor')
- new_inward_second: float32 [3, 768, 768], P(None, 'dp', 'tensor')
- new_output: float32 [768, 768], P('tensor', 'dp')
- new_output_first: float32 [768, 768], P('tensor', 'dp')
- new_output_second: float32 [768, 768], P('tensor', 'dp')
- new_up: float32 [768, 3072], P('dp', 'tensor')
- new_up_first: float32 [768, 3072], P('dp', 'tensor')
- new_up_second: float32 [768, 3072], P('dp', 'tensor')
- new_down: float32 [3072, 768], P('tensor', 'dp')
- new_down_first: float32 [3072, 768], P('tensor', 'dp')
- new_down_second: float32 [3072, 768], P('tensor', 'dp')
- new_heads: float32 [2, 48, 16], P(None, 'tensor', 'dp')
- new_heads_first: float32 [2, 48, 16], P(None, 'tensor', 'dp')
- new_heads_second: float32 [2, 48, 16], P(None, 'tensor', 'dp')
- new_hidden: float32 [192, 16], P('tensor', 'dp')
- new_hidden_first: float32 [192, 16], P('tensor', 'dp')
- new_hidden_second: float32 [192, 16], P('tensor', 'dp')
- new_norm: float32 [6, 768], P(None, 'dp')
- new_norm_first: float32 [6, 768], P(None, 'dp')
- new_norm_second: float32 [6, 768], P(None, 'dp')
The draws below stay inside these ranges and needn't reach their ends.
Inputs may be any that keep to these rules, and one draw needn't show every extreme that they name: Sequence s holds lengths[s] real tokens followed by padding; some sequence is full and some has an eighth of 512.
All inputs are finite; a program needn't handle non-finite values.
Results may differ from the reference program's by a relative error of at most 0.018.
Values may be sent and summed in bfloat16 or wider, within the bound.
No kernel may reach another device: no remote copies, remote signals or barrier semaphores. Data moves between devices by JAX's collectives and lax.ppermute only.
A program may use at most 192 MiB of HBM per device.

```python
import math
import jax
import jax.numpy as jnp
from jax import lax

D = 768
HEADS = 12
HEAD_DIM = 64
FF = 3072
LEN = 512
SEQS = 48
TOKENS = 24576
N_DP = 16


def draw_lengths(key, part):
    short_len = jax.random.randint(jax.random.fold_in(key, 1), (SEQS,), LEN // 8, LEN // 2 + 1)
    picker = jax.random.randint(jax.random.fold_in(key, 2), (SEQS,), 0, 4)
    chosen = jnp.where(picker == 0, LEN, short_len)
    where_full = jax.random.randint(jax.random.fold_in(key, 3), (), 0, SEQS)
    offset = jax.random.randint(jax.random.fold_in(key, 4), (), 1, SEQS)
    where_short = (where_full + offset) % SEQS
    positions = jnp.arange(SEQS)
    chosen = jnp.where(positions == where_full, LEN, chosen)
    chosen = jnp.where(positions == where_short, LEN // 8, chosen)
    return chosen.astype(jnp.int32)


def draw_norm_vectors(key, part):
    base_draw = jax.random.truncated_normal(key, -3.0, 3.0, (6, D), jnp.float32)
    row_index = jnp.arange(6)[:, None]
    gain_rows = (row_index == 1) | (row_index == 4)
    return jnp.where(gain_rows, 1.0 + 0.2 * base_draw, 0.3 * base_draw).astype(jnp.float32)


def with_ends(values, stream_key, low, high):
    extent = values.shape
    spot = [jax.random.randint(jax.random.fold_in(stream_key, axis), (), 0, extent[axis]) for axis in range(len(extent))]
    values = values.at[tuple(spot)].set(low)
    longest = extent.index(max(extent))
    spot[longest] = (spot[longest] + 1) % extent[longest]
    return values.at[tuple(spot)].set(high)


def block_levels(key, shape, pieces, smallest, largest):
    loudness = 1.0
    for axis_at, blocks in pieces:
        draws = jax.random.uniform(jax.random.fold_in(jax.random.fold_in(key, 6), axis_at), (blocks,), jnp.float32, smallest / len(pieces), largest / len(pieces))
        loudness = loudness * jnp.repeat(jnp.exp(draws), shape[axis_at] // blocks).reshape((-1,) + (1,) * (len(shape) - 1 - axis_at))
    return loudness


def scatter_about(stream_key, shape, scale, limit, pieces=(), dtype=jnp.bfloat16):
    result = scale * jax.random.normal(stream_key, shape, jnp.float32)
    if pieces:
        result = result * block_levels(stream_key, shape, pieces, -0.22, 0.18)
    return jnp.clip(result, -limit, limit).astype(dtype)


def setup_inputs(seed: int = 0) -> dict:
    streams_of = jax.random.split(jax.random.key(seed), 27)
    activations = scatter_about(streams_of[0], (TOKENS, D), 1.0, 6.0, ((0, 16),))
    cotangent = scatter_about(streams_of[1], (TOKENS, D), 1.0, 6.0, ((0, 16),))
    token_weight = with_ends(jax.random.randint(streams_of[2], (TOKENS,), 1, 5), jax.random.fold_in(streams_of[2], 1), 1, 4).astype(jnp.int32)
    lengths = draw_lengths(jax.random.fold_in(streams_of[26], 71), 0)
    step_count = jax.random.randint(streams_of[4], (1,), 1, 21).astype(jnp.int32)
    inward_weight = scatter_about(streams_of[5], (3, D, D), D ** -0.5, 0.21875, ((1, 16), (2, 2)), jnp.float32)
    output_weight = scatter_about(streams_of[6], (D, D), (6 * D // LEN) ** -0.5, 2.0, ((0, 2), (1, 16)), jnp.float32)
    up_weight = scatter_about(streams_of[7], (D, FF), D ** -0.5, 0.21875, ((0, 16), (1, 2)), jnp.float32)
    down_weight = scatter_about(streams_of[8], (FF, D), FF ** -0.5, 0.109375, ((0, 2), (1, 16)), jnp.float32)
    heads_bias = scatter_about(streams_of[9], (2, D // N_DP, N_DP), 0.5, 3.0, ((1, 2), (2, 16)), jnp.float32)
    hidden_bias = scatter_about(streams_of[10], (FF // N_DP, N_DP), 0.5, 3.0, ((0, 2), (1, 16)), jnp.float32)
    norm_vectors = draw_norm_vectors(jax.random.fold_in(streams_of[26], 71), 0)
    inward_first = scatter_about(streams_of[12], (3, D, D), (2.0 * TOKENS ** 0.5), 1792.0, ((1, 16), (2, 2)), jnp.float32)
    output_first = scatter_about(streams_of[13], (D, D), (2.0 * (6 * TOKENS // LEN) ** 0.5), 192.0, ((0, 2), (1, 16)), jnp.float32)
    up_first = scatter_about(streams_of[14], (D, FF), (0.6 * TOKENS ** 0.5), 512.0, ((0, 16), (1, 2)), jnp.float32)
    down_first = scatter_about(streams_of[15], (FF, D), (1.1 * TOKENS ** 0.5), 1024.0, ((0, 2), (1, 16)), jnp.float32)
    heads_first = scatter_about(streams_of[16], (2, D // N_DP, N_DP), (2.0 * TOKENS ** 0.5), 1792.0, ((1, 2), (2, 16)), jnp.float32)
    hidden_first = scatter_about(streams_of[17], (FF // N_DP, N_DP), (0.6 * TOKENS ** 0.5), 512.0, ((0, 2), (1, 16)), jnp.float32)
    norm_first = scatter_about(streams_of[18], (6, D), (1.5 * TOKENS ** 0.5), 1280.0, ((1, 16),), jnp.float32)
    inward_second = jnp.clip(jnp.exp(math.log(393216.0) - 1.3862944 * jax.random.uniform(streams_of[19], (3, D, D), jnp.float32) ** block_levels(streams_of[19], (3, D, D), ((1, 16), (2, 2)), -0.2, 0.2)), 98304.0, 393216.0)
    output_second = jnp.clip(jnp.exp(math.log(4608.0) - 1.3862944 * jax.random.uniform(streams_of[20], (D, D), jnp.float32) ** block_levels(streams_of[20], (D, D), ((0, 2), (1, 16)), -0.2, 0.2)), 1152.0, 4608.0)
    up_second = jnp.clip(jnp.exp(math.log(35389.44) - 1.3862944 * jax.random.uniform(streams_of[21], (D, FF), jnp.float32) ** block_levels(streams_of[21], (D, FF), ((0, 16), (1, 2)), -0.2, 0.2)), 8847.36, 35389.44)
    down_second = jnp.clip(jnp.exp(math.log(117964.8) - 1.3862944 * jax.random.uniform(streams_of[22], (FF, D), jnp.float32) ** block_levels(streams_of[22], (FF, D), ((0, 2), (1, 16)), -0.2, 0.2)), 29491.2, 117964.8)
    heads_second = jnp.clip(jnp.exp(math.log(393216.0) - 1.3862944 * jax.random.uniform(streams_of[23], (2, D // N_DP, N_DP), jnp.float32) ** block_levels(streams_of[23], (2, D // N_DP, N_DP), ((1, 2), (2, 16)), -0.2, 0.2)), 98304.0, 393216.0)
    hidden_second = jnp.clip(jnp.exp(math.log(35389.44) - 1.3862944 * jax.random.uniform(streams_of[24], (FF // N_DP, N_DP), jnp.float32) ** block_levels(streams_of[24], (FF // N_DP, N_DP), ((0, 2), (1, 16)), -0.2, 0.2)), 8847.36, 35389.44)
    norm_second = jnp.clip(jnp.exp(math.log(221184.0) - 1.3862944 * jax.random.uniform(streams_of[25], (6, D), jnp.float32) ** block_levels(streams_of[25], (6, D), ((1, 16),), -0.2, 0.2)), 55296.0, 221184.0)
    return {"activations": activations, "cotangent": cotangent, "token_weight": token_weight, "lengths": lengths, "step_count": step_count, "inward_weight": inward_weight, "output_weight": output_weight, "up_weight": up_weight, "down_weight": down_weight, "heads_bias": heads_bias, "hidden_bias": hidden_bias, "norm_vectors": norm_vectors, "inward_first": inward_first, "output_first": output_first, "up_first": up_first, "down_first": down_first, "heads_first": heads_first, "hidden_first": hidden_first, "norm_first": norm_first, "inward_second": inward_second, "output_second": output_second, "up_second": up_second, "down_second": down_second, "heads_second": heads_second, "hidden_second": hidden_second, "norm_second": norm_second}


@jax.custom_vjp
def low(v):
    return lax.optimization_barrier(v.astype(jnp.bfloat16)).astype(jnp.float32)

@jax.custom_vjp
def low_back(v):
    return v

def low_keep(v):
    return (low(v), None)

def low_pass(kept, grad):
    return (grad,)

def back_keep(v):
    return (v, None)

def back_low(kept, grad):
    return (low(grad),)
low.defvjp(low_keep, low_pass)
low_back.defvjp(back_keep, back_low)
highest = lax.Precision.HIGHEST
norm_epsilon = 1e-12

def matmul(left, right):
    return jnp.dot(left, right, precision=highest, preferred_element_type=jnp.float32)

def normalize(total_in):
    average = lax.optimization_barrier(jnp.mean(total_in, axis=-1, keepdims=True))
    centred = total_in - average
    spread = lax.optimization_barrier(jnp.mean(centred * centred, axis=-1, keepdims=True))
    return centred * lax.rsqrt(spread + norm_epsilon)

def attend_one(queries, key_rows, values, length):
    score_scale = 1.0 / math.sqrt(HEAD_DIM)
    scores = jnp.einsum('qhd,khd->hqk', queries, key_rows, precision=highest) * score_scale
    scores = low_back(scores)
    live_mask = jnp.arange(LEN) < length
    scores = jnp.where(live_mask[None, None, :], scores, -jnp.inf)
    weights = low(jax.nn.softmax(scores, axis=-1))
    return jnp.einsum('hqk,khd->qhd', weights, values, precision=highest)

def attend_item(item_parts):
    return attend_one(item_parts[0], item_parts[1], item_parts[2], item_parts[3])

def forward(params, source, lengths_block):
    inward, outward, upward, downward, head_biases, hidden_biases, vectors = params
    row_count = source.shape[0]
    seq_count = row_count // LEN
    head_shape = (seq_count, LEN, HEADS, HEAD_DIM)
    queries = low_back(low(matmul(source, inward[0]) + head_biases[0]))
    key_rows = low_back(low(matmul(source, inward[1])))
    values = low_back(low(matmul(source, inward[2]) + head_biases[1]))
    context = lax.map(jax.checkpoint(attend_item), (queries.reshape(head_shape), key_rows.reshape(head_shape), values.reshape(head_shape), lengths_block))
    context = low_back(low(context.reshape(row_count, D)))
    branch = low_back(matmul(context, outward))
    first_sum = branch + vectors[0] + source
    normed = normalize(first_sum) * vectors[1] + vectors[2]
    hidden = low_back(matmul(low(normed), upward) + hidden_biases)
    active = low(jax.nn.gelu(hidden, approximate=False))
    down_sum = low_back(matmul(active, downward))
    second_sum = down_sum + vectors[3] + normed
    return normalize(second_sum) * vectors[4] + vectors[5]

def adamw(master, gradient, first_moment, second_moment, step_rate, decay_rate, first_correct, second_correct):
    first_new = 0.5 * first_moment + 0.5 * gradient
    second_new = 0.5 * second_moment + 0.5 * gradient * gradient
    moved = first_new / first_correct / (jnp.sqrt(second_new / second_correct) + 1e-08)
    return (master - step_rate * (moved + decay_rate * master), first_new, second_new)

def reference(activations, cotangent, token_weight, lengths, step_count, inward_weight, output_weight, up_weight, down_weight, heads_bias, hidden_bias, norm_vectors, inward_first, output_first, up_first, down_first, heads_first, hidden_first, norm_first, inward_second, output_second, up_second, down_second, heads_second, hidden_second, norm_second):
    masters = (inward_weight, output_weight, up_weight, down_weight, heads_bias, hidden_bias, norm_vectors)
    flat_masters = (inward_weight, output_weight, up_weight, down_weight, heads_bias.reshape(2, D), hidden_bias.reshape(FF), norm_vectors)
    params = tuple((master.astype(jnp.bfloat16).astype(jnp.float32) for master in flat_masters))
    live_mask = (jnp.arange(LEN)[None, :] < lengths[:, None]).reshape(TOKENS)
    scaled = cotangent.astype(jnp.float32) * (token_weight * live_mask.astype(jnp.int32)).astype(jnp.float32)[:, None]
    group_size = math.gcd(SEQS, max(1, 4096 // LEN))
    blocks = SEQS // group_size
    block_rows = group_size * LEN

    def one_block(running, item_parts):
        block_source, block_grad, block_lengths = item_parts

        def apply_layer(layer_params, layer_source):
            return forward(layer_params, layer_source, block_lengths)
        produced, pullback = jax.vjp(apply_layer, params, block_source)
        param_grads, source_grad = pullback(block_grad)
        running = jax.tree.map(jnp.add, running, param_grads)
        return (running, (produced.astype(jnp.bfloat16), source_grad))
    grad_start = jax.tree.map(jnp.zeros_like, params)
    grad_sums, (produced, source_grads) = lax.scan(one_block, grad_start, (activations.astype(jnp.float32).reshape(blocks, block_rows, D), scaled.reshape(blocks, block_rows, D), lengths.reshape(blocks, group_size)))
    layer_output = produced.reshape(TOKENS, D)
    input_grad = source_grads.reshape(TOKENS, D).astype(jnp.float32)
    step_value = step_count[0].astype(jnp.float32)
    first_correct = 1.0 - jnp.power(0.5, step_value)
    second_correct = 1.0 - jnp.power(0.5, step_value)
    plan = (step_value + 4.0) / 12.0
    rates = (D ** (-0.5), (6 * D // LEN) ** (-0.5), D ** (-0.5), FF ** (-0.5), 0.5, 0.5, 0.3)
    decays = (0.01, 0.01, 0.01, 0.01, 0.0, 0.0, 0.0)
    firsts = (inward_first, output_first, up_first, down_first, heads_first, hidden_first, norm_first)
    seconds = (inward_second, output_second, up_second, down_second, heads_second, hidden_second, norm_second)
    results = [layer_output, input_grad]
    for index_of in range(7):
        gradient = grad_sums[index_of].reshape(masters[index_of].shape)
        updated = adamw(masters[index_of], gradient, firsts[index_of], seconds[index_of], rates[index_of] * plan, decays[index_of], first_correct, second_correct)
        results.extend(updated)
    return (results[0], results[1], results[2], results[3], results[4], results[5], results[6], results[7], results[8], results[9], results[10], results[11], results[12], results[13], results[14], results[15], results[16], results[17], results[18], results[19], results[20], results[21], results[22])
```

```python
from functools import partial
import math

import jax
import jax.numpy as jnp
from jax import lax
from jax.experimental import pallas as pl
from jax.experimental.pallas import tpu as pltpu
from jax.sharding import PartitionSpec as P

D = 768
HEAD_DIM = 64
FF = 3072
LEN = 512
LANES = 128
HIDDEN_BLOCK = 768

norm_epsilon = 1e-12
low = jnp.bfloat16
full = jnp.float32


def dot_nn(left, right):
    return lax.dot_general(left, right, (((1,), (0,)), ((), ())), preferred_element_type=full)


def dot_nt(left, right):
    return lax.dot_general(left, right, (((1,), (1,)), ((), ())), preferred_element_type=full)


def column_sum(values):
    return jnp.sum(values, axis=0, keepdims=True)


def row_mean(values):
    return jnp.mean(values, axis=-1, keepdims=True)


def normalize(total_in):
    centred = total_in - row_mean(total_in)
    inverse = lax.rsqrt(row_mean(centred * centred) + norm_epsilon)
    return (centred * inverse, inverse)


def norm_back(incoming, normed, inverse, gain):
    scaled = incoming * gain
    return inverse * (scaled - row_mean(scaled) - normed * row_mean(scaled * normed))


def cost(flops, moved, exps=0):
    return pl.CostEstimate(flops=int(flops), bytes_accessed=int(moved), transcendentals=int(exps))


def params(**extra):
    return pltpu.CompilerParams(vmem_limit_bytes=58 * 1024 * 1024, **extra)


def shape(dims, kind):
    return jax.ShapeDtypeStruct(dims, kind)


def after(value, *others):
    return lax.optimization_barrier((value,) + others)[0]


def hop(value, offset, size):
    return lax.ppermute(value, "dp", [(d, d ^ offset) for d in range(size)])


def swap_cores(value):
    return lax.ppermute(value, "tensor", [(0, 1), (1, 0)])


def split_columns(width):
    return -(-width // (2 * LANES)) * LANES


def gather_planes(shard, size):
    found = [shard] + [hop(shard, 4 * k, size) for k in range(1, size // 4)]
    return found


def gather_pieces(found, size):
    stacked = jnp.stack(found)
    cut = split_columns(stacked.shape[2])
    own_a, own_b = lax.optimization_barrier((stacked[..., :cut], stacked[..., cut:]))
    y_a, x_b = hop(own_a, 2, size), hop(own_b, 1, size)
    x_a, y_b = hop(own_a, 1, size), hop(own_b, 2, size)
    xy_a, xy_b = hop(y_a, 1, size), hop(x_b, 2, size)
    return ((own_a, x_a, y_a, xy_a), (own_b, x_b, y_b, xy_b))


def place_kernel(me_ref, *refs):
    out_ref = refs[-1]
    rows = refs[0].shape[1]
    cut = refs[0].shape[2]
    for plane in range(4):
        for k in range(refs[0].shape[0]):
            start = pl.multiple_of((me_ref[0] ^ (4 * k + plane)) * rows, 16)
            out_ref[pl.ds(start, rows), :cut] = refs[plane][k]
            out_ref[pl.ds(start, rows), cut:] = refs[4 + plane][k]


def place(pieces, me):
    flat = pieces[0] + pieces[1]
    layers, rows, cut = flat[0].shape
    width = cut + flat[4].shape[2]
    total = 4 * layers * rows
    return pl.pallas_call(
        place_kernel,
        out_shape=shape((total, width), low),
        grid_spec=pltpu.PrefetchScalarGridSpec(
            num_scalar_prefetch=1,
            grid=(1,),
            in_specs=[pl.BlockSpec(piece.shape, lambda i, m: (0, 0, 0)) for piece in flat],
            out_specs=pl.BlockSpec((total, width), lambda i, m: (0, 0)),
        ),
        compiler_params=params(),
        cost_estimate=cost(0, 4 * total * width),
        name="place",
    )(me, *flat)


def reduce_start(pieces, size):
    sent_a, kept_a, sent_b, kept_b = pieces
    return (hop(sent_a, 1, size), kept_a, hop(sent_b, 2, size), kept_b)


def reduce_middle(state, size):
    got_a, kept_a, got_b, kept_b = state
    next_a, next_b = lax.optimization_barrier((kept_a[1] + got_a[1], kept_b[1] + got_b[1]))
    return (kept_a, got_a, hop(next_a, 2, size), kept_b, got_b, hop(next_b, 1, size))


def reduce_last(state, size):
    kept_a, got_a, more_a, kept_b, got_b, more_b = state

    def total(kept, got, more):
        return kept[0].astype(full) + got[0].astype(full) + more.astype(full)

    sum_a, sum_b = total(kept_a, got_a, more_a), total(kept_b, got_b, more_b)
    layers = sum_a.shape[0]
    outgoing = lax.optimization_barrier(
        tuple(
            jnp.concatenate([sum_a[k].astype(low), sum_b[k].astype(low)], axis=-1)
            for k in range(1, layers)
        )
    )
    arrived = [hop(piece, 4 * (k + 1), size) for k, piece in enumerate(outgoing)]
    own = jnp.concatenate([sum_a[0], sum_b[0]], axis=-1)
    return (own, arrived)


def reduce_sum(state):
    own, arrived = state
    for piece in arrived:
        own = own + piece.astype(full)
    return own


def attend_kernel(length_ref, x_ref, w_ref, bias_ref, qkv_ref, weight_ref, context_ref):
    length = length_ref[pl.program_id(1)]
    mixed = dot_nn(x_ref[...], w_ref[...])
    queries = (mixed[:, :LANES] + bias_ref[0:1, :]).astype(low)
    key_rows = mixed[:, LANES : 2 * LANES].astype(low)
    values_full = mixed[:, 2 * LANES :] + bias_ref[1:2, :]
    values = values_full.astype(low)
    qkv_ref[:, :LANES] = queries
    qkv_ref[:, LANES : 2 * LANES] = key_rows
    qkv_ref[:, 2 * LANES :] = values
    values_t = values_full.T.astype(low)
    rows = queries.shape[0]
    lane = lax.broadcasted_iota(jnp.int32, (rows, LANES), 1)
    live = lax.broadcasted_iota(jnp.int32, (rows, 1), 0) < length
    scaled = queries * (1.0 / math.sqrt(HEAD_DIM))
    parts = []
    for head in range(2):
        picked = jnp.where((lane >= HEAD_DIM) == bool(head), scaled, jnp.zeros_like(scaled))
        scores = jnp.where(live, dot_nt(key_rows, picked), -jnp.inf)
        grown = jnp.exp(scores - jnp.max(scores, axis=0, keepdims=True))
        weights = (grown * (1.0 / jnp.sum(grown, axis=0, keepdims=True))).astype(low)
        weight_ref[0, head] = weights
        parts.append(dot_nn(values_t[head * HEAD_DIM : (head + 1) * HEAD_DIM, :], weights))
    context_ref[...] = jnp.concatenate(parts, axis=0).T.astype(low)


def attend(lengths, source, inward, biases):
    count = source.shape[0] // LEN
    groups = biases.shape[1] // LANES
    rows = source.shape[0]
    width = 3 * LANES
    return pl.pallas_call(
        attend_kernel,
        out_shape=(
            shape((rows, groups * width), low),
            shape((groups * count, 2, LEN, LEN), low),
            shape((rows, groups * LANES), low),
        ),
        grid_spec=pltpu.PrefetchScalarGridSpec(
            num_scalar_prefetch=1,
            grid=(groups, count),
            in_specs=[
                pl.BlockSpec((LEN, D), lambda g, s, n: (s, 0)),
                pl.BlockSpec((D, width), lambda g, s, n: (0, g)),
                pl.BlockSpec((2, LANES), lambda g, s, n: (0, g)),
            ],
            out_specs=(
                pl.BlockSpec((LEN, width), lambda g, s, n: (s, g)),
                pl.BlockSpec((1, 2, LEN, LEN), lambda g, s, n: (g * count + s, 0, 0, 0)),
                pl.BlockSpec((LEN, LANES), lambda g, s, n: (s, g)),
            ),
        ),
        compiler_params=params(),
        cost_estimate=cost(
            2 * rows * D * groups * width + 8 * groups * count * LEN * LEN * LANES,
            groups * count * 2 * LEN * LEN * 2,
            groups * count * 2 * LEN * LEN,
        ),
        name="attend",
    )(lengths, source, inward, biases)


def attend_back_kernel(qkv_ref, weight_ref, grad_ref, out_ref, sum_ref):
    @pl.when(pl.program_id(1) == 0)
    def _():
        sum_ref[...] = jnp.zeros_like(sum_ref)

    queries = qkv_ref[:, :LANES]
    key_rows = qkv_ref[:, LANES : 2 * LANES]
    values = qkv_ref[:, 2 * LANES :]
    grads = grad_ref[...]
    keys_t = key_rows.astype(full).T.astype(low)
    rows = queries.shape[0]
    lane = lax.broadcasted_iota(jnp.int32, (rows, LANES), 1)
    score_scale = 1.0 / math.sqrt(HEAD_DIM)
    query_parts, key_parts, value_parts = [], [], []
    for head in range(2):
        picked = jnp.where((lane >= HEAD_DIM) == bool(head), grads, jnp.zeros_like(grads))
        weights = weight_ref[0, head]
        wide = weights.astype(full)
        mixed = wide * dot_nt(values, picked)
        score_grads = (mixed - wide * jnp.sum(mixed, axis=0, keepdims=True)).astype(low)
        value_parts.append(dot_nn(weights, grads))
        key_parts.append(dot_nn(score_grads, queries))
        query_parts.append(
            dot_nn(keys_t[head * HEAD_DIM : (head + 1) * HEAD_DIM, :], score_grads)
        )
    first = lane < HEAD_DIM
    query_grads = (jnp.concatenate(query_parts, axis=0).T * score_scale).astype(low)
    key_grads = (jnp.where(first, key_parts[0], key_parts[1]) * score_scale).astype(low)
    value_grads = jnp.where(first, value_parts[0], value_parts[1]).astype(low)
    out_ref[:, :LANES] = query_grads
    out_ref[:, LANES : 2 * LANES] = key_grads
    out_ref[:, 2 * LANES :] = value_grads
    sum_ref[0:1, :] += column_sum(query_grads.astype(full))
    sum_ref[1:2, :] += column_sum(value_grads.astype(full))


def attend_back(qkv, weights, grads, group):
    rows = qkv.shape[0]
    count = rows // LEN
    width = 3 * LANES
    return pl.pallas_call(
        attend_back_kernel,
        out_shape=(shape((rows, width), low), shape((2, LANES), full)),
        grid=(1, count),
        in_specs=[
            pl.BlockSpec((LEN, width), lambda g, s: (s, group)),
            pl.BlockSpec((1, 2, LEN, LEN), lambda g, s: (group * count + s, 0, 0, 0)),
            pl.BlockSpec((LEN, LANES), lambda g, s: (s, group)),
        ],
        out_specs=(
            pl.BlockSpec((LEN, width), lambda g, s: (s, 0)),
            pl.BlockSpec((2, LANES), lambda g, s: (0, 0)),
        ),
        compiler_params=params(),
        cost_estimate=cost(
            16 * count * LEN * LEN * LANES, count * 2 * LEN * LEN * 2 + 4 * rows * width
        ),
        name="attend_back",
    )(qkv, weights, grads)


def outward_kernel(context_ref, w_ref, out_ref):
    out_ref[...] = dot_nt(context_ref[...], w_ref[...]).astype(low)


def outward_part(context, outward, item):
    width = context.shape[1]
    return pl.pallas_call(
        outward_kernel,
        out_shape=shape((LEN, D), low),
        grid=(1,),
        in_specs=[
            pl.BlockSpec((LEN, width), lambda i: (item, 0)),
            pl.BlockSpec((D, width), lambda i: (0, 0)),
        ],
        out_specs=pl.BlockSpec((LEN, D), lambda i: (0, 0)),
        compiler_params=params(),
        cost_estimate=cost(2 * LEN * D * width, 2 * (LEN * D + LEN * width + D * width)),
        name="outward",
    )(context, outward)


def expand_kernel(
    mine_ref, other_ref, x_ref, vector_ref, bias_ref, up_ref, down_ref,
    active_in, slope_in, middle_in, normed_in, inverse_in,
    part_ref, active_ref, slope_ref, middle_ref, normed_ref, inverse_ref, total_ref, held_ref,
):
    step = pl.program_id(0)

    @pl.when(step == 0)
    def _():
        summed = (
            mine_ref[...].astype(full)
            + other_ref[...].astype(full)
            + vector_ref[0:1, :]
            + x_ref[...].astype(full)
        )
        normed, inverse = normalize(summed)
        normed_ref[...] = normed
        inverse_ref[...] = inverse
        held = (normed * vector_ref[1:2, :] + vector_ref[2:3, :]).astype(low)
        held_ref[...] = held
        middle_ref[...] = held

    hidden = dot_nn(held_ref[...], up_ref[...]) + bias_ref[...]
    half = 0.5 + 0.5 * lax.erf(hidden * 0.7071067811865476)
    active = (hidden * half).astype(low)
    active_ref[...] = active
    slope_ref[...] = (
        half + hidden * 0.3989422804014327 * jnp.exp(-0.5 * hidden * hidden)
    ).astype(low)
    part = dot_nt(active, down_ref[...])

    @pl.when(step == 0)
    def _():
        total_ref[...] = part

    @pl.when(step > 0)
    def _():
        total_ref[...] += part

    @pl.when(step == pl.num_programs(0) - 1)
    def _():
        part_ref[...] = total_ref[...].astype(low)


any_spec = pl.BlockSpec(memory_space=pl.ANY)


def expand(mine, other, source, vectors, hidden_bias, upward, downward, held, item):
    rows, hidden = source.shape[0], upward.shape[1]
    block = HIDDEN_BLOCK
    fixed = pl.BlockSpec((LEN, D), lambda j: (0, 0))
    row = pl.BlockSpec((LEN, D), lambda j: (item, 0))
    wide = pl.BlockSpec((LEN, block), lambda j: (item, j))
    weight = pl.BlockSpec((D, block), lambda j: (0, j))
    outs = (
        shape((LEN, D), low),
        shape((rows, hidden), low),
        shape((rows, hidden), low),
        shape((rows, D), low),
        shape((rows, D), full),
        shape((rows, 1), full),
    )
    first = held is None
    kernel = expand_kernel
    if first:
        kernel = lambda *refs: expand_kernel(*refs[:7], *([None] * 5), *refs[7:])
    return pl.pallas_call(
        kernel,
        out_shape=outs,
        grid=(hidden // block,),
        in_specs=[
            fixed,
            fixed,
            row,
            pl.BlockSpec(vectors.shape, lambda j: (0, 0)),
            pl.BlockSpec((1, block), lambda j: (0, j)),
            weight,
            weight,
        ]
        + ([] if first else [any_spec] * 5),
        out_specs=(fixed, wide, wide, row, row, pl.BlockSpec((LEN, 1), lambda j: (item, 0))),
        scratch_shapes=[pltpu.VMEM((LEN, D), full), pltpu.VMEM((LEN, D), low)],
        input_output_aliases={} if first else {7 + i: 1 + i for i in range(5)},
        compiler_params=params(),
        cost_estimate=cost(
            4 * LEN * D * hidden, 4 * D * hidden + 4 * LEN * hidden, 2 * LEN * hidden
        ),
        name="expand",
    )(mine, other, source, vectors, hidden_bias, upward, downward, *(() if first else held))


def contract_kernel(
    mine_ref, other_ref, normed_ref, cotangent_ref, scale_ref, vector_ref, slope_ref,
    up_ref, down_ref, out_in, wide_in, low_in, hidden_in,
    part_ref, sum_ref, hidden_sum_ref, out_ref, wide_ref, low_ref, hidden_ref,
    total_ref, held_ref,
):
    step = pl.program_id(0)

    @pl.when(step == 0)
    def _():
        middle = normed_ref[...] * vector_ref[1:2, :] + vector_ref[2:3, :]
        summed = (
            mine_ref[...].astype(full) + other_ref[...].astype(full) + vector_ref[3:4, :] + middle
        )
        normed, inverse = normalize(summed)
        out_ref[...] = (normed * vector_ref[4:5, :] + vector_ref[5:6, :]).astype(low)
        incoming = cotangent_ref[...].astype(full) * scale_ref[...]
        second = norm_back(incoming, normed, inverse, vector_ref[4:5, :])
        sum_ref[0:1, :] = column_sum(second)
        sum_ref[1:2, :] = column_sum(incoming * normed)
        sum_ref[2:3, :] = column_sum(incoming)
        wide_ref[...] = second
        held = second.astype(low)
        held_ref[...] = held
        low_ref[...] = held

    hidden_grad = (dot_nn(held_ref[...], down_ref[...]) * slope_ref[...].astype(full)).astype(low)
    hidden_ref[...] = hidden_grad
    hidden_sum_ref[...] = column_sum(hidden_grad.astype(full))
    part = dot_nt(hidden_grad, up_ref[...])

    @pl.when(step == 0)
    def _():
        total_ref[...] = part

    @pl.when(step > 0)
    def _():
        total_ref[...] += part

    @pl.when(step == pl.num_programs(0) - 1)
    def _():
        part_ref[...] = total_ref[...].astype(low)


def contract(mine, other, normed, cotangent, scale, vectors, slope, upward, downward, held, item):
    rows, hidden = slope.shape
    block = HIDDEN_BLOCK
    fixed = pl.BlockSpec((LEN, D), lambda j: (0, 0))
    row = pl.BlockSpec((LEN, D), lambda j: (item, 0))
    wide = pl.BlockSpec((LEN, block), lambda j: (item, j))
    weight = pl.BlockSpec((D, block), lambda j: (0, j))
    outs = (
        shape((LEN, D), low),
        shape((3, D), full),
        shape((1, hidden), full),
        shape((rows, D), low),
        shape((rows, D), full),
        shape((rows, D), low),
        shape((rows, hidden), low),
    )
    first = held is None
    kernel = contract_kernel
    if first:
        kernel = lambda *refs: contract_kernel(*refs[:9], *([None] * 4), *refs[9:])
    return pl.pallas_call(
        kernel,
        out_shape=outs,
        grid=(hidden // block,),
        in_specs=[
            fixed,
            fixed,
            row,
            row,
            pl.BlockSpec((LEN, 1), lambda j: (item, 0)),
            pl.BlockSpec(vectors.shape, lambda j: (0, 0)),
            wide,
            weight,
            weight,
        ]
        + ([] if first else [any_spec] * 4),
        out_specs=(
            fixed,
            pl.BlockSpec((3, D), lambda j: (0, 0)),
            pl.BlockSpec((1, block), lambda j: (0, j)),
            row,
            row,
            row,
            wide,
        ),
        scratch_shapes=[pltpu.VMEM((LEN, D), full), pltpu.VMEM((LEN, D), low)],
        input_output_aliases={} if first else {9 + i: 3 + i for i in range(4)},
        compiler_params=params(),
        cost_estimate=cost(4 * LEN * D * hidden, 4 * D * hidden + 4 * LEN * hidden),
        name="contract",
    )(
        mine, other, normed, cotangent, scale, vectors, slope, upward, downward,
        *(() if first else held),
    )


def first_back_kernel(
    mine_ref, other_ref, second_ref, normed_ref, inverse_ref, vector_ref, w_ref,
    wide_in, low_in, grad_in, sum_ref, wide_ref, low_ref, grad_ref,
):
    incoming = mine_ref[...].astype(full) + other_ref[...].astype(full) + second_ref[...]
    normed = normed_ref[...]
    first = norm_back(incoming, normed, inverse_ref[...], vector_ref[1:2, :])
    sum_ref[0:1, :] = column_sum(first)
    sum_ref[1:2, :] = column_sum(incoming * normed)
    sum_ref[2:3, :] = column_sum(incoming)
    wide_ref[...] = first
    held = first.astype(low)
    low_ref[...] = held
    grad_ref[...] = dot_nn(held, w_ref[...]).astype(low)


def first_back(mine, other, second, normed, inverse, vectors, outward, held, item):
    rows, width = second.shape[0], outward.shape[1]
    fixed = pl.BlockSpec((LEN, D), lambda j: (0, 0))
    row = pl.BlockSpec((LEN, D), lambda j: (item, 0))
    first = held is None
    kernel = first_back_kernel
    if first:
        kernel = lambda *refs: first_back_kernel(*refs[:7], *([None] * 3), *refs[7:])
    return pl.pallas_call(
        kernel,
        out_shape=(
            shape((3, D), full),
            shape((rows, D), full),
            shape((rows, D), low),
            shape((rows, width), low),
        ),
        grid=(1,),
        in_specs=[
            fixed,
            fixed,
            row,
            row,
            pl.BlockSpec((LEN, 1), lambda j: (item, 0)),
            pl.BlockSpec(vectors.shape, lambda j: (0, 0)),
            pl.BlockSpec((D, width), lambda j: (0, 0)),
        ]
        + ([] if first else [any_spec] * 3),
        out_specs=(
            pl.BlockSpec((3, D), lambda j: (0, 0)),
            row,
            row,
            pl.BlockSpec((LEN, width), lambda j: (item, 0)),
        ),
        input_output_aliases={} if first else {7 + i: 1 + i for i in range(3)},
        compiler_params=params(),
        cost_estimate=cost(2 * LEN * D * width, 20 * LEN * D),
        name="first_back",
    )(mine, other, second, normed, inverse, vectors, outward, *(() if first else held))


def source_kernel(*refs):
    grads, weights, out_ref = refs[:-2], refs[-2], refs[-1]
    width = 3 * LANES
    total = None
    for group, grad_ref in enumerate(grads):
        part = dot_nt(grad_ref[...], weights[:, group * width : (group + 1) * width])
        total = part if total is None else total + part
    out_ref[...] = total.astype(low)


def source_part(grads, inward, item):
    width = 3 * LANES
    groups = len(grads)
    return pl.pallas_call(
        source_kernel,
        out_shape=shape((LEN, D), low),
        grid=(1,),
        in_specs=[pl.BlockSpec((LEN, width), lambda i: (item, 0)) for _ in grads]
        + [pl.BlockSpec((D, groups * width), lambda i: (0, 0))],
        out_specs=pl.BlockSpec((LEN, D), lambda i: (0, 0)),
        compiler_params=params(),
        cost_estimate=cost(2 * LEN * D * width * groups, 2 * (LEN + D) * width * groups),
        name="source",
    )(*grads, inward)


def transpose_into(left_ref, turned_ref):
    for start in range(0, left_ref.shape[0], LEN):
        turned_ref[:, start : start + LEN] = (
            left_ref[start : start + LEN, :].astype(full).T.astype(low)
        )


def weight_grad_kernel(cut_blocks, me_ref, left_ref, right_ref, *refs):
    turned_ref, total_ref = refs[-2:]
    step = pl.program_id(0)

    @pl.when(step == 0)
    def _():
        transpose_into(left_ref, turned_ref)

    if cut_blocks is None:
        refs[0][...] = dot_nn(turned_ref[...], right_ref[...])
        return
    total_ref[...] = dot_nn(turned_ref[...], right_ref[...])
    sent_a, kept_a, sent_b, kept_b = refs[:4]
    rows = sent_a.shape[2]
    layers = sent_a.shape[1]

    def spread(sent, kept, bit):
        for plane in range(4):
            other = plane >> 1 if bit == 0 else plane & 1
            target = sent if (plane >> bit) & 1 else kept
            for k in range(layers):
                start = pl.multiple_of((me_ref[0] ^ (4 * k + plane)) * rows, 8)
                target[other, k] = total_ref[pl.ds(start, rows), :].astype(low)

    @pl.when(step < cut_blocks)
    def _():
        spread(sent_a, kept_a, 0)

    @pl.when(step >= cut_blocks)
    def _():
        spread(sent_b, kept_b, 1)


def weight_grad(left, right, me, size):
    tokens, width = right.shape
    block = 256 if width % 512 == 0 else LANES
    layers, rows = size // 4, D // size
    cut = split_columns(width)
    fast = me is not None
    cut_blocks = cut // block if fast else None
    last = width // block - 1
    if fast:
        piece = (2, layers, rows)

        def spec_a():
            return pl.BlockSpec(
                piece + (block,), lambda j, m: (0, 0, 0, jnp.minimum(j, cut_blocks - 1))
            )

        def spec_b():
            return pl.BlockSpec(
                piece + (block,), lambda j, m: (0, 0, 0, jnp.maximum(j - cut_blocks, 0))
            )

        outs = (
            shape(piece + (cut,), low),
            shape(piece + (cut,), low),
            shape(piece + (width - cut,), low),
            shape(piece + (width - cut,), low),
        )
        out_specs = (spec_a(), spec_a(), spec_b(), spec_b())
    else:
        outs = (shape((D, width), full),)
        out_specs = (pl.BlockSpec((D, block), lambda j, m: (0, j)),)
        me = jnp.zeros((1,), jnp.int32)
    return pl.pallas_call(
        partial(weight_grad_kernel, cut_blocks),
        out_shape=outs,
        grid_spec=pltpu.PrefetchScalarGridSpec(
            num_scalar_prefetch=1,
            grid=(last + 1,),
            in_specs=[
                pl.BlockSpec((tokens, D), lambda j, m: (0, 0)),
                pl.BlockSpec((tokens, block), lambda j, m: (0, j)),
            ],
            out_specs=out_specs,
            scratch_shapes=[pltpu.VMEM((D, tokens), low), pltpu.VMEM((D, block), full)],
        ),
        compiler_params=params(),
        cost_estimate=cost(2 * tokens * D * width, 2 * (tokens * D + tokens * width + D * width)),
        name="weight_grad",
    )(me, left, right)


def adamw(master, gradient, first_moment, second_moment, step_rate, decay_rate, correct):
    first_new = 0.5 * first_moment + 0.5 * gradient
    second_new = 0.5 * second_moment + 0.5 * gradient * gradient
    moved = first_new / correct / (jnp.sqrt(second_new / correct) + 1e-08)
    return (master - step_rate * (moved + decay_rate * master), first_new, second_new)


def per_device(
    activations,
    cotangent,
    token_weight,
    lengths,
    step_count,
    inward_weight,
    output_weight,
    up_weight,
    down_weight,
    heads_bias,
    hidden_bias,
    norm_vectors,
    *moments,
):
    size = lax.axis_size("dp")
    rows, width = inward_weight.shape[1], inward_weight.shape[2]
    hidden_width = up_weight.shape[1]
    groups = width // LANES
    tokens = activations.shape[0]
    count = tokens // LEN
    fast = size == 16 and rows % 16 == 0
    me = lax.axis_index("dp").astype(jnp.int32).reshape(1) if fast else None

    small = jnp.concatenate(
        [heads_bias.reshape(-1), hidden_bias.reshape(-1), norm_vectors.reshape(-1)]
    )
    per_row = small.shape[0] // rows
    small_block = jnp.pad(small.reshape(rows, per_row), ((0, 0), (0, LANES - per_row)))
    inward_shard = jnp.concatenate(
        [
            inward_weight.reshape(3, rows, groups, LANES)
            .transpose(1, 2, 0, 3)
            .reshape(rows, 3 * width),
            small_block,
        ],
        axis=1,
    ).astype(low)
    outward_shard = output_weight.T.astype(low)
    upward_shard = up_weight.astype(low)
    downward_shard = down_weight.T.astype(low)
    shards = (inward_shard, outward_shard, upward_shard, downward_shard)

    if fast:
        gathered = []
        gate = None
        for shard in shards:
            if gate is not None:
                shard = after(shard, *gate)
            found = gather_planes(shard, size)
            gate = found[1:]
            gathered.append(place(gather_pieces(found, size), me))
    else:
        gathered = [lax.all_gather(shard, "dp", axis=0, tiled=True) for shard in shards]
    inward, outward, upward, downward = gathered

    smalls = inward[:, 3 * width : 3 * width + per_row].astype(full).reshape(size, -1)
    heads_size, hidden_size = heads_bias.size, hidden_bias.size
    head_biases = (
        smalls[:, :heads_size].reshape(size, 2, -1).transpose(1, 2, 0).reshape(2, width)
    )
    hidden_biases = smalls[:, heads_size : heads_size + hidden_size].T.reshape(1, hidden_width)
    vectors = (
        smalls[:, heads_size + hidden_size :].reshape(size, 6, rows).transpose(1, 0, 2)
    ).reshape(6, D)

    live = lax.broadcasted_iota(jnp.int32, (count, LEN), 1) < lengths[:, None]
    scale = (token_weight.reshape(count, LEN) * live.astype(jnp.int32)).astype(full)
    scale = scale.reshape(tokens, 1)

    qkv, weights, context = attend(lengths, activations, inward, head_biases)
    mine = [outward_part(context, outward, item) for item in range(count)]
    other = [swap_cores(part) for part in mine]
    held = None
    mine_down = []
    for item in range(count):
        part, *held = expand(
            mine[item], other[item], activations, vectors, hidden_biases, upward, downward,
            held, item,
        )
        mine_down.append(part)
    active, slope, middle, normed, inverse = held
    other_down = [swap_cores(part) for part in mine_down]
    held = None
    mine_middle, second_sums, hidden_sums = [], [], []
    for item in range(count):
        part, sums, hidden_sum, *held = contract(
            mine_down[item], other_down[item], normed, cotangent, scale, vectors, slope,
            upward, downward, held, item,
        )
        mine_middle.append(part)
        second_sums.append(sums)
        hidden_sums.append(hidden_sum)
    output_rows, second_grad, second_low, hidden_grad = held
    other_middle = [swap_cores(part) for part in mine_middle]

    def reduced(left, right):
        pieces = weight_grad(left, right, me, size)
        if not fast:
            return lax.psum_scatter(pieces[0], "dp", scatter_dimension=0, tiled=True)
        state = reduce_last(reduce_middle(reduce_start(pieces, size), size), size)
        return reduce_sum(state)

    downward_grad = reduced(second_low, active)
    upward_grad = reduced(middle, hidden_grad)
    held = None
    first_sums = []
    for item in range(count):
        sums, *held = first_back(
            mine_middle[item], other_middle[item], second_grad, normed, inverse, vectors,
            outward, held, item,
        )
        first_sums.append(sums)
    first_grad, first_low, context_grad = held
    outward_grad = reduced(first_low, context)
    stacked, head_sums, inward_grads = [], [], []
    for group in range(groups):
        grads, sums = attend_back(qkv, weights, context_grad, group)
        stacked.append(grads)
        head_sums.append(sums)
        inward_grads.append(reduced(activations, grads))
    mine_source = [source_part(stacked, inward, item) for item in range(count)]
    other_source = [swap_cores(part) for part in mine_source]
    input_grad = (
        jnp.concatenate(
            [a.astype(full) + b.astype(full) for a, b in zip(mine_source, other_source)]
        )
        + first_grad
    )

    head_grad = jnp.concatenate(head_sums, axis=1)
    norm_grad = jnp.concatenate([sum(first_sums), sum(second_sums)])
    outgoing = jnp.concatenate(
        [
            head_grad.reshape(2, -1, size).transpose(2, 0, 1).reshape(size, -1),
            sum(hidden_sums).reshape(-1, size).T,
            norm_grad.reshape(6, size, rows).transpose(1, 0, 2).reshape(size, -1),
        ],
        axis=1,
    )
    if fast:
        order = lax.iota(jnp.int32, size) ^ me
        onehot = (order[:, None] == lax.iota(jnp.int32, size)[None, :]).astype(full)
        turned = jnp.dot(onehot, outgoing, precision=lax.Precision.HIGHEST)
        turned = turned.reshape(size // 4, 2, 2, -1)
        kept = turned[:, :, 0] + hop(turned[:, :, 1], 1, size)
        kept = kept[:, 0] + hop(kept[:, 1], 2, size)
        small_grad = kept[0]
        for k in range(1, size // 4):
            small_grad = small_grad + hop(kept[k], 4 * k, size)
    else:
        small_grad = lax.psum_scatter(outgoing, "dp", scatter_dimension=0, tiled=True)
    small_grad = small_grad.reshape(-1)

    inward_grad = jnp.stack(
        [
            jnp.concatenate(
                [grad[:, kind * LANES : (kind + 1) * LANES] for grad in inward_grads], axis=1
            )
            for kind in range(3)
        ]
    )
    grads = (
        inward_grad,
        outward_grad.T,
        upward_grad,
        downward_grad.T,
        small_grad[:heads_size].reshape(heads_bias.shape),
        small_grad[heads_size : heads_size + hidden_size].reshape(hidden_bias.shape),
        small_grad[heads_size + hidden_size :].reshape(norm_vectors.shape),
    )

    step_value = step_count[0].astype(full)
    correct = 1.0 - jnp.power(0.5, step_value)
    plan = (step_value + 4.0) / 12.0
    rates = (D ** (-0.5), (6 * D // LEN) ** (-0.5), D ** (-0.5), FF ** (-0.5), 0.5, 0.5, 0.3)
    decays = (0.01, 0.01, 0.01, 0.01, 0.0, 0.0, 0.0)
    masters = (
        inward_weight,
        output_weight,
        up_weight,
        down_weight,
        heads_bias,
        hidden_bias,
        norm_vectors,
    )
    results = [output_rows, input_grad]
    for at in range(7):
        results.extend(
            adamw(
                masters[at],
                grads[at],
                moments[at],
                moments[7 + at],
                rates[at] * plan,
                decays[at],
                correct,
            )
        )
    return tuple(results)


def solution(mesh):
    matrices = (
        P(None, "dp", "tensor"),
        P("tensor", "dp"),
        P("dp", "tensor"),
        P("tensor", "dp"),
        P(None, "tensor", "dp"),
        P("tensor", "dp"),
        P(None, "dp"),
    )
    in_specs = (
        (P("dp", None), P("dp", None), P("dp"), P("dp"), P()) + matrices + matrices + matrices
    )
    out_specs = (P("dp", None), P("dp", None)) + tuple(
        spec for spec in matrices for _ in range(3)
    )
    return jax.shard_map(
        per_device, mesh=mesh, in_specs=in_specs, out_specs=out_specs, check_vma=False
    )
```

```python
from functools import partial
import math

import jax
import jax.numpy as jnp
from jax import lax
from jax.experimental import pallas as pl
from jax.experimental.pallas import tpu as pltpu
from jax.sharding import PartitionSpec as P

D = 768
HEAD_DIM = 64
FF = 3072
LEN = 512
LANES = 128
ROWS = 256
COST_SHARE = 1

norm_epsilon = 1e-12
low = jnp.bfloat16
full = jnp.float32


def dot_nn(left, right):
    return lax.dot_general(left, right, (((1,), (0,)), ((), ())), preferred_element_type=full)


def dot_nt(left, right):
    return lax.dot_general(left, right, (((1,), (1,)), ((), ())), preferred_element_type=full)


def column_sum(values):
    return jnp.sum(values, axis=0, keepdims=True)


def row_mean(values):
    return jnp.mean(values, axis=-1, keepdims=True)


def normalize(total_in):
    centred = total_in - row_mean(total_in)
    inverse = lax.rsqrt(row_mean(centred * centred) + norm_epsilon)
    return (centred * inverse, inverse)


def norm_back(incoming, normed, inverse, gain):
    scaled = incoming * gain
    return inverse * (scaled - row_mean(scaled) - normed * row_mean(scaled * normed))


def cost(flops, moved, exps=0):
    return pl.CostEstimate(
        flops=int(flops / COST_SHARE),
        bytes_accessed=int(moved / COST_SHARE),
        transcendentals=int(exps / COST_SHARE),
    )


def params(mebibytes=32):
    return pltpu.CompilerParams(vmem_limit_bytes=mebibytes * 1024 * 1024)


def shape(dims, kind):
    return jax.ShapeDtypeStruct(dims, kind)


def after(value, *others):
    return lax.optimization_barrier((value,) + others)[0]


def after_all(values, *others):
    return lax.optimization_barrier(tuple(values) + others)[: len(values)]


def hop(value, offset, size):
    return lax.ppermute(value, "dp", [(d, d ^ offset) for d in range(size)])


def swap_cores(value):
    return lax.ppermute(value, "tensor", [(0, 1), (1, 0)])


def split_columns(width):
    return -(-width // (2 * LANES)) * LANES


def gather_planes(shard, size):
    found = [shard] + [hop(shard, 4 * k, size) for k in range(1, size // 4)]
    return found


def split_halves(found):
    stacked = jnp.stack(found)
    cut = split_columns(stacked.shape[2])
    return lax.optimization_barrier((stacked[..., :cut], stacked[..., cut:]))


def gather_near(own, size):
    return (hop(own[0], 2, size), hop(own[1], 1, size))


def gather_pairs(own, near):
    return lax.optimization_barrier(
        (jnp.concatenate([own[0], near[0]]), jnp.concatenate([own[1], near[1]]))
    )


def gather_far(pairs, size):
    return (hop(pairs[0], 1, size), hop(pairs[1], 2, size))


def place_kernel(me_ref, pair_a, far_a, pair_b, far_b, out_ref):
    layers, rows, cut = pair_a.shape
    layers //= 2
    sources = (
        (pair_a, 0, pair_b, 0),
        (far_a, 0, pair_b, layers),
        (pair_a, layers, far_b, 0),
        (far_a, layers, far_b, layers),
    )
    for plane, (left, left_at, right, right_at) in enumerate(sources):
        for k in range(layers):
            start = pl.multiple_of((me_ref[0] ^ (4 * k + plane)) * rows, 16)
            out_ref[pl.ds(start, rows), :cut] = left[left_at + k]
            out_ref[pl.ds(start, rows), cut:] = right[right_at + k]


def place(pairs, far, me):
    flat = (pairs[0], far[0], pairs[1], far[1])
    layers, rows, cut = pairs[0].shape
    width = cut + pairs[1].shape[2]
    total = 2 * layers * rows
    return pl.pallas_call(
        place_kernel,
        out_shape=shape((total, width), low),
        grid_spec=pltpu.PrefetchScalarGridSpec(
            num_scalar_prefetch=1,
            grid=(1,),
            in_specs=[pl.BlockSpec(piece.shape, lambda i, m: (0, 0, 0)) for piece in flat],
            out_specs=pl.BlockSpec((total, width), lambda i, m: (0, 0)),
        ),
        compiler_params=params(24),
        cost_estimate=cost(0, 4 * total * width),
        name="place",
    )(me, *flat)


def turn_kernel(source_ref, out_ref):
    out_ref[...] = source_ref[...].astype(full).T.astype(low)


def turn(source):
    rows, width = source.shape
    return pl.pallas_call(
        turn_kernel,
        out_shape=shape((width, rows), low),
        grid=(rows // LEN,),
        in_specs=[pl.BlockSpec((LEN, width), lambda i: (i, 0))],
        out_specs=pl.BlockSpec((width, LEN), lambda i: (0, i)),
        compiler_params=params(16),
        cost_estimate=cost(0, 4 * rows * width),
        name="turn",
    )(source)


def reduce_total(kept, got, more):
    return kept[0].astype(full) + got[0].astype(full) + more.astype(full)


def reduce_outgoing(sums):
    layers = sums[0].shape[0]
    outgoing = tuple(
        jnp.concatenate([total[k].astype(low) for total in sums], axis=-1)
        for k in range(1, layers)
    )
    own = jnp.concatenate([total[0] for total in sums], axis=-1)
    return lax.optimization_barrier((own,) + outgoing)


def reduce_planes(outgoing, size):
    return [hop(piece, 4 * (k + 1), size) for k, piece in enumerate(outgoing)]


def reduce_sum(own, arrived):
    for piece in arrived:
        own = own + piece.astype(full)
    return own


def attend_kernel(length_ref, x_ref, w_ref, bias_ref, qkv_ref, weight_ref, context_ref):
    length = length_ref[pl.program_id(0)]
    mixed = dot_nn(x_ref[...], w_ref[...])
    queries = (mixed[:, :LANES] + bias_ref[0:1, :]).astype(low)
    key_rows = mixed[:, LANES : 2 * LANES].astype(low)
    values_full = mixed[:, 2 * LANES :] + bias_ref[1:2, :]
    values = values_full.astype(low)
    qkv_ref[:, :LANES] = queries
    qkv_ref[:, LANES : 2 * LANES] = key_rows
    qkv_ref[:, 2 * LANES :] = values
    values_t = values_full.T.astype(low)
    rows = queries.shape[0]
    lane = lax.broadcasted_iota(jnp.int32, (rows, LANES), 1)
    live = lax.broadcasted_iota(jnp.int32, (rows, 1), 0) < length
    scaled = queries * (1.0 / math.sqrt(HEAD_DIM))
    parts = []
    for head in range(2):
        picked = jnp.where((lane >= HEAD_DIM) == bool(head), scaled, jnp.zeros_like(scaled))
        scores = jnp.where(live, dot_nt(key_rows, picked), -jnp.inf)
        grown = jnp.exp(scores - jnp.max(scores, axis=0, keepdims=True))
        weights = (grown * (1.0 / jnp.sum(grown, axis=0, keepdims=True))).astype(low)
        weight_ref[0, head] = weights
        parts.append(dot_nn(values_t[head * HEAD_DIM : (head + 1) * HEAD_DIM, :], weights))
    context_ref[...] = jnp.concatenate(parts, axis=0).T.astype(low)


def attend(lengths, source, inward, biases, group):
    rows = source.shape[0]
    count = rows // LEN
    width = 3 * LANES
    return pl.pallas_call(
        attend_kernel,
        out_shape=(
            shape((rows, width), low),
            shape((count, 2, LEN, LEN), low),
            shape((rows, LANES), low),
        ),
        grid_spec=pltpu.PrefetchScalarGridSpec(
            num_scalar_prefetch=1,
            grid=(count,),
            in_specs=[
                pl.BlockSpec((LEN, D), lambda s, n: (s, 0)),
                pl.BlockSpec((D, width), lambda s, n: (0, group)),
                pl.BlockSpec((2, LANES), lambda s, n: (0, group)),
            ],
            out_specs=(
                pl.BlockSpec((LEN, width), lambda s, n: (s, 0)),
                pl.BlockSpec((1, 2, LEN, LEN), lambda s, n: (s, 0, 0, 0)),
                pl.BlockSpec((LEN, LANES), lambda s, n: (s, 0)),
            ),
        ),
        compiler_params=params(),
        cost_estimate=cost(
            2 * rows * D * width + 8 * count * LEN * LEN * LANES,
            count * 2 * LEN * LEN * 2,
            count * 2 * LEN * LEN,
        ),
        name="attend",
    )(lengths, source, inward, biases)


def attend_back_kernel(qkv_ref, weight_ref, grad_ref, out_ref, sum_ref):
    @pl.when(pl.program_id(0) == 0)
    def _():
        sum_ref[...] = jnp.zeros_like(sum_ref)

    queries = qkv_ref[:, :LANES]
    key_rows = qkv_ref[:, LANES : 2 * LANES]
    values = qkv_ref[:, 2 * LANES :]
    grads = grad_ref[...]
    keys_t = key_rows.astype(full).T.astype(low)
    rows = queries.shape[0]
    lane = lax.broadcasted_iota(jnp.int32, (rows, LANES), 1)
    score_scale = 1.0 / math.sqrt(HEAD_DIM)
    query_parts, key_parts, value_parts = [], [], []
    for head in range(2):
        picked = jnp.where((lane >= HEAD_DIM) == bool(head), grads, jnp.zeros_like(grads))
        weights = weight_ref[0, head]
        wide = weights.astype(full)
        mixed = wide * dot_nt(values, picked)
        score_grads = (mixed - wide * jnp.sum(mixed, axis=0, keepdims=True)).astype(low)
        value_parts.append(dot_nn(weights, grads))
        key_parts.append(dot_nn(score_grads, queries))
        query_parts.append(
            dot_nn(keys_t[head * HEAD_DIM : (head + 1) * HEAD_DIM, :], score_grads)
        )
    first = lane < HEAD_DIM
    query_grads = (jnp.concatenate(query_parts, axis=0).T * score_scale).astype(low)
    key_grads = (jnp.where(first, key_parts[0], key_parts[1]) * score_scale).astype(low)
    value_grads = jnp.where(first, value_parts[0], value_parts[1]).astype(low)
    out_ref[:, :LANES] = query_grads
    out_ref[:, LANES : 2 * LANES] = key_grads
    out_ref[:, 2 * LANES :] = value_grads
    sum_ref[0:1, :] += column_sum(query_grads.astype(full))
    sum_ref[1:2, :] += column_sum(value_grads.astype(full))


def attend_back(qkv, weights, grads, group):
    rows = qkv.shape[0]
    count = rows // LEN
    width = 3 * LANES
    return pl.pallas_call(
        attend_back_kernel,
        out_shape=(shape((rows, width), low), shape((2, LANES), full)),
        grid=(count,),
        in_specs=[
            pl.BlockSpec((LEN, width), lambda s: (s, 0)),
            pl.BlockSpec((1, 2, LEN, LEN), lambda s: (s, 0, 0, 0)),
            pl.BlockSpec((LEN, LANES), lambda s: (s, group)),
        ],
        out_specs=(
            pl.BlockSpec((LEN, width), lambda s: (s, 0)),
            pl.BlockSpec((2, LANES), lambda s: (0, 0)),
        ),
        compiler_params=params(),
        cost_estimate=cost(
            16 * count * LEN * LEN * LANES, count * 2 * LEN * LEN * 2 + 4 * rows * width
        ),
        name="attend_back",
    )(qkv, weights, grads)


def outward_kernel(*refs):
    contexts, w_ref, out_ref = refs[:-2], refs[-2], refs[-1]
    context = jnp.concatenate([ref[...] for ref in contexts], axis=1)
    out_ref[...] = dot_nt(context, w_ref[...]).astype(low)


def outward_part(contexts, mid, outward_at, item):
    width = len(contexts) * LANES
    steps = LEN // ROWS
    return pl.pallas_call(
        outward_kernel,
        out_shape=shape((LEN, D), low),
        grid=(steps,),
        in_specs=[
            pl.BlockSpec((ROWS, LANES), lambda i: (item * steps + i, 0)) for _ in contexts
        ]
        + [pl.BlockSpec((D, width), lambda i: (0, outward_at // width))],
        out_specs=pl.BlockSpec((ROWS, D), lambda i: (i, 0)),
        compiler_params=params(16),
        cost_estimate=cost(2 * LEN * D * width, 2 * (LEN * D + LEN * width + D * width)),
        name="outward",
    )(*contexts, mid)


def gelu_parts(hidden):
    half = 0.5 + 0.5 * lax.erf(hidden * 0.7071067811865476)
    slope = half + hidden * 0.3989422804014327 * jnp.exp(-0.5 * hidden * hidden)
    return ((hidden * half).astype(low), slope.astype(low))


any_spec = pl.BlockSpec(memory_space=pl.ANY)


def chained(kernel, before, count):
    return lambda *refs: kernel(*refs[:before], *refs[before + count :])


def expand_first_kernel(
    mine_ref, other_ref, x_ref, vector_ref, bias_ref, up_ref, down_ref,
    total_ref, active_ref, slope_ref, middle_ref, normed_ref, inverse_ref,
):
    summed = (
        mine_ref[...].astype(full)
        + other_ref[...].astype(full)
        + vector_ref[0:1, :]
        + x_ref[...].astype(full)
    )
    normed, inverse = normalize(summed)
    normed_ref[...] = normed
    inverse_ref[...] = inverse
    held = (normed * vector_ref[1:2, :] + vector_ref[2:3, :]).astype(low)
    middle_ref[...] = held
    active, slope = gelu_parts(dot_nn(held, up_ref[...]) + bias_ref[...])
    active_ref[...] = active
    slope_ref[...] = slope
    total_ref[...] = dot_nt(active, down_ref[...])


def expand_first(mine, other, source, vectors, hidden_bias, mid, held, item):
    rows, hidden = source.shape[0], hidden_bias.shape[1]
    block = hidden // 2
    steps = LEN // ROWS
    fixed = pl.BlockSpec((ROWS, D), lambda i: (i, 0))
    row = pl.BlockSpec((ROWS, D), lambda i: (item * steps + i, 0))
    wide = pl.BlockSpec((ROWS, block), lambda i: (item * steps + i, 0))
    outs = (
        shape((LEN, D), full),
        shape((rows, hidden), low),
        shape((rows, hidden), low),
        shape((rows, D), low),
        shape((rows, D), full),
        shape((rows, 1), full),
    )
    held = held or ()
    return pl.pallas_call(
        chained(expand_first_kernel, 7, len(held)),
        out_shape=outs,
        grid=(steps,),
        in_specs=[
            fixed,
            fixed,
            row,
            pl.BlockSpec(vectors.shape, lambda i: (0, 0)),
            pl.BlockSpec((1, block), lambda i: (0, 0)),
            pl.BlockSpec((D, block), lambda i: (0, 0)),
            pl.BlockSpec((D, block), lambda i: (0, 1)),
        ]
        + [any_spec] * len(held),
        out_specs=(
            fixed, wide, wide, row, row,
            pl.BlockSpec((ROWS, 1), lambda i: (item * steps + i, 0)),
        ),
        input_output_aliases={7 + i: 1 + i for i in range(len(held))},
        compiler_params=params(),
        cost_estimate=cost(4 * LEN * D * block, 4 * D * block + 16 * LEN * D, 2 * LEN * block),
        name="expand_first",
    )(mine, other, source, vectors, hidden_bias, mid, mid, *held)


def expand_last_kernel(
    total_ref, middle_ref, bias_ref, up_ref, down_ref, part_ref, active_ref, slope_ref
):
    active, slope = gelu_parts(dot_nn(middle_ref[...], up_ref[...]) + bias_ref[...])
    active_ref[...] = active
    slope_ref[...] = slope
    part_ref[...] = (total_ref[...] + dot_nt(active, down_ref[...])).astype(low)


def expand_last(total, middle, hidden_bias, mid, held, item):
    hidden = hidden_bias.shape[1]
    block = hidden // 2
    steps = LEN // ROWS
    fixed = pl.BlockSpec((ROWS, D), lambda i: (i, 0))
    wide = pl.BlockSpec((ROWS, block), lambda i: (item * steps + i, 1))
    return pl.pallas_call(
        chained(expand_last_kernel, 5, 2),
        out_shape=(shape((LEN, D), low),) + tuple(shape(part.shape, low) for part in held),
        grid=(steps,),
        in_specs=[
            fixed,
            pl.BlockSpec((ROWS, D), lambda i: (item * steps + i, 0)),
            pl.BlockSpec((1, block), lambda i: (0, 1)),
            pl.BlockSpec((D, block), lambda i: (0, 0)),
            pl.BlockSpec((D, block), lambda i: (0, 1)),
            any_spec,
            any_spec,
        ],
        out_specs=(fixed, wide, wide),
        input_output_aliases={5: 1, 6: 2},
        compiler_params=params(),
        cost_estimate=cost(4 * LEN * D * block, 4 * D * block + 10 * LEN * D, 2 * LEN * block),
        name="expand_last",
    )(total, middle, hidden_bias, mid, mid, *held)


def contract_kernel(
    mine_ref, other_ref, normed_ref, cotangent_ref, scale_ref, vector_ref, slope_ref,
    up_first, down_first, up_last, down_last,
    part_ref, sum_ref, hidden_sum_ref, out_ref, wide_ref, low_ref, hidden_ref,
):
    @pl.when(pl.program_id(0) == 0)
    def _():
        sum_ref[...] = jnp.zeros_like(sum_ref)
        hidden_sum_ref[...] = jnp.zeros_like(hidden_sum_ref)

    middle = normed_ref[...] * vector_ref[1:2, :] + vector_ref[2:3, :]
    summed = (
        mine_ref[...].astype(full) + other_ref[...].astype(full) + vector_ref[3:4, :] + middle
    )
    normed, inverse = normalize(summed)
    out_ref[...] = (normed * vector_ref[4:5, :] + vector_ref[5:6, :]).astype(low)
    incoming = cotangent_ref[...].astype(full) * scale_ref[...]
    second = norm_back(incoming, normed, inverse, vector_ref[4:5, :])
    sum_ref[0:1, :] += column_sum(second)
    sum_ref[1:2, :] += column_sum(incoming * normed)
    sum_ref[2:3, :] += column_sum(incoming)
    wide_ref[...] = second
    held = second.astype(low)
    low_ref[...] = held
    block = up_first.shape[1]
    total = None
    for at, up_ref, down_ref in ((0, up_first, down_first), (block, up_last, down_last)):
        slope = slope_ref[:, at : at + block].astype(full)
        hidden_grad = (dot_nn(held, down_ref[...]) * slope).astype(low)
        hidden_ref[:, at : at + block] = hidden_grad
        hidden_sum_ref[:, at : at + block] += column_sum(hidden_grad.astype(full))
        part = dot_nt(hidden_grad, up_ref[...])
        total = part if total is None else total + part
    part_ref[...] = total.astype(low)


def contract(mine, other, normed, cotangent, scale, vectors, slope, mids, held, item):
    rows, hidden = slope.shape
    block = hidden // 2
    steps = LEN // ROWS
    fixed = pl.BlockSpec((ROWS, D), lambda i: (i, 0))
    row = pl.BlockSpec((ROWS, D), lambda i: (item * steps + i, 0))
    wide = pl.BlockSpec((ROWS, hidden), lambda i: (item * steps + i, 0))
    weights = [pl.BlockSpec((D, block), lambda i: (0, 0)), pl.BlockSpec((D, block), lambda i: (0, 1))]
    outs = (
        shape((LEN, D), low),
        shape((3, D), full),
        shape((1, hidden), full),
        shape((rows, D), low),
        shape((rows, D), full),
        shape((rows, D), low),
        shape((rows, hidden), low),
    )
    held = held or ()
    return pl.pallas_call(
        chained(contract_kernel, 11, len(held)),
        out_shape=outs,
        grid=(steps,),
        in_specs=[
            fixed,
            fixed,
            row,
            row,
            pl.BlockSpec((ROWS, 1), lambda i: (item * steps + i, 0)),
            pl.BlockSpec(vectors.shape, lambda i: (0, 0)),
            wide,
        ]
        + weights
        + weights
        + [any_spec] * len(held),
        out_specs=(
            fixed,
            pl.BlockSpec((3, D), lambda i: (0, 0)),
            pl.BlockSpec((1, hidden), lambda i: (0, 0)),
            row,
            row,
            row,
            wide,
        ),
        input_output_aliases={11 + i: 3 + i for i in range(len(held))},
        compiler_params=params(),
        cost_estimate=cost(4 * LEN * D * hidden, 4 * D * hidden + 4 * LEN * hidden),
        name="contract",
    )(
        mine, other, normed, cotangent, scale, vectors, slope,
        mids[0], mids[0], mids[1], mids[1], *held,
    )


def first_back_kernel(
    mine_ref, other_ref, second_ref, normed_ref, inverse_ref, vector_ref, w_ref,
    sum_ref, wide_ref, low_ref, grad_ref,
):
    @pl.when(pl.program_id(0) == 0)
    def _():
        sum_ref[...] = jnp.zeros_like(sum_ref)

    incoming = mine_ref[...].astype(full) + other_ref[...].astype(full) + second_ref[...]
    normed = normed_ref[...]
    first = norm_back(incoming, normed, inverse_ref[...], vector_ref[1:2, :])
    sum_ref[0:1, :] += column_sum(first)
    sum_ref[1:2, :] += column_sum(incoming * normed)
    sum_ref[2:3, :] += column_sum(incoming)
    wide_ref[...] = first
    held = first.astype(low)
    low_ref[...] = held
    grad_ref[...] = dot_nn(held, w_ref[...]).astype(low)


def first_back(mine, other, second, normed, inverse, vectors, mid, outward_at, width, held, item):
    rows = second.shape[0]
    steps = LEN // ROWS
    fixed = pl.BlockSpec((ROWS, D), lambda i: (i, 0))
    row = pl.BlockSpec((ROWS, D), lambda i: (item * steps + i, 0))
    held = held or ()
    return pl.pallas_call(
        chained(first_back_kernel, 7, len(held)),
        out_shape=(
            shape((3, D), full),
            shape((rows, D), full),
            shape((rows, D), low),
            shape((rows, width), low),
        ),
        grid=(steps,),
        in_specs=[
            fixed,
            fixed,
            row,
            row,
            pl.BlockSpec((ROWS, 1), lambda i: (item * steps + i, 0)),
            pl.BlockSpec(vectors.shape, lambda i: (0, 0)),
            pl.BlockSpec((D, width), lambda i: (0, outward_at // width)),
        ]
        + [any_spec] * len(held),
        out_specs=(
            pl.BlockSpec((3, D), lambda i: (0, 0)),
            row,
            row,
            pl.BlockSpec((ROWS, width), lambda i: (item * steps + i, 0)),
        ),
        input_output_aliases={7 + i: 1 + i for i in range(len(held))},
        compiler_params=params(24),
        cost_estimate=cost(2 * LEN * D * width, 20 * LEN * D),
        name="first_back",
    )(mine, other, second, normed, inverse, vectors, mid, *held)


def source_kernel(*refs):
    grads, weights, out_ref = refs[:-2], refs[-2], refs[-1]
    width = 3 * LANES
    total = None
    for group, grad_ref in enumerate(grads):
        part = dot_nt(grad_ref[...], weights[:, group * width : (group + 1) * width])
        total = part if total is None else total + part
    out_ref[...] = total.astype(low)


def source_part(grads, inward, item):
    width = 3 * LANES
    groups = len(grads)
    steps = LEN // ROWS
    return pl.pallas_call(
        source_kernel,
        out_shape=shape((LEN, D), low),
        grid=(steps,),
        in_specs=[pl.BlockSpec((ROWS, width), lambda i: (item * steps + i, 0)) for _ in grads]
        + [pl.BlockSpec((D, groups * width), lambda i: (0, 0))],
        out_specs=pl.BlockSpec((ROWS, D), lambda i: (i, 0)),
        compiler_params=params(16),
        cost_estimate=cost(2 * LEN * D * width * groups, 2 * (LEN + D) * width * groups),
        name="source",
    )(*grads, inward)


def transpose_into(left_ref, turned_ref):
    for start in range(0, left_ref.shape[0], LEN):
        turned_ref[:, start : start + LEN] = (
            left_ref[start : start + LEN, :].astype(full).T.astype(low)
        )


def weight_grad_kernel(bit, turned, rights, extra, me_ref, left_ref, *refs):
    right_refs, refs = refs[:rights], refs[rights:]
    if extra:
        extra_ref, refs = refs[0], refs[1:]
    if turned:
        left = left_ref
    else:
        left, refs = refs[-1], refs[:-1]

        @pl.when(pl.program_id(0) == 0)
        def _():
            transpose_into(left_ref, left)

    right = right_refs[0][...]
    if rights > 1:
        right = jnp.concatenate([ref[...] for ref in right_refs], axis=1)
    if bit is None:
        refs[0][...] = dot_nn(left[...], right)
        return
    sent, kept, total_ref = refs
    total_ref[...] = dot_nn(left[...], right)
    layers, rows = sent.shape[1], sent.shape[2]
    width = total_ref.shape[1]
    for plane in range(4):
        other = plane >> 1 if bit == 0 else plane & 1
        target = sent if (plane >> bit) & 1 else kept
        for k in range(layers):
            owner = me_ref[0] ^ (4 * k + plane)
            start = pl.multiple_of(owner * rows, 8)
            target[other, k, :, :width] = total_ref[pl.ds(start, rows), :].astype(low)
            if extra:
                target[other, k, :, width:] = extra_ref[owner]


def weight_grad(left, rights, me, size, bit, turned=False, extra=None):
    tokens = rights[0].shape[0]
    width = sum(right.shape[1] for right in rights)
    block = 512 if width % 512 == 0 else width
    layers, rows = size // 4, D // size
    fast = me is not None
    extras = () if extra is None else (extra,)
    total = width + (0 if extra is None else LANES)
    if fast:
        piece = (2, layers, rows)
        out_block = block + total - width
        outs = (shape(piece + (total,), low),) * 2
        out_specs = tuple(
            pl.BlockSpec(piece + (out_block,), lambda j, m: (0, 0, 0, j)) for _ in range(2)
        )
        scratch = [pltpu.VMEM((D, block), full)]
    else:
        outs = (shape((D, width), full),)
        out_specs = (pl.BlockSpec((D, block), lambda j, m: (0, j)),)
        scratch = []
        me = jnp.zeros((1,), jnp.int32)
        bit = None
    if not turned:
        scratch.append(pltpu.VMEM((D, tokens), low))
    right_blocks = [block] if len(rights) == 1 else [right.shape[1] for right in rights]
    return pl.pallas_call(
        partial(weight_grad_kernel, bit, turned, len(rights), extra is not None),
        out_shape=outs,
        grid_spec=pltpu.PrefetchScalarGridSpec(
            num_scalar_prefetch=1,
            grid=(width // block,),
            in_specs=[pl.BlockSpec(left.shape, lambda j, m: (0, 0))]
            + [pl.BlockSpec((tokens, part), lambda j, m: (0, j)) for part in right_blocks]
            + [pl.BlockSpec(part.shape, lambda j, m: (0, 0, 0)) for part in extras],
            out_specs=out_specs,
            scratch_shapes=scratch,
        ),
        compiler_params=params(24),
        cost_estimate=cost(2 * tokens * D * width, 2 * (tokens * D + tokens * width + D * width)),
        name="weight_grad",
    )(me, left, *rights, *extras)


def adamw(master, gradient, first_moment, second_moment, step_rate, decay_rate, correct):
    first_new = 0.5 * first_moment + 0.5 * gradient
    second_new = 0.5 * second_moment + 0.5 * gradient * gradient
    moved = first_new / correct / (jnp.sqrt(second_new / correct) + 1e-08)
    return (master - step_rate * (moved + decay_rate * master), first_new, second_new)


def per_device(
    activations,
    cotangent,
    token_weight,
    lengths,
    step_count,
    inward_weight,
    output_weight,
    up_weight,
    down_weight,
    heads_bias,
    hidden_bias,
    norm_vectors,
    *moments,
):
    size = lax.axis_size("dp")
    rows, width = inward_weight.shape[1], inward_weight.shape[2]
    hidden_width = up_weight.shape[1]
    groups = width // LANES
    tokens = activations.shape[0]
    count = tokens // LEN
    fast = size == 16 and rows % 16 == 0
    me = lax.axis_index("dp").astype(jnp.int32).reshape(1) if fast else None

    small = jnp.concatenate(
        [heads_bias.reshape(-1), hidden_bias.reshape(-1), norm_vectors.reshape(-1)]
    )
    per_row = small.shape[0] // rows
    small_block = jnp.pad(small.reshape(rows, per_row), ((0, 0), (0, LANES - per_row)))
    inward_shard = jnp.concatenate(
        [
            inward_weight.reshape(3, rows, groups, LANES)
            .transpose(1, 2, 0, 3)
            .reshape(rows, 3 * width),
            small_block,
        ],
        axis=1,
    ).astype(low)
    block = hidden_width // 2
    outward_at = 2 * block
    up_shard, down_shard = up_weight.astype(low), down_weight.T.astype(low)
    first_shard = jnp.concatenate(
        [up_shard[:, :block], down_shard[:, :block], output_weight.T.astype(low)], axis=1
    )
    last_shard = jnp.concatenate([up_shard[:, block:], down_shard[:, block:]], axis=1)

    if fast:
        found = gather_planes(inward_shard, size)
        found_first = gather_planes(after(first_shard, *found[1:]), size)
        found_last = gather_planes(after(last_shard, *found_first[1:]), size)
        turned = turn(activations)
        found[0] = after(found[0], turned)
        own = split_halves(found)
        pairs = gather_pairs(own, gather_near(own, size))
        far = gather_far(pairs, size)
        inward = place(pairs, far, me)
        own_first = split_halves(list(after_all(found_first, *far)))
        near_first = gather_near(own_first, size)
        inward = after(inward, *own_first)
    else:
        inward, mid_first, mid_last = [
            lax.all_gather(shard, "dp", axis=0, tiled=True)
            for shard in (inward_shard, first_shard, last_shard)
        ]
        turned = turn(activations)

    smalls = inward[:, 3 * width : 3 * width + per_row].astype(full).reshape(size, -1)
    heads_size, hidden_size = heads_bias.size, hidden_bias.size
    head_biases = (
        smalls[:, :heads_size].reshape(size, 2, -1).transpose(1, 2, 0).reshape(2, width)
    )
    hidden_biases = smalls[:, heads_size : heads_size + hidden_size].T.reshape(1, hidden_width)
    vectors = (
        smalls[:, heads_size + hidden_size :].reshape(size, 6, rows).transpose(1, 0, 2)
    ).reshape(6, D)

    live = lax.broadcasted_iota(jnp.int32, (count, LEN), 1) < lengths[:, None]
    scale = (token_weight.reshape(count, LEN) * live.astype(jnp.int32)).astype(full)
    scale = scale.reshape(tokens, 1)

    qkv, weights, contexts = [], [], []
    source = activations
    for group in range(groups):
        if fast and group == groups - 1:
            near_first = after_all(near_first, contexts[-1])
            pairs_first = gather_pairs(own_first, near_first)
            far_first = gather_far(pairs_first, size)
            own_last = split_halves(list(after_all(found_last, *pairs_first)))
            near_last = gather_near(own_last, size)
            source = after(activations, *pairs_first, *own_last)
        elif group:
            source = after(activations, contexts[-1])
        parts = attend(lengths, source, inward, head_biases, group)
        for kept, part in zip((qkv, weights, contexts), parts):
            kept.append(part)
    if fast:
        pairs_last = gather_pairs(own_last, after_all(near_last, contexts[-1]))
        far_last = gather_far(pairs_last, size)
        mid_first = place(pairs_first, after_all(far_first, *pairs_last), me)

    mine = [outward_part(contexts, mid_first, outward_at, item) for item in range(count)]
    other = [swap_cores(part) for part in mine]
    held = None
    totals = []
    for item in range(count):
        total, *held = expand_first(
            mine[item], other[item], activations, vectors, hidden_biases, mid_first, held, item
        )
        totals.append(total)
    active, slope, middle, normed, inverse = held
    if fast:
        mid_last = place(pairs_last, after_all(far_last, totals[-1]), me)
    mine_down = []
    held = (active, slope)
    for item in range(count):
        part, *held = expand_last(totals[item], middle, hidden_biases, mid_last, held, item)
        mine_down.append(part)
    active, slope = held
    other_down = [swap_cores(part) for part in mine_down]
    held = None
    mine_middle, second_sums, hidden_sums = [], [], []
    for item in range(count):
        part, sums, hidden_sum, *held = contract(
            mine_down[item], other_down[item], normed, cotangent, scale, vectors, slope,
            (mid_first, mid_last), held, item,
        )
        mine_middle.append(part)
        second_sums.append(sums)
        hidden_sums.append(hidden_sum)
    output_rows, second_grad, second_low, hidden_grad = held
    other_middle = [swap_cores(part) for part in mine_middle]

    def heads_outgoing(sums):
        return jnp.concatenate(sums, axis=1).reshape(2, -1, size).transpose(2, 0, 1)

    def back_first():
        held, sums = None, []
        for item in range(count):
            part, *held = first_back(
                mine_middle[item], other_middle[item], second_grad, normed, inverse, vectors,
                mid_first, outward_at, width, held, item,
            )
            sums.append(part)
        return sums, held

    def small_outgoing(first_sums, head_sums):
        norm_grad = jnp.concatenate([sum(first_sums), sum(second_sums)])
        return jnp.concatenate(
            [
                heads_outgoing(head_sums).reshape(size, -1),
                sum(hidden_sums).reshape(-1, size).T,
                norm_grad.reshape(6, size, rows).transpose(1, 0, 2).reshape(size, -1),
            ],
            axis=1,
        )

    stacked, head_sums = [], []
    if fast:
        sent_down, kept_down = weight_grad(second_low, [active], me, size, 0)
        got_down = hop(sent_down, 1, size)
        sent_up, kept_up = weight_grad(after(middle, sent_down), [hidden_grad], me, size, 1)
        got_up = hop(sent_up, 2, size)
        mine_middle[0] = after(mine_middle[0], sent_up)
        first_sums, (first_grad, first_low, context_grad) = back_first()
        got_down = after(got_down, first_low)
        next_down = kept_down[1] + got_down[1]
        more_down = hop(next_down, 2, size)
        sent_out, kept_out = weight_grad(
            after(first_low, next_down), contexts, me, size, 0
        )
        got_out = hop(sent_out, 1, size)

        grads, sums = attend_back(qkv[0], weights[0], after(context_grad, sent_out), 0)
        stacked.append(grads)
        head_sums.append(sums)
        got_up = after(got_up, grads)
        next_up = kept_up[1] + got_up[1]
        more_up = hop(next_up, 1, size)
        sent_0, kept_0 = weight_grad(after(turned, next_up), [stacked[0]], me, size, 1, True)
        got_0 = hop(sent_0, 2, size)

        grads, sums = attend_back(qkv[1], weights[1], after(context_grad, sent_0), 1)
        stacked.append(grads)
        head_sums.append(sums)
        sent_1, kept_1 = weight_grad(turned, [stacked[1]], me, size, 0, True)
        got_1 = hop(sent_1, 1, size)

        grads, sums = attend_back(qkv[2], weights[2], after(context_grad, sent_1), 2)
        stacked.append(grads)
        head_sums.append(sums)
        more_down, more_up, got_out, got_0 = after_all((more_down, more_up, got_out, got_0), grads)
        own_wide, *out_wide = reduce_outgoing(
            (
                reduce_total(kept_down, got_down, more_down),
                reduce_total(kept_up, got_up, more_up),
            )
        )
        planes_wide = reduce_planes(out_wide, size)
        next_out, next_0 = after_all((kept_out[1] + got_out[1], kept_0[1] + got_0[1]), own_wide)
        more_out, more_0 = hop(next_out, 2, size), hop(next_0, 1, size)
        extra = small_outgoing(first_sums, head_sums).reshape(size, rows, per_row)
        extra = jnp.pad(extra, ((0, 0), (0, 0), (0, LANES - per_row))).astype(low)
        sent_2, kept_2 = weight_grad(
            after(turned, next_out, next_0), [stacked[2]], me, size, 1, True, extra
        )
        got_2 = hop(sent_2, 2, size)

        first_grads = after(stacked[0], sent_2)
        mine_source = [source_part([first_grads] + stacked[1:], inward, 0)]
        more_out, more_0 = after_all((more_out, more_0), mine_source[0])
        own_near, *out_near = reduce_outgoing(
            (reduce_total(kept_out, got_out, more_out), reduce_total(kept_0, got_0, more_0))
        )
        planes_near = reduce_planes(out_near, size)
        first_grads = after(first_grads, own_near)
        mine_source.append(source_part([first_grads] + stacked[1:], inward, 1))
        got_1, got_2 = after_all((got_1, got_2), mine_source[1])
        next_1, next_2 = after_all((kept_1[1] + got_1[1], kept_2[1] + got_2[1]))
        more_1, more_2 = hop(next_1, 2, size), hop(next_2, 1, size)
        first_grads = after(first_grads, next_1, next_2)
        mine_source.append(source_part([first_grads] + stacked[1:], inward, 2))
        more_1, more_2 = after_all((more_1, more_2), mine_source[2])
        own_far, *out_far = reduce_outgoing(
            (reduce_total(kept_1, got_1, more_1), reduce_total(kept_2, got_2, more_2))
        )
        planes_far = reduce_planes(out_far, size)
        wide_grad = reduce_sum(own_wide, planes_wide)
        near_grad = reduce_sum(own_near, planes_near)
        far_grad = reduce_sum(own_far, planes_far)
        downward_grad, upward_grad = wide_grad[:, :hidden_width], wide_grad[:, hidden_width:]
        outward_grad = near_grad[:, :width]
        cut = 3 * LANES
        inward_grads = [near_grad[:, width:], far_grad[:, :cut], far_grad[:, cut : 2 * cut]]
        small_grad = far_grad[:, 2 * cut : 2 * cut + per_row].reshape(-1)
    else:

        def reduced(value):
            return lax.psum_scatter(value, "dp", scatter_dimension=0, tiled=True)

        first_sums, (first_grad, first_low, context_grad) = back_first()
        downward_grad = reduced(weight_grad(second_low, [active], None, size, None)[0])
        upward_grad = reduced(weight_grad(middle, [hidden_grad], None, size, None)[0])
        outward_grad = reduced(weight_grad(first_low, contexts, None, size, None)[0])
        inward_grads = []
        for group in range(groups):
            grads, sums = attend_back(qkv[group], weights[group], context_grad, group)
            stacked.append(grads)
            head_sums.append(sums)
            inward_grads.append(
                reduced(weight_grad(turned, [grads], None, size, None, True)[0])
            )
        mine_source = [source_part(stacked, inward, item) for item in range(count)]
        small_grad = reduced(small_outgoing(first_sums, head_sums)).reshape(-1)
    other_source = [swap_cores(part) for part in mine_source]
    input_grad = (
        jnp.concatenate(
            [a.astype(full) + b.astype(full) for a, b in zip(mine_source, other_source)]
        )
        + first_grad
    )

    inward_grad = jnp.stack(
        [
            jnp.concatenate(
                [grad[:, kind * LANES : (kind + 1) * LANES] for grad in inward_grads], axis=1
            )
            for kind in range(3)
        ]
    )
    grads = (
        inward_grad,
        outward_grad.T,
        upward_grad,
        downward_grad.T,
        small_grad[:heads_size].reshape(heads_bias.shape),
        small_grad[heads_size : heads_size + hidden_size].reshape(hidden_bias.shape),
        small_grad[heads_size + hidden_size :].reshape(norm_vectors.shape),
    )

    step_value = step_count[0].astype(full)
    correct = 1.0 - jnp.power(0.5, step_value)
    plan = (step_value + 4.0) / 12.0
    rates = (D ** (-0.5), (6 * D // LEN) ** (-0.5), D ** (-0.5), FF ** (-0.5), 0.5, 0.5, 0.3)
    decays = (0.01, 0.01, 0.01, 0.01, 0.0, 0.0, 0.0)
    masters = (
        inward_weight,
        output_weight,
        up_weight,
        down_weight,
        heads_bias,
        hidden_bias,
        norm_vectors,
    )
    results = [output_rows, input_grad]
    for at in range(7):
        results.extend(
            adamw(
                masters[at],
                grads[at],
                moments[at],
                moments[7 + at],
                rates[at] * plan,
                decays[at],
                correct,
            )
        )
    return tuple(results)


def solution(mesh):
    matrices = (
        P(None, "dp", "tensor"),
        P("tensor", "dp"),
        P("dp", "tensor"),
        P("tensor", "dp"),
        P(None, "tensor", "dp"),
        P("tensor", "dp"),
        P(None, "dp"),
    )
    in_specs = (
        (P("dp", None), P("dp", None), P("dp"), P("dp"), P()) + matrices + matrices + matrices
    )
    out_specs = (P("dp", None), P("dp", None)) + tuple(
        spec for spec in matrices for _ in range(3)
    )
    return jax.shard_map(
        per_device, mesh=mesh, in_specs=in_specs, out_specs=out_specs, check_vma=False
    )
```

```python
from functools import partial
import math

import jax
import jax.numpy as jnp
from jax import lax
from jax.experimental import pallas as pl
from jax.experimental.pallas import tpu as pltpu
from jax.sharding import PartitionSpec as P

D = 768
HEAD_DIM = 64
FF = 3072
LEN = 512
LANES = 128
ROWS = 256
COST_SHARE = 1
EXPAND, CONTRACT, GRADS = 16, 20, 20

norm_epsilon = 1e-12
low = jnp.bfloat16
full = jnp.float32


def dot_nn(left, right):
    return lax.dot_general(left, right, (((1,), (0,)), ((), ())), preferred_element_type=full)


def dot_nt(left, right):
    return lax.dot_general(left, right, (((1,), (1,)), ((), ())), preferred_element_type=full)


def column_sum(values):
    return jnp.sum(values, axis=0, keepdims=True)


def row_mean(values):
    return jnp.mean(values, axis=-1, keepdims=True)


def normalize(total_in):
    centred = total_in - row_mean(total_in)
    inverse = lax.rsqrt(row_mean(centred * centred) + norm_epsilon)
    return (centred * inverse, inverse)


def norm_back(incoming, normed, inverse, gain):
    scaled = incoming * gain
    return inverse * (scaled - row_mean(scaled) - normed * row_mean(scaled * normed))


def cost(flops, moved, exps=0):
    return pl.CostEstimate(
        flops=int(flops / COST_SHARE),
        bytes_accessed=int(moved / COST_SHARE),
        transcendentals=int(exps / COST_SHARE),
    )


def params(mebibytes=12):
    return pltpu.CompilerParams(vmem_limit_bytes=mebibytes * 1024 * 1024)


def shape(dims, kind):
    return jax.ShapeDtypeStruct(dims, kind)


def main(dims, kind):
    return pltpu.HBM(dims, kind)


def after(value, *others):
    return lax.optimization_barrier((value,) + others)[0]


def after_all(values, *others):
    return lax.optimization_barrier(tuple(values) + others)[: len(values)]


def hop(value, offset, size):
    return lax.ppermute(value, "dp", [(d, d ^ offset) for d in range(size)])


def swap_cores(value):
    return lax.ppermute(value, "tensor", [(0, 1), (1, 0)])


def split_columns(width):
    return -(-width // (2 * LANES)) * LANES


def gather_planes(shard, size):
    found = [shard] + [hop(shard, 4 * k, size) for k in range(1, size // 4)]
    return found


def gather_doubled(shard, size):
    pair = jnp.stack([shard, hop(shard, 8, size)])
    near = hop(pair, 4, size)
    return [pair[0], near[0], pair[1], near[1]]


def split_halves(found):
    stacked = jnp.stack(found)
    cut = split_columns(stacked.shape[2])
    return lax.optimization_barrier((stacked[..., :cut], stacked[..., cut:]))


def gather_near(own, size):
    return (hop(own[0], 2, size), hop(own[1], 1, size))


def gather_pairs(own, near):
    return lax.optimization_barrier(
        (jnp.concatenate([own[0], near[0]]), jnp.concatenate([own[1], near[1]]))
    )


def gather_far(pairs, size):
    return (hop(pairs[0], 1, size), hop(pairs[1], 2, size))


def place_kernel(me_ref, pair_a, far_a, pair_b, far_b, out_ref):
    layers, rows, cut = pair_a.shape
    layers //= 2
    sources = (
        (pair_a, 0, pair_b, 0),
        (far_a, 0, pair_b, layers),
        (pair_a, layers, far_b, 0),
        (far_a, layers, far_b, layers),
    )
    for plane, (left, left_at, right, right_at) in enumerate(sources):
        for k in range(layers):
            start = pl.multiple_of((me_ref[0] ^ (4 * k + plane)) * rows, 16)
            out_ref[pl.ds(start, rows), :cut] = left[left_at + k]
            out_ref[pl.ds(start, rows), cut:] = right[right_at + k]


def place(pairs, far, me):
    flat = (pairs[0], far[0], pairs[1], far[1])
    layers, rows, cut = pairs[0].shape
    width = cut + pairs[1].shape[2]
    total = 2 * layers * rows
    return pl.pallas_call(
        place_kernel,
        out_shape=shape((total, width), low),
        grid_spec=pltpu.PrefetchScalarGridSpec(
            num_scalar_prefetch=1,
            grid=(1,),
            in_specs=[pl.BlockSpec(piece.shape, lambda i, m: (0, 0, 0)) for piece in flat],
            out_specs=pl.BlockSpec((total, width), lambda i, m: (0, 0)),
        ),
        compiler_params=params(12),
        cost_estimate=cost(0, 4 * total * width),
        name="place",
    )(me, *flat)


def turn_kernel(source_ref, out_ref):
    out_ref[...] = source_ref[...].astype(full).T.astype(low)


def turn(source):
    rows, width = source.shape
    return pl.pallas_call(
        turn_kernel,
        out_shape=shape((width, rows), low),
        grid=(rows // LEN,),
        in_specs=[pl.BlockSpec((LEN, width), lambda i: (i, 0))],
        out_specs=pl.BlockSpec((width, LEN), lambda i: (0, i)),
        compiler_params=params(16),
        cost_estimate=cost(0, 4 * rows * width),
        name="turn",
    )(source)


def combine_kernel(count, *refs):
    own_ref, out_ref = refs[-2:]
    start = 0
    for at in range(count):
        kept, got, more = refs[3 * at : 3 * at + 3]
        total = kept[0].astype(full) + got[0].astype(full) + more[...].astype(full)
        width = total.shape[2]
        for k in range(total.shape[0]):
            if k % 2:
                out_ref[k // 2, :, start : start + width] = total[k].astype(low)
            else:
                own_ref[k // 2, :, start : start + width] = total[k]
        start += width


def combine(halves):
    layers, rows = halves[0][2].shape[:2]
    width = sum(more.shape[2] for _, _, more in halves)
    flat, specs = [], []
    for kept, got, more in halves:
        part = (1,) + more.shape
        flat += [kept, got, more]
        specs += [pl.BlockSpec(part, lambda i: (0, 0, 0, 0))] * 2
        specs += [pl.BlockSpec(more.shape, lambda i: (0, 0, 0))]
    piece = (layers // 2, rows, width)
    return pl.pallas_call(
        partial(combine_kernel, len(halves)),
        out_shape=(shape(piece, full), shape(piece, low)),
        grid=(1,),
        in_specs=specs,
        out_specs=(pl.BlockSpec(piece, lambda i: (0, 0, 0)),) * 2,
        compiler_params=params(16),
        cost_estimate=cost(3 * layers * rows * width, 8 * layers * rows * width),
        name="combine",
    )(*flat)


def far_half(own, near):
    return (own[1] + near[1].astype(full)).astype(low)


def reduce_sum(own, near, far):
    return own[0] + near[0].astype(full) + far.astype(full)


def attend_kernel(length_ref, x_ref, w_ref, bias_ref, qkv_ref, weight_ref, context_ref):
    length = length_ref[pl.program_id(0)]
    mixed = dot_nn(x_ref[...], w_ref[...])
    queries = (mixed[:, :LANES] + bias_ref[0:1, :]).astype(low)
    key_rows = mixed[:, LANES : 2 * LANES].astype(low)
    values_full = mixed[:, 2 * LANES :] + bias_ref[1:2, :]
    values = values_full.astype(low)
    qkv_ref[:, :LANES] = queries
    qkv_ref[:, LANES : 2 * LANES] = key_rows
    qkv_ref[:, 2 * LANES :] = values
    values_t = values_full.T.astype(low)
    rows = queries.shape[0]
    lane = lax.broadcasted_iota(jnp.int32, (rows, LANES), 1)
    live = lax.broadcasted_iota(jnp.int32, (rows, 1), 0) < length
    scaled = queries * (1.0 / math.sqrt(HEAD_DIM))
    parts = []
    for head in range(2):
        picked = jnp.where((lane >= HEAD_DIM) == bool(head), scaled, jnp.zeros_like(scaled))
        scores = jnp.where(live, dot_nt(key_rows, picked), -jnp.inf)
        grown = jnp.exp(scores - jnp.max(scores, axis=0, keepdims=True))
        weights = (grown * (1.0 / jnp.sum(grown, axis=0, keepdims=True))).astype(low)
        weight_ref[0, head] = weights
        parts.append(dot_nn(values_t[head * HEAD_DIM : (head + 1) * HEAD_DIM, :], weights))
    context_ref[...] = jnp.concatenate(parts, axis=0).T.astype(low)


def attend(lengths, source, inward, biases, group):
    rows = source.shape[0]
    count = rows // LEN
    width = 3 * LANES
    return pl.pallas_call(
        attend_kernel,
        out_shape=(
            main((rows, width), low),
            main((count, 2, LEN, LEN), low),
            main((rows, LANES), low),
        ),
        grid_spec=pltpu.PrefetchScalarGridSpec(
            num_scalar_prefetch=1,
            grid=(count,),
            in_specs=[
                pl.BlockSpec((LEN, D), lambda s, n: (s, 0)),
                pl.BlockSpec((D, width), lambda s, n: (0, group)),
                pl.BlockSpec((2, LANES), lambda s, n: (0, group)),
            ],
            out_specs=(
                pl.BlockSpec((LEN, width), lambda s, n: (s, 0)),
                pl.BlockSpec((1, 2, LEN, LEN), lambda s, n: (s, 0, 0, 0)),
                pl.BlockSpec((LEN, LANES), lambda s, n: (s, 0)),
            ),
        ),
        compiler_params=params(),
        cost_estimate=cost(
            2 * rows * D * width + 8 * count * LEN * LEN * LANES,
            count * 2 * LEN * LEN * 2,
            count * 2 * LEN * LEN,
        ),
        name="attend",
    )(lengths, source, inward, biases)


def attend_back_kernel(qkv_ref, weight_ref, *refs):
    grad_refs, out_ref, sum_ref = refs[:-2], refs[-2], refs[-1]

    @pl.when(pl.program_id(0) == 0)
    def _():
        sum_ref[...] = jnp.zeros_like(sum_ref)

    queries = qkv_ref[:, :LANES]
    key_rows = qkv_ref[:, LANES : 2 * LANES]
    values = qkv_ref[:, 2 * LANES :]
    grads = grad_refs[0][...]
    for item in range(1, len(grad_refs)):
        grads = jnp.where(pl.program_id(0) == item, grad_refs[item][...], grads)
    keys_t = key_rows.astype(full).T.astype(low)
    rows = queries.shape[0]
    lane = lax.broadcasted_iota(jnp.int32, (rows, LANES), 1)
    score_scale = 1.0 / math.sqrt(HEAD_DIM)
    query_parts, key_parts, value_parts = [], [], []
    for head in range(2):
        picked = jnp.where((lane >= HEAD_DIM) == bool(head), grads, jnp.zeros_like(grads))
        weights = weight_ref[0, head]
        wide = weights.astype(full)
        mixed = wide * dot_nt(values, picked)
        score_grads = (mixed - wide * jnp.sum(mixed, axis=0, keepdims=True)).astype(low)
        value_parts.append(dot_nn(weights, grads))
        key_parts.append(dot_nn(score_grads, queries))
        query_parts.append(
            dot_nn(keys_t[head * HEAD_DIM : (head + 1) * HEAD_DIM, :], score_grads)
        )
    first = lane < HEAD_DIM
    query_grads = (jnp.concatenate(query_parts, axis=0).T * score_scale).astype(low)
    key_grads = (jnp.where(first, key_parts[0], key_parts[1]) * score_scale).astype(low)
    value_grads = jnp.where(first, value_parts[0], value_parts[1]).astype(low)
    out_ref[:, :LANES] = query_grads
    out_ref[:, LANES : 2 * LANES] = key_grads
    out_ref[:, 2 * LANES :] = value_grads
    sum_ref[0:1, :] += column_sum(query_grads.astype(full))
    sum_ref[1:2, :] += column_sum(value_grads.astype(full))


def attend_back(qkv, weights, grads, group):
    rows = qkv.shape[0]
    count = rows // LEN
    width = 3 * LANES
    return pl.pallas_call(
        attend_back_kernel,
        out_shape=(main((rows, width), low), main((2, LANES), full)),
        grid=(count,),
        in_specs=[
            pl.BlockSpec((LEN, width), lambda s: (s, 0)),
            pl.BlockSpec((1, 2, LEN, LEN), lambda s: (s, 0, 0, 0)),
        ]
        + [pl.BlockSpec((LEN, LANES), lambda s: (0, group)) for _ in grads],
        out_specs=(
            pl.BlockSpec((LEN, width), lambda s: (s, 0)),
            pl.BlockSpec((2, LANES), lambda s: (0, 0)),
        ),
        compiler_params=params(),
        cost_estimate=cost(
            16 * count * LEN * LEN * LANES, count * 2 * LEN * LEN * 2 + 4 * rows * width
        ),
        name="attend_back",
    )(qkv, weights, *grads)


def outward_kernel(*refs):
    contexts, w_ref, out_ref = refs[:-2], refs[-2], refs[-1]
    context = jnp.concatenate([ref[...] for ref in contexts], axis=1)
    out_ref[...] = dot_nt(context, w_ref[...]).astype(low)


def outward_part(contexts, mid, outward_at, item):
    width = len(contexts) * LANES
    steps = LEN // ROWS
    return pl.pallas_call(
        outward_kernel,
        out_shape=shape((LEN, D), low),
        grid=(steps,),
        in_specs=[
            pl.BlockSpec((ROWS, LANES), lambda i: (item * steps + i, 0)) for _ in contexts
        ]
        + [pl.BlockSpec((D, width), lambda i: (0, outward_at // width))],
        out_specs=pl.BlockSpec((ROWS, D), lambda i: (i, 0)),
        compiler_params=params(16),
        cost_estimate=cost(2 * LEN * D * width, 2 * (LEN * D + LEN * width + D * width)),
        name="outward",
    )(*contexts, mid)


def gelu_parts(hidden):
    half = 0.5 + 0.5 * lax.erf(hidden * 0.7071067811865476)
    slope = half + hidden * 0.3989422804014327 * jnp.exp(-0.5 * hidden * hidden)
    return ((hidden * half).astype(low), slope.astype(low))


def expand_first_kernel(
    mine_ref, other_ref, x_ref, vector_ref, bias_ref, up_ref, down_ref,
    total_ref, active_ref, slope_ref, middle_ref, normed_ref, inverse_ref,
):
    summed = (
        mine_ref[...].astype(full)
        + other_ref[...].astype(full)
        + vector_ref[0:1, :]
        + x_ref[...].astype(full)
    )
    normed, inverse = normalize(summed)
    normed_ref[...] = normed
    inverse_ref[...] = inverse
    held = (normed * vector_ref[1:2, :] + vector_ref[2:3, :]).astype(low)
    middle_ref[...] = held
    active, slope = gelu_parts(dot_nn(held, up_ref[...]) + bias_ref[...])
    active_ref[...] = active
    slope_ref[...] = slope
    total_ref[...] = dot_nt(active, down_ref[...])


def expand_first(mine, other, source, vectors, hidden_bias, mid, item):
    hidden = hidden_bias.shape[1]
    block = hidden // 2
    steps = LEN // ROWS
    row = pl.BlockSpec((ROWS, D), lambda i: (i, 0))
    wide = pl.BlockSpec((ROWS, block), lambda i: (i, 0))
    return pl.pallas_call(
        expand_first_kernel,
        out_shape=(
            main((LEN, D), full),
            main((LEN, block), low),
            main((LEN, block), low),
            main((LEN, D), low),
            main((LEN, D), full),
            main((LEN, 1), full),
        ),
        grid=(steps,),
        in_specs=[
            row,
            row,
            pl.BlockSpec((ROWS, D), lambda i: (item * steps + i, 0)),
            pl.BlockSpec(vectors.shape, lambda i: (0, 0)),
            pl.BlockSpec((1, block), lambda i: (0, 0)),
            pl.BlockSpec((D, block), lambda i: (0, 0)),
            pl.BlockSpec((D, block), lambda i: (0, 1)),
        ],
        out_specs=(row, wide, wide, row, row, pl.BlockSpec((ROWS, 1), lambda i: (i, 0))),
        compiler_params=params(EXPAND),
        cost_estimate=cost(4 * LEN * D * block, 4 * D * block + 16 * LEN * D, 2 * LEN * block),
        name="expand_first",
    )(mine, other, source, vectors, hidden_bias, mid, mid)


def expand_last_kernel(
    total_ref, middle_ref, bias_ref, up_ref, down_ref, part_ref, active_ref, slope_ref
):
    active, slope = gelu_parts(dot_nn(middle_ref[...], up_ref[...]) + bias_ref[...])
    active_ref[...] = active
    slope_ref[...] = slope
    part_ref[...] = (total_ref[...] + dot_nt(active, down_ref[...])).astype(low)


def expand_last(total, middle, hidden_bias, mid):
    hidden = hidden_bias.shape[1]
    block = hidden // 2
    row = pl.BlockSpec((ROWS, D), lambda i: (i, 0))
    wide = pl.BlockSpec((ROWS, block), lambda i: (i, 0))
    return pl.pallas_call(
        expand_last_kernel,
        out_shape=(main((LEN, D), low), main((LEN, block), low), main((LEN, block), low)),
        grid=(LEN // ROWS,),
        in_specs=[
            row,
            row,
            pl.BlockSpec((1, block), lambda i: (0, 1)),
            pl.BlockSpec((D, block), lambda i: (0, 0)),
            pl.BlockSpec((D, block), lambda i: (0, 1)),
        ],
        out_specs=(row, wide, wide),
        compiler_params=params(EXPAND),
        cost_estimate=cost(4 * LEN * D * block, 4 * D * block + 10 * LEN * D, 2 * LEN * block),
        name="expand_last",
    )(total, middle, hidden_bias, mid, mid)


def contract_kernel(
    mine_ref, other_ref, normed_ref, cotangent_ref, scale_ref, vector_ref,
    slope_first, slope_last, up_first, down_first, up_last, down_last,
    part_ref, sum_ref, hidden_sum_ref, out_ref, wide_ref, low_ref, hidden_first, hidden_last,
):
    @pl.when(pl.program_id(0) == 0)
    def _():
        sum_ref[...] = jnp.zeros_like(sum_ref)
        hidden_sum_ref[...] = jnp.zeros_like(hidden_sum_ref)

    middle = normed_ref[...] * vector_ref[1:2, :] + vector_ref[2:3, :]
    summed = (
        mine_ref[...].astype(full) + other_ref[...].astype(full) + vector_ref[3:4, :] + middle
    )
    normed, inverse = normalize(summed)
    out_ref[...] = (normed * vector_ref[4:5, :] + vector_ref[5:6, :]).astype(low)
    incoming = cotangent_ref[...].astype(full) * scale_ref[...]
    second = norm_back(incoming, normed, inverse, vector_ref[4:5, :])
    sum_ref[0:1, :] += column_sum(second)
    sum_ref[1:2, :] += column_sum(incoming * normed)
    sum_ref[2:3, :] += column_sum(incoming)
    wide_ref[...] = second
    held = second.astype(low)
    low_ref[...] = held
    block = up_first.shape[1]
    total = None
    for at, slope_ref, up_ref, down_ref, hidden_ref in (
        (0, slope_first, up_first, down_first, hidden_first),
        (block, slope_last, up_last, down_last, hidden_last),
    ):
        hidden_grad = (dot_nn(held, down_ref[...]) * slope_ref[...].astype(full)).astype(low)
        hidden_ref[...] = hidden_grad
        hidden_sum_ref[:, at : at + block] += column_sum(hidden_grad.astype(full))
        part = dot_nt(hidden_grad, up_ref[...])
        total = part if total is None else total + part
    part_ref[...] = total.astype(low)


def contract(mine, other, normed, cotangent, scale, vectors, slopes, mids, item):
    block = slopes[0].shape[1]
    hidden = 2 * block
    steps = LEN // ROWS
    row = pl.BlockSpec((ROWS, D), lambda i: (i, 0))
    wide = pl.BlockSpec((ROWS, block), lambda i: (i, 0))
    weights = [pl.BlockSpec((D, block), lambda i: (0, 0)), pl.BlockSpec((D, block), lambda i: (0, 1))]
    return pl.pallas_call(
        contract_kernel,
        out_shape=(
            main((LEN, D), low),
            main((3, D), full),
            main((1, hidden), full),
            main((LEN, D), low),
            main((LEN, D), full),
            main((LEN, D), low),
            main((LEN, block), low),
            main((LEN, block), low),
        ),
        grid=(steps,),
        in_specs=[
            row,
            row,
            row,
            pl.BlockSpec((ROWS, D), lambda i: (item * steps + i, 0)),
            pl.BlockSpec((ROWS, 1), lambda i: (item * steps + i, 0)),
            pl.BlockSpec(vectors.shape, lambda i: (0, 0)),
            wide,
            wide,
        ]
        + weights
        + weights,
        out_specs=(
            row,
            pl.BlockSpec((3, D), lambda i: (0, 0)),
            pl.BlockSpec((1, hidden), lambda i: (0, 0)),
            row,
            row,
            row,
            wide,
            wide,
        ),
        compiler_params=params(CONTRACT),
        cost_estimate=cost(4 * LEN * D * hidden, 4 * D * hidden + 4 * LEN * hidden),
        name="contract",
    )(
        mine, other, normed, cotangent, scale, vectors, *slopes,
        mids[0], mids[0], mids[1], mids[1],
    )


def first_back_kernel(
    mine_ref, other_ref, second_ref, normed_ref, inverse_ref, vector_ref, w_ref,
    sum_ref, wide_ref, low_ref, grad_ref,
):
    @pl.when(pl.program_id(0) == 0)
    def _():
        sum_ref[...] = jnp.zeros_like(sum_ref)

    incoming = mine_ref[...].astype(full) + other_ref[...].astype(full) + second_ref[...]
    normed = normed_ref[...]
    first = norm_back(incoming, normed, inverse_ref[...], vector_ref[1:2, :])
    sum_ref[0:1, :] += column_sum(first)
    sum_ref[1:2, :] += column_sum(incoming * normed)
    sum_ref[2:3, :] += column_sum(incoming)
    wide_ref[...] = first
    held = first.astype(low)
    low_ref[...] = held
    grad_ref[...] = dot_nn(held, w_ref[...]).astype(low)


def first_back(mine, other, second, normed, inverse, vectors, mid, outward_at, width):
    row = pl.BlockSpec((ROWS, D), lambda i: (i, 0))
    return pl.pallas_call(
        first_back_kernel,
        out_shape=(
            main((3, D), full),
            main((LEN, D), full),
            main((LEN, D), low),
            main((LEN, width), low),
        ),
        grid=(LEN // ROWS,),
        in_specs=[
            row,
            row,
            row,
            row,
            pl.BlockSpec((ROWS, 1), lambda i: (i, 0)),
            pl.BlockSpec(vectors.shape, lambda i: (0, 0)),
            pl.BlockSpec((D, width), lambda i: (0, outward_at // width)),
        ],
        out_specs=(
            pl.BlockSpec((3, D), lambda i: (0, 0)),
            row,
            row,
            pl.BlockSpec((ROWS, width), lambda i: (i, 0)),
        ),
        compiler_params=params(12),
        cost_estimate=cost(2 * LEN * D * width, 20 * LEN * D),
        name="first_back",
    )(mine, other, second, normed, inverse, vectors, mid)


def source_kernel(*refs):
    grads, weights, out_ref = refs[:-2], refs[-2], refs[-1]
    width = 3 * LANES
    total = None
    for group, grad_ref in enumerate(grads):
        part = dot_nt(grad_ref[...], weights[:, group * width : (group + 1) * width])
        total = part if total is None else total + part
    out_ref[...] = total.astype(low)


def source_part(grads, inward, item):
    width = 3 * LANES
    groups = len(grads)
    steps = LEN // ROWS
    return pl.pallas_call(
        source_kernel,
        out_shape=shape((LEN, D), low),
        grid=(steps,),
        in_specs=[pl.BlockSpec((ROWS, width), lambda i: (item * steps + i, 0)) for _ in grads]
        + [pl.BlockSpec((D, groups * width), lambda i: (0, 0))],
        out_specs=pl.BlockSpec((ROWS, D), lambda i: (i, 0)),
        compiler_params=params(16),
        cost_estimate=cost(2 * LEN * D * width * groups, 2 * (LEN + D) * width * groups),
        name="source",
    )(*grads, inward)


def finish_kernel(*refs):
    out_ref = refs[-1]
    count = (len(refs) - 1) // 3
    for item in range(count):
        mine, other, first = refs[item], refs[count + item], refs[2 * count + item]
        out_ref[item * LEN : (item + 1) * LEN, :] = (
            mine[...].astype(full) + other[...].astype(full) + first[...]
        )


def finish(mine, other, first):
    rows = len(mine) * LEN
    flat = (*mine, *other, *first)
    return pl.pallas_call(
        finish_kernel,
        out_shape=shape((rows, D), full),
        grid=(1,),
        in_specs=[pl.BlockSpec((LEN, D), lambda i: (0, 0)) for _ in flat],
        out_specs=pl.BlockSpec((rows, D), lambda i: (0, 0)),
        compiler_params=params(20),
        cost_estimate=cost(2 * rows * D, 12 * rows * D),
        name="finish",
    )(*flat)


def weight_grad_kernel(bits, layout, count, turned, extra, me_ref, *refs):
    blocks = len(layout[0])
    lefts, refs = refs[:count], refs[count:]
    rights = []
    for part in layout:
        rights.append([])
        for pieces in part:
            rights[-1].append(refs[:pieces])
            refs = refs[pieces:]
    if extra:
        extra_ref, refs = refs[0], refs[1:]
    if turned:
        lefts = [lefts[0][...]]
    else:
        lefts = [left[...].astype(full).T.astype(low) for left in lefts]
    if len(lefts) > blocks:
        lefts = [jnp.concatenate(lefts, axis=1)]
    for at, part in enumerate(rights):
        total = None
        for left, pieces in zip(lefts, part):
            right = pieces[0][...]
            if len(pieces) > 1:
                right = jnp.concatenate([piece[...] for piece in pieces], axis=1)
            value = dot_nn(left, right)
            total = value if total is None else total + value
        if bits is None:
            refs[at][...] = total
            continue
        bit = bits[at]
        sent, kept, total_ref = refs[2 * at], refs[2 * at + 1], refs[2 * len(rights) + at]
        total_ref[...] = total
        layers, rows = sent.shape[1], sent.shape[2]
        width = total_ref.shape[1]
        for plane in range(4):
            other = plane >> 1 if bit == 0 else plane & 1
            target = sent if (plane >> bit) & 1 else kept
            for k in range(layers):
                owner = me_ref[0] ^ (4 * k + plane)
                start = pl.multiple_of(owner * rows, 8)
                target[other, k, :, :width] = total_ref[pl.ds(start, rows), :].astype(low)
                if extra:
                    target[other, k, :, width:] = extra_ref[owner]


def weight_grad(lefts, parts, me, size, bits, turned=False, extra=None):
    widths = [sum(piece.shape[1] for piece in part[0]) for part in parts]
    layout = tuple(tuple(len(pieces) for pieces in part) for part in parts)
    rights = [piece for part in parts for pieces in part for piece in pieces]
    layers, rows = size // 4, D // size
    extras = () if extra is None else (extra,)
    more = 0 if extra is None else LANES
    if me is not None:
        outs = tuple(
            shape((2, layers, rows, width + more), low) for width in widths for _ in range(2)
        )
        scratch = [pltpu.VMEM((D, width), full) for width in widths]
    else:
        outs = tuple(shape((D, width), full) for width in widths)
        scratch = []
        me = jnp.zeros((1,), jnp.int32)
        bits = None
    tokens = sum(pieces[0].shape[0] for pieces in parts[0])

    def whole(array):
        return pl.BlockSpec(array.shape, lambda j, m: (0,) * len(array.shape))

    flat = (*lefts, *rights, *extras)
    return pl.pallas_call(
        partial(
            weight_grad_kernel, bits, layout, len(lefts), turned, extra is not None
        ),
        out_shape=outs,
        grid_spec=pltpu.PrefetchScalarGridSpec(
            num_scalar_prefetch=1,
            grid=(1,),
            in_specs=[whole(array) for array in flat],
            out_specs=tuple(whole(array) for array in outs),
            scratch_shapes=scratch,
        ),
        compiler_params=params(GRADS),
        cost_estimate=cost(2 * tokens * D * sum(widths), 2 * tokens * (D + sum(widths))),
        name="weight_grad",
    )(me, *flat)


def adamw(master, gradient, first_moment, second_moment, step_rate, decay_rate, correct):
    first_new = 0.5 * first_moment + 0.5 * gradient
    second_new = 0.5 * second_moment + 0.5 * gradient * gradient
    moved = first_new / correct / (jnp.sqrt(second_new / correct) + 1e-08)
    return (master - step_rate * (moved + decay_rate * master), first_new, second_new)


def per_device(
    activations,
    cotangent,
    token_weight,
    lengths,
    step_count,
    inward_weight,
    output_weight,
    up_weight,
    down_weight,
    heads_bias,
    hidden_bias,
    norm_vectors,
    *moments,
):
    size = lax.axis_size("dp")
    rows, width = inward_weight.shape[1], inward_weight.shape[2]
    hidden_width = up_weight.shape[1]
    groups = width // LANES
    tokens = activations.shape[0]
    count = tokens // LEN
    fast = size == 16 and rows % 16 == 0
    me = lax.axis_index("dp").astype(jnp.int32).reshape(1) if fast else None

    small = jnp.concatenate(
        [heads_bias.reshape(-1), hidden_bias.reshape(-1), norm_vectors.reshape(-1)]
    )
    per_row = small.shape[0] // rows
    small_block = jnp.pad(small.reshape(rows, per_row), ((0, 0), (0, LANES - per_row)))
    inward_shard = jnp.concatenate(
        [
            inward_weight.reshape(3, rows, groups, LANES)
            .transpose(1, 2, 0, 3)
            .reshape(rows, 3 * width),
            small_block,
        ],
        axis=1,
    ).astype(low)
    block = hidden_width // 2
    outward_at = 2 * block
    up_shard, down_shard = up_weight.astype(low), down_weight.T.astype(low)
    first_shard = jnp.concatenate(
        [up_shard[:, :block], down_shard[:, :block], output_weight.T.astype(low)], axis=1
    )
    last_shard = jnp.concatenate([up_shard[:, block:], down_shard[:, block:]], axis=1)

    if fast:
        found = gather_planes(inward_shard, size)
        found_first = gather_doubled(after(first_shard, *found[1:]), size)
        found_last = gather_doubled(after(last_shard, *found_first[1:]), size)
        turned = turn(activations)
        found[0] = after(found[0], turned)
        own = split_halves(found)
        pairs = gather_pairs(own, gather_near(own, size))
        far = gather_far(pairs, size)
        own_first = split_halves(found_first)
        far = after_all(far, *own_first)
        own_first = after_all(own_first, *far)
        inward = place(pairs, far, me)
        near_first = gather_near(own_first, size)
        inward = after(inward, *own_first)
    else:
        inward, mid_first, mid_last = [
            lax.all_gather(shard, "dp", axis=0, tiled=True)
            for shard in (inward_shard, first_shard, last_shard)
        ]
        turned = turn(activations)

    smalls = inward[:, 3 * width : 3 * width + per_row].astype(full).reshape(size, -1)
    heads_size, hidden_size = heads_bias.size, hidden_bias.size
    head_biases = (
        smalls[:, :heads_size].reshape(size, 2, -1).transpose(1, 2, 0).reshape(2, width)
    )
    hidden_biases = smalls[:, heads_size : heads_size + hidden_size].T.reshape(1, hidden_width)
    vectors = (
        smalls[:, heads_size + hidden_size :].reshape(size, 6, rows).transpose(1, 0, 2)
    ).reshape(6, D)

    live = lax.broadcasted_iota(jnp.int32, (count, LEN), 1) < lengths[:, None]
    scale = (token_weight.reshape(count, LEN) * live.astype(jnp.int32)).astype(full)
    scale = scale.reshape(tokens, 1)

    qkv, weights, contexts = [], [], []
    source = activations
    for group in range(groups):
        if fast and group == 1:
            near_first = after_all(near_first, contexts[-1])
            pairs_first = gather_pairs(own_first, near_first)
            far_first = gather_far(pairs_first, size)
            own_last = split_halves(list(after_all(found_last, *pairs_first)))
            near_last = gather_near(own_last, size)
            source = after(activations, *pairs_first, *own_last)
        elif group:
            source = after(activations, contexts[-1])
        parts = attend(lengths, source, inward, head_biases, group)
        for kept, part in zip((qkv, weights, contexts), parts):
            kept.append(part)
    if fast:
        pairs_last = gather_pairs(own_last, after_all(near_last, contexts[-1]))
        far_last = gather_far(pairs_last, size)
        mid_first = place(pairs_first, after_all(far_first, *pairs_last), me)

    mine = [outward_part(contexts, mid_first, outward_at, item) for item in range(count)]
    other = [swap_cores(part) for part in mine]
    opened = [
        expand_first(
            mine[item], other[item], activations, vectors, hidden_biases, mid_first, item
        )
        for item in range(count)
    ]
    totals, active_first, slope_first, middle, normed, inverse = zip(*opened)
    if fast:
        mid_last = place(pairs_last, after_all(far_last, *totals), me)
    closed = [
        expand_last(totals[item], middle[item], hidden_biases, mid_last) for item in range(count)
    ]
    mine_down, active_last, slope_last = zip(*closed)
    other_down = [swap_cores(part) for part in mine_down]
    turned_back = [
        contract(
            mine_down[item], other_down[item], normed[item], cotangent, scale, vectors,
            (slope_first[item], slope_last[item]), (mid_first, mid_last), item,
        )
        for item in range(count)
    ]
    (
        mine_middle, second_sums, hidden_sums, output_rows,
        second_grad, second_low, hidden_first, hidden_last,
    ) = zip(*turned_back)
    other_middle = [swap_cores(part) for part in mine_middle]

    def by_item(*arrays):
        return [[[piece] for piece in array] for array in arrays]

    def heads_outgoing(sums):
        return jnp.concatenate(sums, axis=1).reshape(2, -1, size).transpose(2, 0, 1)

    def back_first(start):
        return zip(
            *[
                first_back(
                    after(mine_middle[item], *start), other_middle[item], second_grad[item],
                    normed[item], inverse[item], vectors, mid_first, outward_at, width,
                )
                for item in range(count)
            ]
        )

    def small_outgoing(first_sums, head_sums):
        norm_grad = jnp.concatenate([sum(first_sums), sum(second_sums)])
        return jnp.concatenate(
            [
                heads_outgoing(head_sums).reshape(size, -1),
                sum(hidden_sums).reshape(-1, size).T,
                norm_grad.reshape(6, size, rows).transpose(1, 0, 2).reshape(size, -1),
            ],
            axis=1,
        )

    stacked, head_sums = [], []
    if fast:
        down_parts = [
            [[first, last] for first, last in zip(active_first, active_last)]
        ]
        up_parts = [[[first, last] for first, last in zip(hidden_first, hidden_last)]]
        sent_down, kept_down = weight_grad(second_low, down_parts, me, size, (0,))
        got_down = hop(sent_down, 1, size)
        middle_gate = after_all(middle, sent_down)
        sent_up, kept_up = weight_grad(middle_gate, up_parts, me, size, (1,))
        got_up = hop(sent_up, 2, size)
        first_sums, first_grad, first_low, context_grad = back_first((sent_up,))

        got_down = after(got_down, *first_low)
        next_down = kept_down[1] + got_down[1]
        more_down = hop(next_down, 2, size)
        sent_out, kept_out = weight_grad(
            after_all(first_low, next_down), [[contexts]], me, size, (0,)
        )
        got_out = hop(sent_out, 1, size)

        def attention(group, *gates):
            grads, sums = attend_back(
                after(qkv[group], *gates), weights[group], context_grad, group
            )
            stacked.append(grads)
            head_sums.append(sums)

        attention(0, sent_out)
        sent_0, kept_0 = weight_grad((turned,), [[[stacked[0]]]], me, size, (1,), True)
        got_0 = hop(sent_0, 2, size)
        got_up = after(got_up, sent_0)
        next_up = kept_up[1] + got_up[1]
        more_up = hop(next_up, 1, size)

        attention(1, next_up)
        got_out, got_0, more_down = after_all((got_out, got_0, more_down), stacked[1])
        next_out, next_0 = after_all((kept_out[1] + got_out[1], kept_0[1] + got_0[1]))
        more_out, more_0 = hop(next_out, 2, size), hop(next_0, 1, size)
        own_down, out_down = combine([(kept_down, got_down, more_down)])
        near_down = hop(out_down, 4, size)
        gated = after(turned, next_out, next_0, out_down)
        sent_1, kept_1 = weight_grad((gated,), [[[stacked[1]]]], me, size, (0,), True)
        got_1 = hop(sent_1, 1, size)

        attention(2, sent_1)
        extra = small_outgoing(first_sums, head_sums).reshape(size, rows, per_row)
        extra = jnp.pad(extra, ((0, 0), (0, 0), (0, LANES - per_row))).astype(low)
        more_up, near_down, more_out, more_0 = after_all(
            (more_up, near_down, more_out, more_0), stacked[2]
        )
        own_up, out_up = combine([(kept_up, got_up, more_up)])
        near_up = hop(out_up, 4, size)
        next_far = far_half(own_down, near_down)
        far_down = hop(next_far, 8, size)
        own_near, out_near = combine([(kept_out, got_out, more_out), (kept_0, got_0, more_0)])
        near_near = hop(out_near, 4, size)
        gated = after(turned, out_up, next_far, out_near)
        sent_2, kept_2 = weight_grad((gated,), [[[stacked[2]]]], me, size, (1,), True, extra)
        got_2 = hop(sent_2, 2, size)

        def source_of(item, *gates):
            return source_part([after(stacked[0], *gates)] + stacked[1:], inward, item)

        mine_source = [source_of(0, sent_2)]
        near_up = after(near_up, mine_source[0])
        next_far = far_half(own_up, near_up)
        far_up = hop(next_far, 8, size)
        mine_source.append(source_of(1, next_far))
        got_1, got_2 = after_all((got_1, got_2), mine_source[1])
        next_1, next_2 = after_all((kept_1[1] + got_1[1], kept_2[1] + got_2[1]))
        more_1, more_2 = hop(next_1, 2, size), hop(next_2, 1, size)
        mine_source.append(source_of(2, next_1, next_2))
        near_near, far_down = after_all((near_near, far_down), mine_source[2])
        next_far = far_half(own_near, near_near)
        far_near = hop(next_far, 8, size)
        more_1, more_2 = after_all((more_1, more_2), next_far)
        own_last, out_last = combine([(kept_1, got_1, more_1), (kept_2, got_2, more_2)])
        near_last = hop(out_last, 4, size)
        output_rows = jnp.concatenate(after_all(output_rows, out_last))
        other_source = [swap_cores(part) for part in mine_source]
        input_grad = finish(mine_source, after_all(other_source, out_last), first_grad)
        near_last = after(near_last, input_grad, output_rows)
        far_last = hop(far_half(own_last, near_last), 8, size)
        downward_grad = reduce_sum(own_down, near_down, far_down)
        upward_grad = reduce_sum(own_up, near_up, far_up)
        near_grad = reduce_sum(own_near, near_near, far_near)
        far_grad = reduce_sum(own_last, near_last, far_last)
        outward_grad = near_grad[:, :width]
        cut = 3 * LANES
        inward_grads = [near_grad[:, width:], far_grad[:, :cut], far_grad[:, cut : 2 * cut]]
        small_grad = far_grad[:, 2 * cut : 2 * cut + per_row].reshape(-1)
    else:

        def reduced(lefts, parts, turned=False):
            values = weight_grad(lefts, parts, None, size, None, turned)
            return lax.psum_scatter(
                jnp.concatenate(values, axis=1), "dp", scatter_dimension=0, tiled=True
            )

        first_sums, first_grad, first_low, context_grad = back_first(())
        downward_grad = reduced(second_low, by_item(active_first, active_last))
        upward_grad = reduced(middle, by_item(hidden_first, hidden_last))
        outward_grad = reduced(first_low, [[contexts]])
        inward_grads = []
        for group in range(groups):
            grads, sums = attend_back(qkv[group], weights[group], context_grad, group)
            stacked.append(grads)
            head_sums.append(sums)
            inward_grads.append(reduced((turned,), [[[grads]]], True))
        mine_source = [source_part(stacked, inward, item) for item in range(count)]
        small_grad = lax.psum_scatter(
            small_outgoing(first_sums, head_sums), "dp", scatter_dimension=0, tiled=True
        ).reshape(-1)
        other_source = [swap_cores(part) for part in mine_source]
        input_grad = finish(mine_source, other_source, first_grad)
        output_rows = jnp.concatenate(output_rows)

    inward_grad = jnp.stack(
        [
            jnp.concatenate(
                [grad[:, kind * LANES : (kind + 1) * LANES] for grad in inward_grads], axis=1
            )
            for kind in range(3)
        ]
    )
    grads = (
        inward_grad,
        outward_grad.T,
        upward_grad,
        downward_grad.T,
        small_grad[:heads_size].reshape(heads_bias.shape),
        small_grad[heads_size : heads_size + hidden_size].reshape(hidden_bias.shape),
        small_grad[heads_size + hidden_size :].reshape(norm_vectors.shape),
    )

    step_value = step_count[0].astype(full)
    correct = 1.0 - jnp.power(0.5, step_value)
    plan = (step_value + 4.0) / 12.0
    rates = (D ** (-0.5), (6 * D // LEN) ** (-0.5), D ** (-0.5), FF ** (-0.5), 0.5, 0.5, 0.3)
    decays = (0.01, 0.01, 0.01, 0.01, 0.0, 0.0, 0.0)
    masters = (
        inward_weight,
        output_weight,
        up_weight,
        down_weight,
        heads_bias,
        hidden_bias,
        norm_vectors,
    )
    results = [output_rows, input_grad]
    for at in range(7):
        results.extend(
            adamw(
                masters[at],
                grads[at],
                moments[at],
                moments[7 + at],
                rates[at] * plan,
                decays[at],
                correct,
            )
        )
    return tuple(results)


def solution(mesh):
    matrices = (
        P(None, "dp", "tensor"),
        P("tensor", "dp"),
        P("dp", "tensor"),
        P("tensor", "dp"),
        P(None, "tensor", "dp"),
        P("tensor", "dp"),
        P(None, "dp"),
    )
    in_specs = (
        (P("dp", None), P("dp", None), P("dp"), P("dp"), P()) + matrices + matrices + matrices
    )
    out_specs = (P("dp", None), P("dp", None)) + tuple(
        spec for spec in matrices for _ in range(3)
    )
    return jax.shard_map(
        per_device, mesh=mesh, in_specs=in_specs, out_specs=out_specs, check_vma=False
    )
```

```python
from functools import partial
import math

import jax
import jax.numpy as jnp
from jax import lax
from jax.experimental import pallas as pl
from jax.experimental.pallas import tpu as pltpu
from jax.sharding import PartitionSpec as P

D = 768
HEAD_DIM = 64
FF = 3072
LEN = 512
LANES = 128
ROWS = 256
COST_SHARE = 1
ATTEND, BACK, EXPAND, CONTRACT, GRADS = 12, 12, 16, 24, 20

norm_epsilon = 1e-12
low = jnp.bfloat16
full = jnp.float32


def dot_nn(left, right):
    return lax.dot_general(left, right, (((1,), (0,)), ((), ())), preferred_element_type=full)


def dot_nt(left, right):
    return lax.dot_general(left, right, (((1,), (1,)), ((), ())), preferred_element_type=full)


def column_sum(values):
    return jnp.sum(values, axis=0, keepdims=True)


def row_mean(values):
    return jnp.mean(values, axis=-1, keepdims=True)


def normalize(total_in):
    centred = total_in - row_mean(total_in)
    inverse = lax.rsqrt(row_mean(centred * centred) + norm_epsilon)
    return (centred * inverse, inverse)


def norm_back(incoming, normed, inverse, gain):
    scaled = incoming * gain
    return inverse * (scaled - row_mean(scaled) - normed * row_mean(scaled * normed))


def cost(flops, moved, exps=0):
    return pl.CostEstimate(
        flops=int(flops / COST_SHARE),
        bytes_accessed=int(moved / COST_SHARE),
        transcendentals=int(exps / COST_SHARE),
    )


def params(mebibytes=12):
    return pltpu.CompilerParams(vmem_limit_bytes=mebibytes * 1024 * 1024)


def shape(dims, kind):
    return jax.ShapeDtypeStruct(dims, kind)


def main(dims, kind):
    return pltpu.HBM(dims, kind)


def streamed(*arrays):
    return [pltpu.with_memory_space_constraint(array, pltpu.HBM) for array in arrays]


def after(value, *others):
    return lax.optimization_barrier((value,) + others)[0]


def after_all(values, *others):
    return lax.optimization_barrier(tuple(values) + others)[: len(values)]


def hop(value, offset, size):
    return lax.ppermute(value, "dp", [(d, d ^ offset) for d in range(size)])


def swap_cores(value):
    return lax.ppermute(value, "tensor", [(0, 1), (1, 0)])


def split_columns(width):
    return -(-width // (2 * LANES)) * LANES


def gather_planes(shard, size):
    found = [shard] + [hop(shard, 4 * k, size) for k in range(1, size // 4)]
    return found


def gather_doubled(shard, size):
    pair = jnp.stack([shard, hop(shard, 8, size)])
    return (pair, hop(pair, 4, size))


def doubled_planes(pair, near):
    return [pair[0], near[0], pair[1], near[1]]


def split_halves(found):
    stacked = jnp.stack(found)
    cut = split_columns(stacked.shape[2])
    return lax.optimization_barrier((stacked[..., :cut], stacked[..., cut:]))


def gather_near(own, size):
    return (hop(own[0], 2, size), hop(own[1], 1, size))


def gather_pairs(own, near):
    return lax.optimization_barrier(
        (jnp.concatenate([own[0], near[0]]), jnp.concatenate([own[1], near[1]]))
    )


def gather_far(pairs, size):
    return (hop(pairs[0], 1, size), hop(pairs[1], 2, size))


def place_kernel(me_ref, pair_a, far_a, pair_b, far_b, out_ref):
    layers, rows, cut = pair_a.shape
    layers //= 2
    sources = (
        (pair_a, 0, pair_b, 0),
        (far_a, 0, pair_b, layers),
        (pair_a, layers, far_b, 0),
        (far_a, layers, far_b, layers),
    )
    for plane, (left, left_at, right, right_at) in enumerate(sources):
        for k in range(layers):
            start = pl.multiple_of((me_ref[0] ^ (4 * k + plane)) * rows, 16)
            out_ref[pl.ds(start, rows), :cut] = left[left_at + k]
            out_ref[pl.ds(start, rows), cut:] = right[right_at + k]


def place(pairs, far, me):
    flat = (pairs[0], far[0], pairs[1], far[1])
    layers, rows, cut = pairs[0].shape
    width = cut + pairs[1].shape[2]
    total = 2 * layers * rows
    return pl.pallas_call(
        place_kernel,
        out_shape=shape((total, width), low),
        grid_spec=pltpu.PrefetchScalarGridSpec(
            num_scalar_prefetch=1,
            grid=(1,),
            in_specs=[pl.BlockSpec(piece.shape, lambda i, m: (0, 0, 0)) for piece in flat],
            out_specs=pl.BlockSpec((total, width), lambda i, m: (0, 0)),
        ),
        compiler_params=params(12),
        cost_estimate=cost(0, 4 * total * width),
        name="place",
    )(me, *flat)


def turn_kernel(source_ref, out_ref):
    out_ref[...] = source_ref[...].astype(full).T.astype(low)


def turn(source):
    rows, width = source.shape
    return pl.pallas_call(
        turn_kernel,
        out_shape=shape((width, rows), low),
        grid=(rows // LEN,),
        in_specs=[pl.BlockSpec((LEN, width), lambda i: (i, 0))],
        out_specs=pl.BlockSpec((width, LEN), lambda i: (0, i)),
        compiler_params=params(16),
        cost_estimate=cost(0, 4 * rows * width),
        name="turn",
    )(source)


def combine_kernel(count, *refs):
    own_ref, out_ref = refs[-2:]
    start = 0
    for at in range(count):
        kept, got, more = refs[3 * at : 3 * at + 3]
        total = kept[0].astype(full) + got[0].astype(full) + more[...].astype(full)
        width = total.shape[2]
        for k in range(total.shape[0]):
            if k % 2:
                out_ref[k // 2, :, start : start + width] = total[k].astype(low)
            else:
                own_ref[k // 2, :, start : start + width] = total[k]
        start += width


def combine(halves):
    layers, rows = halves[0][2].shape[:2]
    width = sum(more.shape[2] for _, _, more in halves)
    flat, specs = [], []
    for kept, got, more in halves:
        part = (1,) + more.shape
        flat += [kept, got, more]
        specs += [pl.BlockSpec(part, lambda i: (0, 0, 0, 0))] * 2
        specs += [pl.BlockSpec(more.shape, lambda i: (0, 0, 0))]
    piece = (layers // 2, rows, width)
    return pl.pallas_call(
        partial(combine_kernel, len(halves)),
        out_shape=(shape(piece, full), shape(piece, low)),
        grid=(1,),
        in_specs=specs,
        out_specs=(pl.BlockSpec(piece, lambda i: (0, 0, 0)),) * 2,
        compiler_params=params(16),
        cost_estimate=cost(3 * layers * rows * width, 8 * layers * rows * width),
        name="combine",
    )(*flat)


def far_half(own, near):
    return (own[1] + near[1].astype(full)).astype(low)


def reduce_sum(own, near, far):
    return own[0] + near[0].astype(full) + far.astype(full)


def attend_kernel(length_ref, x_ref, w_ref, bias_ref, qkv_ref, weight_ref, context_ref):
    length = length_ref[pl.program_id(1)]
    mixed = dot_nn(x_ref[...], w_ref[...])
    queries = (mixed[:, :LANES] + bias_ref[0:1, :]).astype(low)
    key_rows = mixed[:, LANES : 2 * LANES].astype(low)
    values_full = mixed[:, 2 * LANES :] + bias_ref[1:2, :]
    values = values_full.astype(low)
    qkv_ref[:, :LANES] = queries
    qkv_ref[:, LANES : 2 * LANES] = key_rows
    qkv_ref[:, 2 * LANES :] = values
    values_t = values_full.T.astype(low)
    rows = queries.shape[0]
    lane = lax.broadcasted_iota(jnp.int32, (rows, LANES), 1)
    live = lax.broadcasted_iota(jnp.int32, (rows, 1), 0) < length
    scaled = queries * (1.0 / math.sqrt(HEAD_DIM))
    parts = []
    for head in range(2):
        picked = jnp.where((lane >= HEAD_DIM) == bool(head), scaled, jnp.zeros_like(scaled))
        scores = jnp.where(live, dot_nt(key_rows, picked), -jnp.inf)
        grown = jnp.exp(scores - jnp.max(scores, axis=0, keepdims=True))
        weights = (grown * (1.0 / jnp.sum(grown, axis=0, keepdims=True))).astype(low)
        weight_ref[0, head] = weights
        parts.append(dot_nn(values_t[head * HEAD_DIM : (head + 1) * HEAD_DIM, :], weights))
    context_ref[...] = jnp.concatenate(parts, axis=0).T.astype(low)


def attend(lengths, source, inward, biases, first, groups):
    rows = source.shape[0]
    count = rows // LEN
    width = 3 * LANES
    return pl.pallas_call(
        attend_kernel,
        out_shape=(
            main((rows, groups * width), low),
            main((groups * count, 2, LEN, LEN), low),
            main((rows, groups * LANES), low),
        ),
        grid_spec=pltpu.PrefetchScalarGridSpec(
            num_scalar_prefetch=1,
            grid=(groups, count),
            in_specs=[
                pl.BlockSpec((LEN, D), lambda g, s, n: (s, 0)),
                pl.BlockSpec((D, width), lambda g, s, n: (0, first + g)),
                pl.BlockSpec((2, LANES), lambda g, s, n: (0, first + g)),
            ],
            out_specs=(
                pl.BlockSpec((LEN, width), lambda g, s, n: (s, g)),
                pl.BlockSpec((1, 2, LEN, LEN), lambda g, s, n: (g * count + s, 0, 0, 0)),
                pl.BlockSpec((LEN, LANES), lambda g, s, n: (s, g)),
            ),
        ),
        compiler_params=params(ATTEND),
        cost_estimate=cost(
            groups * (2 * rows * D * width + 8 * count * LEN * LEN * LANES),
            groups * count * 2 * LEN * LEN * 2,
            groups * count * 2 * LEN * LEN,
        ),
        name="attend",
    )(lengths, *streamed(source), inward, biases)


def attend_back_kernel(qkv_ref, weight_ref, grad_ref, out_ref, sum_ref):
    @pl.when(pl.program_id(0) == 0)
    def _():
        sum_ref[...] = jnp.zeros_like(sum_ref)

    queries = qkv_ref[:, :LANES]
    key_rows = qkv_ref[:, LANES : 2 * LANES]
    values = qkv_ref[:, 2 * LANES :]
    grads = grad_ref[...]
    keys_t = key_rows.astype(full).T.astype(low)
    rows = queries.shape[0]
    lane = lax.broadcasted_iota(jnp.int32, (rows, LANES), 1)
    score_scale = 1.0 / math.sqrt(HEAD_DIM)
    query_parts, key_parts, value_parts = [], [], []
    for head in range(2):
        picked = jnp.where((lane >= HEAD_DIM) == bool(head), grads, jnp.zeros_like(grads))
        weights = weight_ref[0, head]
        wide = weights.astype(full)
        mixed = wide * dot_nt(values, picked)
        score_grads = (mixed - wide * jnp.sum(mixed, axis=0, keepdims=True)).astype(low)
        value_parts.append(dot_nn(weights, grads))
        key_parts.append(dot_nn(score_grads, queries))
        query_parts.append(
            dot_nn(keys_t[head * HEAD_DIM : (head + 1) * HEAD_DIM, :], score_grads)
        )
    first = lane < HEAD_DIM
    query_grads = (jnp.concatenate(query_parts, axis=0).T * score_scale).astype(low)
    key_grads = (jnp.where(first, key_parts[0], key_parts[1]) * score_scale).astype(low)
    value_grads = jnp.where(first, value_parts[0], value_parts[1]).astype(low)
    out_ref[:, :LANES] = query_grads
    out_ref[:, LANES : 2 * LANES] = key_grads
    out_ref[:, 2 * LANES :] = value_grads
    sum_ref[0:1, :] += column_sum(query_grads.astype(full))
    sum_ref[1:2, :] += column_sum(value_grads.astype(full))


def attend_back(qkv, weights, at, grads, group):
    rows = qkv.shape[0]
    count = rows // LEN
    width = 3 * LANES
    return pl.pallas_call(
        attend_back_kernel,
        out_shape=(main((rows, width), low), shape((2, LANES), full)),
        grid=(count,),
        in_specs=[
            pl.BlockSpec((LEN, width), lambda s: (s, at)),
            pl.BlockSpec((1, 2, LEN, LEN), lambda s: (at * count + s, 0, 0, 0)),
            pl.BlockSpec((LEN, LANES), lambda s: (s, group)),
        ],
        out_specs=(
            pl.BlockSpec((LEN, width), lambda s: (s, 0)),
            pl.BlockSpec((2, LANES), lambda s: (0, 0)),
        ),
        compiler_params=params(BACK),
        cost_estimate=cost(
            16 * count * LEN * LEN * LANES, count * 2 * LEN * LEN * 2 + 4 * rows * width
        ),
        name="attend_back",
    )(*streamed(qkv, weights, grads))


def outward_kernel(*refs):
    contexts, w_ref, out_ref = refs[:-2], refs[-2], refs[-1]
    context = jnp.concatenate([ref[...] for ref in contexts], axis=1)
    out_ref[...] = dot_nt(context, w_ref[...]).astype(low)


def row_block(width):
    return pl.BlockSpec((ROWS, width), lambda i: (i, 0))


def fixed_block(dims, at=0):
    return pl.BlockSpec(dims, lambda i: (0, at))


def outward_part(contexts, mid, outward_at):
    rows = contexts[0].shape[0]
    width = sum(context.shape[1] for context in contexts)
    return pl.pallas_call(
        outward_kernel,
        out_shape=shape((rows, D), low),
        grid=(rows // ROWS,),
        in_specs=[row_block(context.shape[1]) for context in contexts]
        + [fixed_block((D, width), outward_at // width)],
        out_specs=row_block(D),
        compiler_params=params(),
        cost_estimate=cost(2 * rows * D * width, 2 * (rows * D + rows * width + D * width)),
        name="outward",
    )(*streamed(*contexts), mid)


def gelu_parts(hidden):
    half = 0.5 + 0.5 * lax.erf(hidden * 0.7071067811865476)
    slope = half + hidden * 0.3989422804014327 * jnp.exp(-0.5 * hidden * hidden)
    return ((hidden * half).astype(low), slope.astype(low))


def expand_first_kernel(
    mine_ref, other_ref, x_ref, vector_ref, bias_ref, up_ref, down_ref,
    total_ref, active_ref, slope_ref, middle_ref, normed_ref, inverse_ref,
):
    summed = (
        mine_ref[...].astype(full)
        + other_ref[...].astype(full)
        + vector_ref[0:1, :]
        + x_ref[...].astype(full)
    )
    normed, inverse = normalize(summed)
    normed_ref[...] = normed
    inverse_ref[...] = inverse
    held = (normed * vector_ref[1:2, :] + vector_ref[2:3, :]).astype(low)
    middle_ref[...] = held
    active, slope = gelu_parts(dot_nn(held, up_ref[...]) + bias_ref[...])
    active_ref[...] = active
    slope_ref[...] = slope
    total_ref[...] = dot_nt(active, down_ref[...])


def expand_first(mine, other, source, vectors, hidden_bias, mid):
    rows, hidden = source.shape[0], hidden_bias.shape[1]
    block = hidden // 2
    return pl.pallas_call(
        expand_first_kernel,
        out_shape=(
            main((rows, D), full),
            main((rows, block), low),
            main((rows, block), low),
            main((rows, D), low),
            main((rows, D), full),
            main((rows, 1), full),
        ),
        grid=(rows // ROWS,),
        in_specs=[
            row_block(D),
            row_block(D),
            row_block(D),
            fixed_block(vectors.shape),
            fixed_block((1, block)),
            fixed_block((D, block)),
            fixed_block((D, block), 1),
        ],
        out_specs=(
            row_block(D), row_block(block), row_block(block), row_block(D), row_block(D),
            row_block(1),
        ),
        compiler_params=params(EXPAND),
        cost_estimate=cost(4 * rows * D * block, 4 * D * block + 16 * rows * D, 2 * rows * block),
        name="expand_first",
    )(mine, other, *streamed(source), vectors, hidden_bias, mid, mid)


def expand_last_kernel(
    total_ref, middle_ref, bias_ref, up_ref, down_ref, part_ref, active_ref, slope_ref
):
    active, slope = gelu_parts(dot_nn(middle_ref[...], up_ref[...]) + bias_ref[...])
    active_ref[...] = active
    slope_ref[...] = slope
    part_ref[...] = (total_ref[...] + dot_nt(active, down_ref[...])).astype(low)


def expand_last(total, middle, hidden_bias, mid):
    rows, hidden = total.shape[0], hidden_bias.shape[1]
    block = hidden // 2
    return pl.pallas_call(
        expand_last_kernel,
        out_shape=(shape((rows, D), low), main((rows, block), low), main((rows, block), low)),
        grid=(rows // ROWS,),
        in_specs=[
            row_block(D),
            row_block(D),
            fixed_block((1, block), 1),
            fixed_block((D, block)),
            fixed_block((D, block), 1),
        ],
        out_specs=(row_block(D), row_block(block), row_block(block)),
        compiler_params=params(EXPAND),
        cost_estimate=cost(4 * rows * D * block, 4 * D * block + 10 * rows * D, 2 * rows * block),
        name="expand_last",
    )(*streamed(total, middle), hidden_bias, mid, mid)


def contract_kernel(
    mine_ref, other_ref, normed_ref, cotangent_ref, scale_ref, vector_ref,
    slope_first, slope_last, up_first, down_first, up_last, down_last,
    part_ref, sum_ref, hidden_sum_ref, out_ref, wide_ref, low_ref, hidden_first, hidden_last,
):
    @pl.when(pl.program_id(0) == 0)
    def _():
        sum_ref[...] = jnp.zeros_like(sum_ref)
        hidden_sum_ref[...] = jnp.zeros_like(hidden_sum_ref)

    middle = normed_ref[...] * vector_ref[1:2, :] + vector_ref[2:3, :]
    summed = (
        mine_ref[...].astype(full) + other_ref[...].astype(full) + vector_ref[3:4, :] + middle
    )
    normed, inverse = normalize(summed)
    out_ref[...] = (normed * vector_ref[4:5, :] + vector_ref[5:6, :]).astype(low)
    incoming = cotangent_ref[...].astype(full) * scale_ref[...]
    second = norm_back(incoming, normed, inverse, vector_ref[4:5, :])
    sum_ref[0:1, :] += column_sum(second)
    sum_ref[1:2, :] += column_sum(incoming * normed)
    sum_ref[2:3, :] += column_sum(incoming)
    wide_ref[...] = second
    held = second.astype(low)
    low_ref[...] = held
    block = up_first.shape[1]
    total = None
    for at, slope_ref, up_ref, down_ref, hidden_ref in (
        (0, slope_first, up_first, down_first, hidden_first),
        (block, slope_last, up_last, down_last, hidden_last),
    ):
        hidden_grad = (dot_nn(held, down_ref[...]) * slope_ref[...].astype(full)).astype(low)
        hidden_ref[...] = hidden_grad
        hidden_sum_ref[:, at : at + block] += column_sum(hidden_grad.astype(full))
        part = dot_nt(hidden_grad, up_ref[...])
        total = part if total is None else total + part
    part_ref[...] = total.astype(low)


def contract(mine, other, normed, cotangent, scale, vectors, slopes, mids):
    rows, block = slopes[0].shape
    hidden = 2 * block
    weights = [fixed_block((D, block)), fixed_block((D, block), 1)]
    return pl.pallas_call(
        contract_kernel,
        out_shape=(
            shape((rows, D), low),
            shape((3, D), full),
            shape((1, hidden), full),
            main((rows, D), low),
            main((rows, D), full),
            main((rows, D), low),
            main((rows, block), low),
            main((rows, block), low),
        ),
        grid=(rows // ROWS,),
        in_specs=[
            row_block(D),
            row_block(D),
            row_block(D),
            row_block(D),
            row_block(1),
            fixed_block(vectors.shape),
            row_block(block),
            row_block(block),
        ]
        + weights
        + weights,
        out_specs=(
            row_block(D),
            fixed_block((3, D)),
            fixed_block((1, hidden)),
            row_block(D),
            row_block(D),
            row_block(D),
            row_block(block),
            row_block(block),
        ),
        compiler_params=params(CONTRACT),
        cost_estimate=cost(4 * rows * D * hidden, 4 * D * hidden + 4 * rows * hidden),
        name="contract",
    )(
        mine, other, *streamed(normed, cotangent), scale, vectors, *streamed(*slopes),
        mids[0], mids[0], mids[1], mids[1],
    )


def first_back_kernel(
    mine_ref, other_ref, second_ref, normed_ref, inverse_ref, vector_ref, w_ref,
    sum_ref, wide_ref, low_ref, grad_ref,
):
    @pl.when(pl.program_id(0) == 0)
    def _():
        sum_ref[...] = jnp.zeros_like(sum_ref)

    incoming = mine_ref[...].astype(full) + other_ref[...].astype(full) + second_ref[...]
    normed = normed_ref[...]
    first = norm_back(incoming, normed, inverse_ref[...], vector_ref[1:2, :])
    sum_ref[0:1, :] += column_sum(first)
    sum_ref[1:2, :] += column_sum(incoming * normed)
    sum_ref[2:3, :] += column_sum(incoming)
    wide_ref[...] = first
    held = first.astype(low)
    low_ref[...] = held
    grad_ref[...] = dot_nn(held, w_ref[...]).astype(low)


def first_back(mine, other, second, normed, inverse, vectors, mid, outward_at, width):
    rows = second.shape[0]
    return pl.pallas_call(
        first_back_kernel,
        out_shape=(
            shape((3, D), full),
            main((rows, D), full),
            main((rows, D), low),
            main((rows, width), low),
        ),
        grid=(rows // ROWS,),
        in_specs=[row_block(D)] * 4
        + [
            row_block(1),
            fixed_block(vectors.shape),
            fixed_block((D, width), outward_at // width),
        ],
        out_specs=(fixed_block((3, D)), row_block(D), row_block(D), row_block(width)),
        compiler_params=params(BACK),
        cost_estimate=cost(2 * rows * D * width, 20 * rows * D),
        name="first_back",
    )(mine, other, *streamed(second, normed, inverse), vectors, mid)


def source_kernel(*refs):
    grads, weights, out_ref = refs[:-2], refs[-2], refs[-1]
    width = 3 * LANES
    total = None
    for group, grad_ref in enumerate(grads):
        part = dot_nt(grad_ref[...], weights[:, group * width : (group + 1) * width])
        total = part if total is None else total + part
    out_ref[...] = total.astype(low)


def source_part(grads, inward):
    rows, width = grads[0].shape
    groups = len(grads)
    return pl.pallas_call(
        source_kernel,
        out_shape=shape((rows, D), low),
        grid=(rows // ROWS,),
        in_specs=[row_block(width) for _ in grads] + [fixed_block((D, groups * width))],
        out_specs=row_block(D),
        compiler_params=params(),
        cost_estimate=cost(2 * rows * D * width * groups, 2 * (rows + D) * width * groups),
        name="source",
    )(*streamed(*grads), inward)


def finish_kernel(mine_ref, other_ref, first_ref, out_ref):
    out_ref[...] = mine_ref[...].astype(full) + other_ref[...].astype(full) + first_ref[...]


def finish(mine, other, first):
    rows = first.shape[0]
    return pl.pallas_call(
        finish_kernel,
        out_shape=main((rows, D), full),
        grid=(rows // ROWS,),
        in_specs=[row_block(D)] * 3,
        out_specs=row_block(D),
        compiler_params=params(),
        cost_estimate=cost(2 * rows * D, 12 * rows * D),
        name="finish",
    )(mine, other, *streamed(first))


def weight_grad_kernel(bit, count, turned, extra, me_ref, left_ref, *refs):
    rights, refs = refs[:count], refs[count:]
    if extra:
        extra_ref, refs = refs[0], refs[1:]
    left = left_ref
    if not turned:
        left, refs = refs[-1], refs[:-1]

        def turn_block(i, carry):
            start = pl.multiple_of(i * ROWS, ROWS)
            block = left_ref[pl.ds(start, ROWS), :].astype(full)
            left[:, pl.ds(start, ROWS)] = block.T.astype(low)
            return carry

        lax.fori_loop(0, left_ref.shape[0] // ROWS, turn_block, 0, unroll=True)
    total_ref = refs[-1] if bit is not None else refs[0]
    block = 2 * ROWS if rights[0].shape[1] % D else D
    if rights[0].shape[1] % block:
        right = jnp.concatenate([piece[...] for piece in rights], axis=1)
        total_ref[...] = dot_nn(left[...], right)
    else:
        for at, piece in enumerate(rights):
            steps = piece.shape[1] // block

            def multiply(j, carry, at=at, piece=piece, steps=steps):
                start = pl.multiple_of(j * block, LANES)
                into = pl.multiple_of((at * steps + j) * block, LANES)
                total_ref[:, pl.ds(into, block)] = dot_nn(
                    left[...], piece[:, pl.ds(start, block)]
                )
                return carry

            if steps == 1:
                multiply(0, 0)
            else:
                lax.fori_loop(0, steps, multiply, 0)
    if bit is None:
        return
    layers, rows = refs[0].shape[1:3]
    width = total_ref.shape[1]
    for target, far in ((refs[0], 1), (refs[1], 0)):

        def spread(i, carry, target=target, far=far):
            other, k = i // layers, i % layers
            plane = 2 * other + far if bit == 0 else other + 2 * far
            owner = me_ref[0] ^ (4 * k + plane)
            start = pl.multiple_of(owner * rows, 8)
            target[other, k, :, :width] = total_ref[pl.ds(start, rows), :].astype(low)
            if extra:
                target[other, k, :, width:] = extra_ref[owner]
            return carry

        lax.fori_loop(0, 2 * layers, spread, 0)


def weight_grad(left, rights, me, size, bit, turned=False, extra=None):
    tokens = rights[0].shape[0]
    width = sum(right.shape[1] for right in rights)
    layers, rows = size // 4, D // size
    extras = () if extra is None else (extra,)
    if me is not None:
        total = width + (0 if extra is None else LANES)
        outs = (shape((2, layers, rows, total), low),) * 2
        scratch = [pltpu.VMEM((D, width), full)]
    else:
        outs = (shape((D, width), full),)
        scratch = []
        me = jnp.zeros((1,), jnp.int32)
        bit = None
    if not turned:
        scratch.append(pltpu.VMEM((D, tokens), low))

    def whole(array):
        return pl.BlockSpec(array.shape, lambda j, m: (0,) * len(array.shape))

    flat = (left, *rights, *extras)
    return pl.pallas_call(
        partial(weight_grad_kernel, bit, len(rights), turned, extra is not None),
        out_shape=outs,
        grid_spec=pltpu.PrefetchScalarGridSpec(
            num_scalar_prefetch=1,
            grid=(1,),
            in_specs=[whole(array) for array in flat],
            out_specs=tuple(whole(array) for array in outs),
            scratch_shapes=scratch,
        ),
        compiler_params=params(GRADS),
        cost_estimate=cost(2 * tokens * D * width, 2 * tokens * (D + width)),
        name="weight_grad",
    )(me, *flat)


def adamw(master, gradient, first_moment, second_moment, step_rate, decay_rate, correct):
    first_new = 0.5 * first_moment + 0.5 * gradient
    second_new = 0.5 * second_moment + 0.5 * gradient * gradient
    moved = first_new / correct / (jnp.sqrt(second_new / correct) + 1e-08)
    return (master - step_rate * (moved + decay_rate * master), first_new, second_new)


def per_device(
    activations,
    cotangent,
    token_weight,
    lengths,
    step_count,
    inward_weight,
    output_weight,
    up_weight,
    down_weight,
    heads_bias,
    hidden_bias,
    norm_vectors,
    *moments,
):
    size = lax.axis_size("dp")
    rows, width = inward_weight.shape[1], inward_weight.shape[2]
    hidden_width = up_weight.shape[1]
    groups = width // LANES
    tokens = activations.shape[0]
    count = tokens // LEN
    fast = size == 16 and rows % 16 == 0
    me = lax.axis_index("dp").astype(jnp.int32).reshape(1) if fast else None

    small = jnp.concatenate(
        [heads_bias.reshape(-1), hidden_bias.reshape(-1), norm_vectors.reshape(-1)]
    )
    per_row = small.shape[0] // rows
    small_block = jnp.pad(small.reshape(rows, per_row), ((0, 0), (0, LANES - per_row)))
    inward_shard = jnp.concatenate(
        [
            inward_weight.reshape(3, rows, groups, LANES)
            .transpose(1, 2, 0, 3)
            .reshape(rows, 3 * width),
            small_block,
        ],
        axis=1,
    ).astype(low)
    block = hidden_width // 2
    outward_at = 2 * block
    up_shard, down_shard = up_weight.astype(low), down_weight.T.astype(low)
    first_shard = jnp.concatenate(
        [up_shard[:, :block], down_shard[:, :block], output_weight.T.astype(low)], axis=1
    )
    last_shard = jnp.concatenate([up_shard[:, block:], down_shard[:, block:]], axis=1)

    if fast:
        found = gather_planes(inward_shard, size)
        found_first = gather_doubled(after(first_shard, *found[1:]), size)
        found_last = gather_doubled(after(last_shard, found_first[1]), size)
        turned = turn(activations)
        found[0] = after(found[0], turned)
        own = split_halves(found)
        pairs = gather_pairs(own, gather_near(own, size))
        far = gather_far(pairs, size)
        own_first = split_halves(doubled_planes(*found_first))
        far = after_all(far, *own_first)
        own_first = after_all(own_first, *far)
        inward = place(pairs, far, me)
        near_first = gather_near(own_first, size)
        inward = after(inward, *own_first)
    else:
        inward, mid_first, mid_last = [
            lax.all_gather(shard, "dp", axis=0, tiled=True)
            for shard in (inward_shard, first_shard, last_shard)
        ]
        turned = turn(activations)

    smalls = inward[:, 3 * width : 3 * width + per_row].astype(full).reshape(size, -1)
    heads_size, hidden_size = heads_bias.size, hidden_bias.size
    head_biases = (
        smalls[:, :heads_size].reshape(size, 2, -1).transpose(1, 2, 0).reshape(2, width)
    )
    hidden_biases = smalls[:, heads_size : heads_size + hidden_size].T.reshape(1, hidden_width)
    vectors = (
        smalls[:, heads_size + hidden_size :].reshape(size, 6, rows).transpose(1, 0, 2)
    ).reshape(6, D)

    live = lax.broadcasted_iota(jnp.int32, (count, LEN), 1) < lengths[:, None]
    scale = (token_weight.reshape(count, LEN) * live.astype(jnp.int32)).astype(full)
    scale = scale.reshape(tokens, 1)

    first_pair = attend(lengths, activations, inward, head_biases, 0, 1)
    if fast:
        near_first = after_all(near_first, first_pair[2])
        pairs_first = gather_pairs(own_first, near_first)
        far_first = gather_far(pairs_first, size)
        own_last = split_halves(doubled_planes(*after_all(found_last, *pairs_first)))
        near_last = gather_near(own_last, size)
        gated = after(activations, *pairs_first, *own_last, vectors, hidden_biases)
    else:
        gated = after(activations, first_pair[2])
    later_pairs = attend(lengths, gated, inward, head_biases, 1, groups - 1)
    contexts = [first_pair[2], later_pairs[2]]
    if fast:
        pairs_last = gather_pairs(own_last, after_all(near_last, later_pairs[2]))
        far_last = gather_far(pairs_last, size)
        mid_first = place(pairs_first, after_all(far_first, *pairs_last), me)

    mine = outward_part(contexts, mid_first, outward_at)
    total, active_first, slope_first, middle, normed, inverse = expand_first(
        mine, swap_cores(mine), activations, vectors, hidden_biases, mid_first
    )
    if fast:
        mid_last = place(pairs_last, after_all(far_last, total), me)
    mine_down, active_last, slope_last = expand_last(total, middle, hidden_biases, mid_last)
    (
        mine_middle, second_sums, hidden_sums, output_rows,
        second_grad, second_low, hidden_first, hidden_last,
    ) = contract(
        mine_down, swap_cores(mine_down), normed, cotangent, scale, vectors,
        (slope_first, slope_last), (mid_first, mid_last),
    )
    other_middle = swap_cores(mine_middle)
    actives, hiddens = (active_first, active_last), (hidden_first, hidden_last)

    def back_first(*gates):
        return first_back(
            after(mine_middle, *gates), other_middle, second_grad, normed, inverse, vectors,
            mid_first, outward_at, width,
        )

    def attention_grads(group, *gates):
        at = max(group - 1, 0)
        qkv, weights, _ = later_pairs if group else first_pair
        return attend_back(after(qkv, *gates), weights, at, context_grad, group)

    def heads_outgoing(sums):
        return jnp.concatenate(sums, axis=1).reshape(2, -1, size).transpose(2, 0, 1)

    def small_outgoing(first_sums, head_sums):
        norm_grad = jnp.concatenate([first_sums, second_sums])
        return jnp.concatenate(
            [
                heads_outgoing(head_sums).reshape(size, -1),
                hidden_sums.reshape(-1, size).T,
                norm_grad.reshape(6, size, rows).transpose(1, 0, 2).reshape(size, -1),
            ],
            axis=1,
        )

    stacked, head_sums = [], []
    if fast:
        sent_down, kept_down = weight_grad(second_low, actives, me, size, 0)
        got_down = hop(sent_down, 1, size)
        sent_up, kept_up = weight_grad(after(middle, sent_down), hiddens, me, size, 1)
        got_up = hop(sent_up, 2, size)
        first_sums, first_grad, first_low, context_grad = back_first(sent_up)

        got_down = after(got_down, first_low)
        next_down = kept_down[1] + got_down[1]
        more_down = hop(next_down, 2, size)
        sent_out, kept_out = weight_grad(after(first_low, next_down), contexts, me, size, 0)
        got_out = hop(sent_out, 1, size)

        def attention(group, *gates):
            grads, sums = attention_grads(group, *gates)
            stacked.append(grads)
            head_sums.append(sums)

        attention(0, sent_out)
        sent_0, kept_0 = weight_grad(turned, [stacked[0]], me, size, 1, True)
        got_0 = hop(sent_0, 2, size)
        got_up = after(got_up, sent_0)
        next_up = kept_up[1] + got_up[1]
        more_up = hop(next_up, 1, size)

        attention(1, next_up)
        got_out, got_0, more_down = after_all((got_out, got_0, more_down), stacked[1])
        next_out, next_0 = after_all((kept_out[1] + got_out[1], kept_0[1] + got_0[1]))
        more_out, more_0 = hop(next_out, 2, size), hop(next_0, 1, size)
        own_down, out_down = combine([(kept_down, got_down, more_down)])
        near_down = hop(out_down, 4, size)
        gated = after(turned, next_out, next_0, out_down)
        sent_1, kept_1 = weight_grad(gated, [stacked[1]], me, size, 0, True)
        got_1 = hop(sent_1, 1, size)

        attention(2, sent_1)
        extra = small_outgoing(first_sums, head_sums).reshape(size, rows, per_row)
        extra = jnp.pad(extra, ((0, 0), (0, 0), (0, LANES - per_row))).astype(low)
        more_up, near_down, more_out, more_0 = after_all(
            (more_up, near_down, more_out, more_0), stacked[2]
        )
        own_up, out_up = combine([(kept_up, got_up, more_up)])
        near_up = hop(out_up, 4, size)
        next_far = far_half(own_down, near_down)
        far_down = hop(next_far, 8, size)
        own_near, out_near = combine([(kept_out, got_out, more_out), (kept_0, got_0, more_0)])
        near_near = hop(out_near, 4, size)
        gated = after(turned, out_up, next_far, out_near)
        sent_2, kept_2 = weight_grad(gated, [stacked[2]], me, size, 1, True, extra)
        got_2 = hop(sent_2, 2, size)

        mine_source = source_part([after(stacked[0], sent_2)] + stacked[1:], inward)
        other_source = swap_cores(mine_source)
        near_up, got_1, got_2 = after_all((near_up, got_1, got_2), mine_source)
        next_far = far_half(own_up, near_up)
        far_up = hop(next_far, 8, size)
        got_1, got_2 = after_all((got_1, got_2), next_far)
        next_1, next_2 = after_all((kept_1[1] + got_1[1], kept_2[1] + got_2[1]))
        more_1, more_2 = hop(next_1, 2, size), hop(next_2, 1, size)
        near_near, far_down = after_all((near_near, far_down), next_1, next_2)
        next_far = far_half(own_near, near_near)
        far_near = hop(next_far, 8, size)
        more_1, more_2 = after_all((more_1, more_2), next_far)
        own_last, out_last = combine([(kept_1, got_1, more_1), (kept_2, got_2, more_2)])
        near_last = hop(out_last, 4, size)
        input_grad = finish(mine_source, after(other_source, out_last), first_grad)
        near_last = after(near_last, input_grad)
        far_last = hop(far_half(own_last, near_last), 8, size)
        downward_grad = reduce_sum(own_down, near_down, far_down)
        upward_grad = reduce_sum(own_up, near_up, far_up)
        near_grad = reduce_sum(own_near, near_near, far_near)
        far_grad = reduce_sum(own_last, near_last, far_last)
        outward_grad = near_grad[:, :width]
        cut = 3 * LANES
        inward_grads = [near_grad[:, width:], far_grad[:, :cut], far_grad[:, cut : 2 * cut]]
        small_grad = far_grad[:, 2 * cut : 2 * cut + per_row].reshape(-1)
    else:

        def reduced(left, rights, turned=False):
            (value,) = weight_grad(left, rights, None, size, None, turned)
            return lax.psum_scatter(value, "dp", scatter_dimension=0, tiled=True)

        first_sums, first_grad, first_low, context_grad = back_first()
        downward_grad = reduced(second_low, actives)
        upward_grad = reduced(middle, hiddens)
        outward_grad = reduced(first_low, contexts)
        inward_grads = []
        for group in range(groups):
            grads, sums = attention_grads(group)
            stacked.append(grads)
            head_sums.append(sums)
            inward_grads.append(reduced(turned, [grads], True))
        mine_source = source_part(stacked, inward)
        small_grad = lax.psum_scatter(
            small_outgoing(first_sums, head_sums), "dp", scatter_dimension=0, tiled=True
        ).reshape(-1)
        input_grad = finish(mine_source, swap_cores(mine_source), first_grad)

    inward_grad = jnp.stack(
        [
            jnp.concatenate(
                [grad[:, kind * LANES : (kind + 1) * LANES] for grad in inward_grads], axis=1
            )
            for kind in range(3)
        ]
    )
    grads = (
        inward_grad,
        outward_grad.T,
        upward_grad,
        downward_grad.T,
        small_grad[:heads_size].reshape(heads_bias.shape),
        small_grad[heads_size : heads_size + hidden_size].reshape(hidden_bias.shape),
        small_grad[heads_size + hidden_size :].reshape(norm_vectors.shape),
    )

    step_value = step_count[0].astype(full)
    correct = 1.0 - jnp.power(0.5, step_value)
    plan = (step_value + 4.0) / 12.0
    rates = (D ** (-0.5), (6 * D // LEN) ** (-0.5), D ** (-0.5), FF ** (-0.5), 0.5, 0.5, 0.3)
    decays = (0.01, 0.01, 0.01, 0.01, 0.0, 0.0, 0.0)
    masters = (
        inward_weight,
        output_weight,
        up_weight,
        down_weight,
        heads_bias,
        hidden_bias,
        norm_vectors,
    )
    results = [output_rows, input_grad]
    for at in range(7):
        results.extend(
            adamw(
                masters[at],
                grads[at],
                moments[at],
                moments[7 + at],
                rates[at] * plan,
                decays[at],
                correct,
            )
        )
    return tuple(results)


def solution(mesh):
    matrices = (
        P(None, "dp", "tensor"),
        P("tensor", "dp"),
        P("dp", "tensor"),
        P("tensor", "dp"),
        P(None, "tensor", "dp"),
        P("tensor", "dp"),
        P(None, "dp"),
    )
    in_specs = (
        (P("dp", None), P("dp", None), P("dp"), P("dp"), P()) + matrices + matrices + matrices
    )
    out_specs = (P("dp", None), P("dp", None)) + tuple(
        spec for spec in matrices for _ in range(3)
    )
    return jax.shard_map(
        per_device, mesh=mesh, in_specs=in_specs, out_specs=out_specs, check_vma=False
    )
```

```python
from functools import partial
import math

import jax
import jax.numpy as jnp
from jax import lax
from jax.experimental import pallas as pl
from jax.experimental.pallas import tpu as pltpu
from jax.sharding import PartitionSpec as P

D = 768
HEAD_DIM = 64
FF = 3072
LEN = 512
LANES = 128
ROWS = 384
COST_SHARE = 1
ATTEND, BACK, EXPAND, CONTRACT, GRADS = 12, 20, 28, 40, 20

norm_epsilon = 1e-12
low = jnp.bfloat16
full = jnp.float32


def dot_nn(left, right):
    return lax.dot_general(left, right, (((1,), (0,)), ((), ())), preferred_element_type=full)


def dot_nt(left, right):
    return lax.dot_general(left, right, (((1,), (1,)), ((), ())), preferred_element_type=full)


def column_sum(values):
    return jnp.sum(values, axis=0, keepdims=True)


def row_mean(values):
    return jnp.mean(values, axis=-1, keepdims=True)


def normalize(total_in):
    centred = total_in - row_mean(total_in)
    inverse = lax.rsqrt(row_mean(centred * centred) + norm_epsilon)
    return (centred * inverse, inverse)


def norm_back(incoming, normed, inverse, gain):
    scaled = incoming * gain
    return inverse * (scaled - row_mean(scaled) - normed * row_mean(scaled * normed))


def cost(flops, moved, exps=0):
    return pl.CostEstimate(
        flops=int(flops / COST_SHARE),
        bytes_accessed=int(moved / COST_SHARE),
        transcendentals=int(exps / COST_SHARE),
    )


def params(mebibytes=12):
    return pltpu.CompilerParams(vmem_limit_bytes=mebibytes * 1024 * 1024)


def shape(dims, kind):
    return jax.ShapeDtypeStruct(dims, kind)


def main(dims, kind):
    return pltpu.HBM(dims, kind)


def streamed(*arrays):
    return [pltpu.with_memory_space_constraint(array, pltpu.HBM) for array in arrays]


def after(value, *others):
    return lax.optimization_barrier((value,) + others)[0]


def after_all(values, *others):
    return lax.optimization_barrier(tuple(values) + others)[: len(values)]


def hop(value, offset, size):
    return lax.ppermute(value, "dp", [(d, d ^ offset) for d in range(size)])


def swap_cores(value):
    return lax.ppermute(value, "tensor", [(0, 1), (1, 0)])


def split_columns(width):
    return -(-width // (2 * LANES)) * LANES


def gather_planes(shard, size):
    found = [shard] + [hop(shard, 4 * k, size) for k in range(1, size // 4)]
    return found


def gather_doubled(shard, size):
    pair = jnp.stack([shard, hop(shard, 8, size)])
    return (pair, hop(pair, 4, size))


def doubled_planes(pair, near):
    return [pair[0], near[0], pair[1], near[1]]


def split_halves(found):
    stacked = jnp.stack(found)
    cut = split_columns(stacked.shape[2])
    return lax.optimization_barrier((stacked[..., :cut], stacked[..., cut:]))


def gather_near(own, size):
    return (hop(own[0], 2, size), hop(own[1], 1, size))


def gather_pairs(own, near):
    return lax.optimization_barrier(
        (jnp.concatenate([own[0], near[0]]), jnp.concatenate([own[1], near[1]]))
    )


def gather_far(pairs, size):
    return (hop(pairs[0], 1, size), hop(pairs[1], 2, size))


def place_kernel(me_ref, pair_a, far_a, pair_b, far_b, out_ref):
    layers, rows, cut = pair_a.shape
    layers //= 2
    sources = (
        (pair_a, 0, pair_b, 0),
        (far_a, 0, pair_b, layers),
        (pair_a, layers, far_b, 0),
        (far_a, layers, far_b, layers),
    )
    for plane, (left, left_at, right, right_at) in enumerate(sources):
        for k in range(layers):
            start = pl.multiple_of((me_ref[0] ^ (4 * k + plane)) * rows, 16)
            out_ref[pl.ds(start, rows), :cut] = left[left_at + k]
            out_ref[pl.ds(start, rows), cut:] = right[right_at + k]


def place(pairs, far, me):
    flat = (pairs[0], far[0], pairs[1], far[1])
    layers, rows, cut = pairs[0].shape
    width = cut + pairs[1].shape[2]
    total = 2 * layers * rows
    return pl.pallas_call(
        place_kernel,
        out_shape=shape((total, width), low),
        grid_spec=pltpu.PrefetchScalarGridSpec(
            num_scalar_prefetch=1,
            grid=(1,),
            in_specs=[pl.BlockSpec(piece.shape, lambda i, m: (0, 0, 0)) for piece in flat],
            out_specs=pl.BlockSpec((total, width), lambda i, m: (0, 0)),
        ),
        compiler_params=params(12),
        cost_estimate=cost(0, 4 * total * width),
        name="place",
    )(me, *flat)


def turn_kernel(source_ref, out_ref):
    out_ref[...] = source_ref[...].astype(full).T.astype(low)


def turn(source):
    rows, width = source.shape
    return pl.pallas_call(
        turn_kernel,
        out_shape=shape((width, rows), low),
        grid=(rows // LEN,),
        in_specs=[pl.BlockSpec((LEN, width), lambda i: (i, 0))],
        out_specs=pl.BlockSpec((width, LEN), lambda i: (0, i)),
        compiler_params=params(16),
        cost_estimate=cost(0, 4 * rows * width),
        name="turn",
    )(source)


def combine_kernel(count, *refs):
    own_ref, out_ref = refs[-2:]
    start = 0
    for at in range(count):
        kept, got, more = refs[3 * at : 3 * at + 3]
        total = kept[0].astype(full) + got[0].astype(full) + more[...].astype(full)
        width = total.shape[2]
        for k in range(total.shape[0]):
            if k % 2:
                out_ref[k // 2, :, start : start + width] = total[k].astype(low)
            else:
                own_ref[k // 2, :, start : start + width] = total[k]
        start += width


def combine(halves):
    layers, rows = halves[0][2].shape[:2]
    width = sum(more.shape[2] for _, _, more in halves)
    flat, specs = [], []
    for kept, got, more in halves:
        part = (1,) + more.shape
        flat += [kept, got, more]
        specs += [pl.BlockSpec(part, lambda i: (0, 0, 0, 0))] * 2
        specs += [pl.BlockSpec(more.shape, lambda i: (0, 0, 0))]
    piece = (layers // 2, rows, width)
    return pl.pallas_call(
        partial(combine_kernel, len(halves)),
        out_shape=(shape(piece, full), shape(piece, low)),
        grid=(1,),
        in_specs=specs,
        out_specs=(pl.BlockSpec(piece, lambda i: (0, 0, 0)),) * 2,
        compiler_params=params(16),
        cost_estimate=cost(3 * layers * rows * width, 8 * layers * rows * width),
        name="combine",
    )(*flat)


def far_half(own, near):
    return (own[1] + near[1].astype(full)).astype(low)


def reduce_sum(own, near, far):
    return own[0] + near[0].astype(full) + far.astype(full)


def attend_kernel(length_ref, x_ref, w_ref, bias_ref, qkv_ref, weight_ref, context_ref):
    length = length_ref[pl.program_id(1)]
    mixed = dot_nn(x_ref[...], w_ref[...])
    queries = (mixed[:, :LANES] + bias_ref[0:1, :]).astype(low)
    key_rows = mixed[:, LANES : 2 * LANES].astype(low)
    values_full = mixed[:, 2 * LANES :] + bias_ref[1:2, :]
    values = values_full.astype(low)
    qkv_ref[:, :LANES] = queries
    qkv_ref[:, LANES : 2 * LANES] = key_rows
    qkv_ref[:, 2 * LANES :] = values
    values_t = values_full.T.astype(low)
    rows = queries.shape[0]
    lane = lax.broadcasted_iota(jnp.int32, (rows, LANES), 1)
    live = lax.broadcasted_iota(jnp.int32, (rows, 1), 0) < length
    scaled = queries * (1.0 / math.sqrt(HEAD_DIM))
    parts = []
    for head in range(2):
        picked = jnp.where((lane >= HEAD_DIM) == bool(head), scaled, jnp.zeros_like(scaled))
        scores = jnp.where(live, dot_nt(key_rows, picked), -jnp.inf)
        grown = jnp.exp(scores - jnp.max(scores, axis=0, keepdims=True))
        weights = (grown * (1.0 / jnp.sum(grown, axis=0, keepdims=True))).astype(low)
        weight_ref[0, head] = weights
        parts.append(dot_nn(values_t[head * HEAD_DIM : (head + 1) * HEAD_DIM, :], weights))
    context_ref[...] = jnp.concatenate(parts, axis=0).T.astype(low)


def attend(lengths, source, inward, biases, first, groups):
    rows = source.shape[0]
    count = rows // LEN
    width = 3 * LANES
    return pl.pallas_call(
        attend_kernel,
        out_shape=(
            main((rows, groups * width), low),
            main((groups * count, 2, LEN, LEN), low),
            main((rows, groups * LANES), low),
        ),
        grid_spec=pltpu.PrefetchScalarGridSpec(
            num_scalar_prefetch=1,
            grid=(groups, count),
            in_specs=[
                pl.BlockSpec((LEN, D), lambda g, s, n: (s, 0)),
                pl.BlockSpec((D, width), lambda g, s, n: (0, first + g)),
                pl.BlockSpec((2, LANES), lambda g, s, n: (0, first + g)),
            ],
            out_specs=(
                pl.BlockSpec((LEN, width), lambda g, s, n: (s, g)),
                pl.BlockSpec((1, 2, LEN, LEN), lambda g, s, n: (g * count + s, 0, 0, 0)),
                pl.BlockSpec((LEN, LANES), lambda g, s, n: (s, g)),
            ),
        ),
        compiler_params=params(ATTEND),
        cost_estimate=cost(
            groups * (2 * rows * D * width + 8 * count * LEN * LEN * LANES),
            groups * count * 2 * LEN * LEN * 2,
            groups * count * 2 * LEN * LEN,
        ),
        name="attend",
    )(lengths, *streamed(source), inward, biases)


def attend_back_kernel(qkv_ref, weight_ref, grad_ref, out_ref, sum_ref):
    @pl.when(pl.program_id(0) == 0)
    def _():
        sum_ref[...] = jnp.zeros_like(sum_ref)

    queries = qkv_ref[:, :LANES]
    key_rows = qkv_ref[:, LANES : 2 * LANES]
    values = qkv_ref[:, 2 * LANES :]
    grads = grad_ref[...]
    keys_t = key_rows.astype(full).T.astype(low)
    rows = queries.shape[0]
    lane = lax.broadcasted_iota(jnp.int32, (rows, LANES), 1)
    score_scale = 1.0 / math.sqrt(HEAD_DIM)
    query_parts, key_parts, value_parts = [], [], []
    for head in range(2):
        picked = jnp.where((lane >= HEAD_DIM) == bool(head), grads, jnp.zeros_like(grads))
        weights = weight_ref[0, head]
        wide = weights.astype(full)
        mixed = wide * dot_nt(values, picked)
        score_grads = (mixed - wide * jnp.sum(mixed, axis=0, keepdims=True)).astype(low)
        value_parts.append(dot_nn(weights, grads))
        key_parts.append(dot_nn(score_grads, queries))
        query_parts.append(
            dot_nn(keys_t[head * HEAD_DIM : (head + 1) * HEAD_DIM, :], score_grads)
        )
    first = lane < HEAD_DIM
    query_grads = (jnp.concatenate(query_parts, axis=0).T * score_scale).astype(low)
    key_grads = (jnp.where(first, key_parts[0], key_parts[1]) * score_scale).astype(low)
    value_grads = jnp.where(first, value_parts[0], value_parts[1]).astype(low)
    out_ref[:, :LANES] = query_grads
    out_ref[:, LANES : 2 * LANES] = key_grads
    out_ref[:, 2 * LANES :] = value_grads
    sum_ref[0:1, :] += column_sum(query_grads.astype(full))
    sum_ref[1:2, :] += column_sum(value_grads.astype(full))


def attend_back(qkv, weights, at, grads, group):
    rows = qkv.shape[0]
    count = rows // LEN
    width = 3 * LANES
    return pl.pallas_call(
        attend_back_kernel,
        out_shape=(main((rows, width), low), shape((2, LANES), full)),
        grid=(count,),
        in_specs=[
            pl.BlockSpec((LEN, width), lambda s: (s, at)),
            pl.BlockSpec((1, 2, LEN, LEN), lambda s: (at * count + s, 0, 0, 0)),
            pl.BlockSpec((LEN, LANES), lambda s: (s, group)),
        ],
        out_specs=(
            pl.BlockSpec((LEN, width), lambda s: (s, 0)),
            pl.BlockSpec((2, LANES), lambda s: (0, 0)),
        ),
        compiler_params=params(BACK),
        cost_estimate=cost(
            16 * count * LEN * LEN * LANES, count * 2 * LEN * LEN * 2 + 4 * rows * width
        ),
        name="attend_back",
    )(*streamed(qkv, weights, grads))


def outward_kernel(*refs):
    contexts, w_ref, out_ref = refs[:-2], refs[-2], refs[-1]
    context = jnp.concatenate([ref[...] for ref in contexts], axis=1)
    out_ref[...] = dot_nt(context, w_ref[...]).astype(low)


def row_block(width):
    return pl.BlockSpec((ROWS, width), lambda i: (i, 0))


def fixed_block(dims, at=0):
    return pl.BlockSpec(dims, lambda i: (0, at))


def outward_part(contexts, mid, outward_at):
    rows = contexts[0].shape[0]
    width = sum(context.shape[1] for context in contexts)
    return pl.pallas_call(
        outward_kernel,
        out_shape=shape((rows, D), low),
        grid=(rows // ROWS,),
        in_specs=[row_block(context.shape[1]) for context in contexts]
        + [fixed_block((D, width), outward_at // width)],
        out_specs=row_block(D),
        compiler_params=params(),
        cost_estimate=cost(2 * rows * D * width, 2 * (rows * D + rows * width + D * width)),
        name="outward",
    )(*streamed(*contexts), mid)


def gelu_parts(hidden):
    half = 0.5 + 0.5 * lax.erf(hidden * 0.7071067811865476)
    slope = half + hidden * 0.3989422804014327 * jnp.exp(-0.5 * hidden * hidden)
    return ((hidden * half).astype(low), slope.astype(low))


def expand_first_kernel(
    mine_ref, other_ref, x_ref, vector_ref, bias_ref, up_ref, down_ref,
    total_ref, active_ref, slope_ref, middle_ref, normed_ref, inverse_ref,
):
    summed = (
        mine_ref[...].astype(full)
        + other_ref[...].astype(full)
        + vector_ref[0:1, :]
        + x_ref[...].astype(full)
    )
    normed, inverse = normalize(summed)
    normed_ref[...] = normed
    inverse_ref[...] = inverse
    held = (normed * vector_ref[1:2, :] + vector_ref[2:3, :]).astype(low)
    middle_ref[...] = held
    active, slope = gelu_parts(dot_nn(held, up_ref[...]) + bias_ref[...])
    active_ref[...] = active
    slope_ref[...] = slope
    total_ref[...] = dot_nt(active, down_ref[...])


def expand_first(mine, other, source, vectors, hidden_bias, mid):
    rows, hidden = source.shape[0], hidden_bias.shape[1]
    block = hidden // 2
    return pl.pallas_call(
        expand_first_kernel,
        out_shape=(
            main((rows, D), full),
            main((rows, block), low),
            main((rows, block), low),
            main((rows, D), low),
            main((rows, D), full),
            main((rows, 1), full),
        ),
        grid=(rows // ROWS,),
        in_specs=[
            row_block(D),
            row_block(D),
            row_block(D),
            fixed_block(vectors.shape),
            fixed_block((1, block)),
            fixed_block((D, block)),
            fixed_block((D, block), 1),
        ],
        out_specs=(
            row_block(D), row_block(block), row_block(block), row_block(D), row_block(D),
            row_block(1),
        ),
        compiler_params=params(EXPAND),
        cost_estimate=cost(4 * rows * D * block, 4 * D * block + 16 * rows * D, 2 * rows * block),
        name="expand_first",
    )(mine, other, *streamed(source), vectors, hidden_bias, mid, mid)


def expand_last_kernel(
    total_ref, middle_ref, bias_ref, up_ref, down_ref, part_ref, active_ref, slope_ref
):
    active, slope = gelu_parts(dot_nn(middle_ref[...], up_ref[...]) + bias_ref[...])
    active_ref[...] = active
    slope_ref[...] = slope
    part_ref[...] = (total_ref[...] + dot_nt(active, down_ref[...])).astype(low)


def expand_last(total, middle, hidden_bias, mid):
    rows, hidden = total.shape[0], hidden_bias.shape[1]
    block = hidden // 2
    return pl.pallas_call(
        expand_last_kernel,
        out_shape=(shape((rows, D), low), main((rows, block), low), main((rows, block), low)),
        grid=(rows // ROWS,),
        in_specs=[
            row_block(D),
            row_block(D),
            fixed_block((1, block), 1),
            fixed_block((D, block)),
            fixed_block((D, block), 1),
        ],
        out_specs=(row_block(D), row_block(block), row_block(block)),
        compiler_params=params(EXPAND),
        cost_estimate=cost(4 * rows * D * block, 4 * D * block + 10 * rows * D, 2 * rows * block),
        name="expand_last",
    )(*streamed(total, middle), hidden_bias, mid, mid)


def contract_kernel(
    mine_ref, other_ref, normed_ref, cotangent_ref, scale_ref, vector_ref,
    slope_first, slope_last, up_first, down_first, up_last, down_last,
    part_ref, sum_ref, hidden_sum_ref, out_ref, wide_ref, low_ref, hidden_first, hidden_last,
):
    @pl.when(pl.program_id(0) == 0)
    def _():
        sum_ref[...] = jnp.zeros_like(sum_ref)
        hidden_sum_ref[...] = jnp.zeros_like(hidden_sum_ref)

    middle = normed_ref[...] * vector_ref[1:2, :] + vector_ref[2:3, :]
    summed = (
        mine_ref[...].astype(full) + other_ref[...].astype(full) + vector_ref[3:4, :] + middle
    )
    normed, inverse = normalize(summed)
    out_ref[...] = (normed * vector_ref[4:5, :] + vector_ref[5:6, :]).astype(low)
    incoming = cotangent_ref[...].astype(full) * scale_ref[...]
    second = norm_back(incoming, normed, inverse, vector_ref[4:5, :])
    sum_ref[0:1, :] += column_sum(second)
    sum_ref[1:2, :] += column_sum(incoming * normed)
    sum_ref[2:3, :] += column_sum(incoming)
    wide_ref[...] = second
    held = second.astype(low)
    low_ref[...] = held
    block = up_first.shape[1]
    total = None
    for at, slope_ref, up_ref, down_ref, hidden_ref in (
        (0, slope_first, up_first, down_first, hidden_first),
        (block, slope_last, up_last, down_last, hidden_last),
    ):
        hidden_grad = (dot_nn(held, down_ref[...]) * slope_ref[...].astype(full)).astype(low)
        hidden_ref[...] = hidden_grad
        hidden_sum_ref[:, at : at + block] += column_sum(hidden_grad.astype(full))
        part = dot_nt(hidden_grad, up_ref[...])
        total = part if total is None else total + part
    part_ref[...] = total.astype(low)


def contract(mine, other, normed, cotangent, scale, vectors, slopes, mids):
    rows, block = slopes[0].shape
    hidden = 2 * block
    weights = [fixed_block((D, block)), fixed_block((D, block), 1)]
    return pl.pallas_call(
        contract_kernel,
        out_shape=(
            shape((rows, D), low),
            shape((3, D), full),
            shape((1, hidden), full),
            main((rows, D), low),
            main((rows, D), full),
            main((rows, D), low),
            main((rows, block), low),
            main((rows, block), low),
        ),
        grid=(rows // ROWS,),
        in_specs=[
            row_block(D),
            row_block(D),
            row_block(D),
            row_block(D),
            row_block(1),
            fixed_block(vectors.shape),
            row_block(block),
            row_block(block),
        ]
        + weights
        + weights,
        out_specs=(
            row_block(D),
            fixed_block((3, D)),
            fixed_block((1, hidden)),
            row_block(D),
            row_block(D),
            row_block(D),
            row_block(block),
            row_block(block),
        ),
        compiler_params=params(CONTRACT),
        cost_estimate=cost(4 * rows * D * hidden, 4 * D * hidden + 4 * rows * hidden),
        name="contract",
    )(
        mine, other, *streamed(normed, cotangent), scale, vectors, *streamed(*slopes),
        mids[0], mids[0], mids[1], mids[1],
    )


def first_back_kernel(
    mine_ref, other_ref, second_ref, normed_ref, inverse_ref, vector_ref, w_ref,
    sum_ref, wide_ref, low_ref, grad_ref,
):
    @pl.when(pl.program_id(0) == 0)
    def _():
        sum_ref[...] = jnp.zeros_like(sum_ref)

    incoming = mine_ref[...].astype(full) + other_ref[...].astype(full) + second_ref[...]
    normed = normed_ref[...]
    first = norm_back(incoming, normed, inverse_ref[...], vector_ref[1:2, :])
    sum_ref[0:1, :] += column_sum(first)
    sum_ref[1:2, :] += column_sum(incoming * normed)
    sum_ref[2:3, :] += column_sum(incoming)
    wide_ref[...] = first
    held = first.astype(low)
    low_ref[...] = held
    grad_ref[...] = dot_nn(held, w_ref[...]).astype(low)


def first_back(mine, other, second, normed, inverse, vectors, mid, outward_at, width):
    rows = second.shape[0]
    return pl.pallas_call(
        first_back_kernel,
        out_shape=(
            shape((3, D), full),
            main((rows, D), full),
            main((rows, D), low),
            main((rows, width), low),
        ),
        grid=(rows // ROWS,),
        in_specs=[row_block(D)] * 4
        + [
            row_block(1),
            fixed_block(vectors.shape),
            fixed_block((D, width), outward_at // width),
        ],
        out_specs=(fixed_block((3, D)), row_block(D), row_block(D), row_block(width)),
        compiler_params=params(BACK),
        cost_estimate=cost(2 * rows * D * width, 20 * rows * D),
        name="first_back",
    )(mine, other, *streamed(second, normed, inverse), vectors, mid)


def source_kernel(*refs):
    grads, weights, out_ref = refs[:-2], refs[-2], refs[-1]
    width = 3 * LANES
    total = None
    for group, grad_ref in enumerate(grads):
        part = dot_nt(grad_ref[...], weights[:, group * width : (group + 1) * width])
        total = part if total is None else total + part
    out_ref[...] = total.astype(low)


def source_part(grads, inward):
    rows, width = grads[0].shape
    groups = len(grads)
    return pl.pallas_call(
        source_kernel,
        out_shape=shape((rows, D), low),
        grid=(rows // ROWS,),
        in_specs=[row_block(width) for _ in grads] + [fixed_block((D, groups * width))],
        out_specs=row_block(D),
        compiler_params=params(),
        cost_estimate=cost(2 * rows * D * width * groups, 2 * (rows + D) * width * groups),
        name="source",
    )(*streamed(*grads), inward)


def finish_kernel(mine_ref, other_ref, first_ref, out_ref):
    out_ref[...] = mine_ref[...].astype(full) + other_ref[...].astype(full) + first_ref[...]


def finish(mine, other, first):
    rows = first.shape[0]
    return pl.pallas_call(
        finish_kernel,
        out_shape=main((rows, D), full),
        grid=(rows // ROWS,),
        in_specs=[row_block(D)] * 3,
        out_specs=row_block(D),
        compiler_params=params(),
        cost_estimate=cost(2 * rows * D, 12 * rows * D),
        name="finish",
    )(mine, other, *streamed(first))


def weight_grad_kernel(bit, count, turned, extra, me_ref, left_ref, *refs):
    rights, refs = refs[:count], refs[count:]
    if extra:
        extra_ref, refs = refs[0], refs[1:]
    left = left_ref
    if not turned:
        left, refs = refs[-1], refs[:-1]

        def turn_block(i, carry):
            start = pl.multiple_of(i * ROWS, ROWS)
            block = left_ref[pl.ds(start, ROWS), :].astype(full)
            left[:, pl.ds(start, ROWS)] = block.T.astype(low)
            return carry

        lax.fori_loop(0, left_ref.shape[0] // ROWS, turn_block, 0, unroll=True)
    total_ref = refs[-1] if bit is not None else refs[0]
    block = 2 * ROWS if rights[0].shape[1] % D else D
    if rights[0].shape[1] % block:
        right = jnp.concatenate([piece[...] for piece in rights], axis=1)
        total_ref[...] = dot_nn(left[...], right)
    else:
        for at, piece in enumerate(rights):
            steps = piece.shape[1] // block

            def multiply(j, carry, at=at, piece=piece, steps=steps):
                start = pl.multiple_of(j * block, LANES)
                into = pl.multiple_of((at * steps + j) * block, LANES)
                total_ref[:, pl.ds(into, block)] = dot_nn(
                    left[...], piece[:, pl.ds(start, block)]
                )
                return carry

            if steps == 1:
                multiply(0, 0)
            else:
                lax.fori_loop(0, steps, multiply, 0)
    if bit is None:
        return
    layers, rows = refs[0].shape[1:3]
    width = total_ref.shape[1]
    for target, far in ((refs[0], 1), (refs[1], 0)):

        def spread(i, carry, target=target, far=far):
            other, k = i // layers, i % layers
            plane = 2 * other + far if bit == 0 else other + 2 * far
            owner = me_ref[0] ^ (4 * k + plane)
            start = pl.multiple_of(owner * rows, 8)
            target[other, k, :, :width] = total_ref[pl.ds(start, rows), :].astype(low)
            if extra:
                target[other, k, :, width:] = extra_ref[owner]
            return carry

        lax.fori_loop(0, 2 * layers, spread, 0)


def weight_grad(left, rights, me, size, bit, turned=False, extra=None):
    tokens = rights[0].shape[0]
    width = sum(right.shape[1] for right in rights)
    layers, rows = size // 4, D // size
    extras = () if extra is None else (extra,)
    if me is not None:
        total = width + (0 if extra is None else LANES)
        outs = (shape((2, layers, rows, total), low),) * 2
        scratch = [pltpu.VMEM((D, width), full)]
    else:
        outs = (shape((D, width), full),)
        scratch = []
        me = jnp.zeros((1,), jnp.int32)
        bit = None
    if not turned:
        scratch.append(pltpu.VMEM((D, tokens), low))

    def whole(array):
        return pl.BlockSpec(array.shape, lambda j, m: (0,) * len(array.shape))

    flat = (left, *rights, *extras)
    return pl.pallas_call(
        partial(weight_grad_kernel, bit, len(rights), turned, extra is not None),
        out_shape=outs,
        grid_spec=pltpu.PrefetchScalarGridSpec(
            num_scalar_prefetch=1,
            grid=(1,),
            in_specs=[whole(array) for array in flat],
            out_specs=tuple(whole(array) for array in outs),
            scratch_shapes=scratch,
        ),
        compiler_params=params(GRADS),
        cost_estimate=cost(2 * tokens * D * width, 2 * tokens * (D + width)),
        name="weight_grad",
    )(me, *flat)


def adamw(master, gradient, first_moment, second_moment, step_rate, decay_rate, correct):
    first_new = 0.5 * first_moment + 0.5 * gradient
    second_new = 0.5 * second_moment + 0.5 * gradient * gradient
    moved = first_new / correct / (jnp.sqrt(second_new / correct) + 1e-08)
    return (master - step_rate * (moved + decay_rate * master), first_new, second_new)


def per_device(
    activations,
    cotangent,
    token_weight,
    lengths,
    step_count,
    inward_weight,
    output_weight,
    up_weight,
    down_weight,
    heads_bias,
    hidden_bias,
    norm_vectors,
    *moments,
):
    size = lax.axis_size("dp")
    rows, width = inward_weight.shape[1], inward_weight.shape[2]
    hidden_width = up_weight.shape[1]
    groups = width // LANES
    tokens = activations.shape[0]
    count = tokens // LEN
    fast = size == 16 and rows % 16 == 0
    me = lax.axis_index("dp").astype(jnp.int32).reshape(1) if fast else None

    small = jnp.concatenate(
        [heads_bias.reshape(-1), hidden_bias.reshape(-1), norm_vectors.reshape(-1)]
    )
    per_row = small.shape[0] // rows
    small_block = jnp.pad(small.reshape(rows, per_row), ((0, 0), (0, LANES - per_row)))
    inward_shard = jnp.concatenate(
        [
            inward_weight.reshape(3, rows, groups, LANES)
            .transpose(1, 2, 0, 3)
            .reshape(rows, 3 * width),
            small_block,
        ],
        axis=1,
    ).astype(low)
    block = hidden_width // 2
    outward_at = 2 * block
    up_shard, down_shard = up_weight.astype(low), down_weight.T.astype(low)
    first_shard = jnp.concatenate(
        [up_shard[:, :block], down_shard[:, :block], output_weight.T.astype(low)], axis=1
    )
    last_shard = jnp.concatenate([up_shard[:, block:], down_shard[:, block:]], axis=1)

    if fast:
        found = gather_planes(inward_shard, size)
        found_first = gather_doubled(after(first_shard, *found[1:]), size)
        found_last = gather_doubled(after(last_shard, found_first[1]), size)
        turned = turn(activations)
        found[0] = after(found[0], turned)
        own = split_halves(found)
        pairs = gather_pairs(own, gather_near(own, size))
        far = gather_far(pairs, size)
        own_first = split_halves(doubled_planes(*found_first))
        far = after_all(far, *own_first)
        own_first = after_all(own_first, *far)
        inward = place(pairs, far, me)
        near_first = gather_near(own_first, size)
        inward = after(inward, *own_first)
    else:
        inward, mid_first, mid_last = [
            lax.all_gather(shard, "dp", axis=0, tiled=True)
            for shard in (inward_shard, first_shard, last_shard)
        ]
        turned = turn(activations)

    smalls = inward[:, 3 * width : 3 * width + per_row].astype(full).reshape(size, -1)
    heads_size, hidden_size = heads_bias.size, hidden_bias.size
    head_biases = (
        smalls[:, :heads_size].reshape(size, 2, -1).transpose(1, 2, 0).reshape(2, width)
    )
    hidden_biases = smalls[:, heads_size : heads_size + hidden_size].T.reshape(1, hidden_width)
    vectors = (
        smalls[:, heads_size + hidden_size :].reshape(size, 6, rows).transpose(1, 0, 2)
    ).reshape(6, D)

    live = lax.broadcasted_iota(jnp.int32, (count, LEN), 1) < lengths[:, None]
    scale = (token_weight.reshape(count, LEN) * live.astype(jnp.int32)).astype(full)
    scale = scale.reshape(tokens, 1)

    first_pair = attend(lengths, activations, inward, head_biases, 0, 1)
    if fast:
        near_first = after_all(near_first, first_pair[2])
        pairs_first = gather_pairs(own_first, near_first)
        far_first = gather_far(pairs_first, size)
        own_last = split_halves(doubled_planes(*after_all(found_last, *pairs_first)))
        near_last = gather_near(own_last, size)
        gated = after(activations, *pairs_first, *own_last, vectors, hidden_biases)
    else:
        gated = after(activations, first_pair[2])
    later_pairs = attend(lengths, gated, inward, head_biases, 1, groups - 1)
    contexts = [first_pair[2], later_pairs[2]]
    if fast:
        pairs_last = gather_pairs(own_last, after_all(near_last, later_pairs[2]))
        far_last = gather_far(pairs_last, size)
        mid_first = place(pairs_first, after_all(far_first, *pairs_last), me)

    mine = outward_part(contexts, mid_first, outward_at)
    total, active_first, slope_first, middle, normed, inverse = expand_first(
        mine, swap_cores(mine), activations, vectors, hidden_biases, mid_first
    )
    if fast:
        mid_last = place(pairs_last, after_all(far_last, total), me)
    mine_down, active_last, slope_last = expand_last(total, middle, hidden_biases, mid_last)
    (
        mine_middle, second_sums, hidden_sums, output_rows,
        second_grad, second_low, hidden_first, hidden_last,
    ) = contract(
        mine_down, swap_cores(mine_down), normed, cotangent, scale, vectors,
        (slope_first, slope_last), (mid_first, mid_last),
    )
    other_middle = swap_cores(mine_middle)
    actives, hiddens = (active_first, active_last), (hidden_first, hidden_last)

    def back_first(*gates):
        return first_back(
            after(mine_middle, *gates), other_middle, second_grad, normed, inverse, vectors,
            mid_first, outward_at, width,
        )

    def attention_grads(group, *gates):
        at = max(group - 1, 0)
        qkv, weights, _ = later_pairs if group else first_pair
        return attend_back(after(qkv, *gates), weights, at, context_grad, group)

    def heads_outgoing(sums):
        return jnp.concatenate(sums, axis=1).reshape(2, -1, size).transpose(2, 0, 1)

    def small_outgoing(first_sums, head_sums):
        norm_grad = jnp.concatenate([first_sums, second_sums])
        return jnp.concatenate(
            [
                heads_outgoing(head_sums).reshape(size, -1),
                hidden_sums.reshape(-1, size).T,
                norm_grad.reshape(6, size, rows).transpose(1, 0, 2).reshape(size, -1),
            ],
            axis=1,
        )

    stacked, head_sums = [], []
    if fast:
        sent_down, kept_down = weight_grad(second_low, actives, me, size, 0)
        got_down = hop(sent_down, 1, size)
        sent_up, kept_up = weight_grad(after(middle, sent_down), hiddens, me, size, 1)
        got_up = hop(sent_up, 2, size)
        first_sums, first_grad, first_low, context_grad = back_first(sent_up)

        sent_out, kept_out = weight_grad(first_low, contexts, me, size, 0)
        got_out = hop(sent_out, 1, size)

        def attention(group, *gates):
            grads, sums = attention_grads(group, *gates)
            stacked.append(grads)
            head_sums.append(sums)

        attention(0, sent_out)
        got_down = after(got_down, stacked[0])
        next_down = kept_down[1] + got_down[1]
        more_down = hop(next_down, 2, size)
        gated = after(turned, next_down)
        sent_0, kept_0 = weight_grad(gated, [stacked[0]], me, size, 1, True)
        got_0 = hop(sent_0, 2, size)
        got_up = after(got_up, sent_0)
        next_up = kept_up[1] + got_up[1]
        more_up = hop(next_up, 1, size)

        attention(1, next_up)
        got_out, got_0, more_down = after_all((got_out, got_0, more_down), stacked[1])
        next_out, next_0 = after_all((kept_out[1] + got_out[1], kept_0[1] + got_0[1]))
        more_out, more_0 = hop(next_out, 2, size), hop(next_0, 1, size)
        own_down, out_down = combine([(kept_down, got_down, more_down)])
        near_down = hop(out_down, 4, size)
        gated = after(turned, next_out, next_0, out_down)
        sent_1, kept_1 = weight_grad(gated, [stacked[1]], me, size, 0, True)
        got_1 = hop(sent_1, 1, size)

        attention(2, sent_1)
        extra = small_outgoing(first_sums, head_sums).reshape(size, rows, per_row)
        extra = jnp.pad(extra, ((0, 0), (0, 0), (0, LANES - per_row))).astype(low)
        more_up, near_down, more_out, more_0 = after_all(
            (more_up, near_down, more_out, more_0), stacked[2]
        )
        own_up, out_up = combine([(kept_up, got_up, more_up)])
        near_up = hop(out_up, 4, size)
        next_far = far_half(own_down, near_down)
        far_down = hop(next_far, 8, size)
        own_near, out_near = combine([(kept_out, got_out, more_out), (kept_0, got_0, more_0)])
        near_near = hop(out_near, 4, size)
        gated = after(turned, out_up, next_far, out_near)
        sent_2, kept_2 = weight_grad(gated, [stacked[2]], me, size, 1, True, extra)
        got_2 = hop(sent_2, 2, size)

        mine_source = source_part([after(stacked[0], sent_2)] + stacked[1:], inward)
        other_source = swap_cores(mine_source)
        near_up, got_1, got_2 = after_all((near_up, got_1, got_2), mine_source)
        next_far = far_half(own_up, near_up)
        far_up = hop(next_far, 8, size)
        got_1, got_2 = after_all((got_1, got_2), next_far)
        next_1, next_2 = after_all((kept_1[1] + got_1[1], kept_2[1] + got_2[1]))
        more_1, more_2 = hop(next_1, 2, size), hop(next_2, 1, size)
        near_near, far_down = after_all((near_near, far_down), next_1, next_2)
        next_far = far_half(own_near, near_near)
        far_near = hop(next_far, 8, size)
        more_1, more_2 = after_all((more_1, more_2), next_far)
        own_last, out_last = combine([(kept_1, got_1, more_1), (kept_2, got_2, more_2)])
        near_last = hop(out_last, 4, size)
        input_grad = finish(mine_source, after(other_source, out_last), first_grad)
        near_last = after(near_last, input_grad)
        far_last = hop(far_half(own_last, near_last), 8, size)
        downward_grad = reduce_sum(own_down, near_down, far_down)
        upward_grad = reduce_sum(own_up, near_up, far_up)
        near_grad = reduce_sum(own_near, near_near, far_near)
        far_grad = reduce_sum(own_last, near_last, far_last)
        outward_grad = near_grad[:, :width]
        cut = 3 * LANES
        inward_grads = [near_grad[:, width:], far_grad[:, :cut], far_grad[:, cut : 2 * cut]]
        small_grad = far_grad[:, 2 * cut : 2 * cut + per_row].reshape(-1)
    else:

        def reduced(left, rights, turned=False):
            (value,) = weight_grad(left, rights, None, size, None, turned)
            return lax.psum_scatter(value, "dp", scatter_dimension=0, tiled=True)

        first_sums, first_grad, first_low, context_grad = back_first()
        downward_grad = reduced(second_low, actives)
        upward_grad = reduced(middle, hiddens)
        outward_grad = reduced(first_low, contexts)
        inward_grads = []
        for group in range(groups):
            grads, sums = attention_grads(group)
            stacked.append(grads)
            head_sums.append(sums)
            inward_grads.append(reduced(turned, [grads], True))
        mine_source = source_part(stacked, inward)
        small_grad = lax.psum_scatter(
            small_outgoing(first_sums, head_sums), "dp", scatter_dimension=0, tiled=True
        ).reshape(-1)
        input_grad = finish(mine_source, swap_cores(mine_source), first_grad)

    inward_grad = jnp.stack(
        [
            jnp.concatenate(
                [grad[:, kind * LANES : (kind + 1) * LANES] for grad in inward_grads], axis=1
            )
            for kind in range(3)
        ]
    )
    grads = (
        inward_grad,
        outward_grad.T,
        upward_grad,
        downward_grad.T,
        small_grad[:heads_size].reshape(heads_bias.shape),
        small_grad[heads_size : heads_size + hidden_size].reshape(hidden_bias.shape),
        small_grad[heads_size + hidden_size :].reshape(norm_vectors.shape),
    )

    step_value = step_count[0].astype(full)
    correct = 1.0 - jnp.power(0.5, step_value)
    plan = (step_value + 4.0) / 12.0
    rates = (D ** (-0.5), (6 * D // LEN) ** (-0.5), D ** (-0.5), FF ** (-0.5), 0.5, 0.5, 0.3)
    decays = (0.01, 0.01, 0.01, 0.01, 0.0, 0.0, 0.0)
    masters = (
        inward_weight,
        output_weight,
        up_weight,
        down_weight,
        heads_bias,
        hidden_bias,
        norm_vectors,
    )
    results = [output_rows, input_grad]
    for at in range(7):
        results.extend(
            adamw(
                masters[at],
                grads[at],
                moments[at],
                moments[7 + at],
                rates[at] * plan,
                decays[at],
                correct,
            )
        )
    return tuple(results)


def solution(mesh):
    matrices = (
        P(None, "dp", "tensor"),
        P("tensor", "dp"),
        P("dp", "tensor"),
        P("tensor", "dp"),
        P(None, "tensor", "dp"),
        P("tensor", "dp"),
        P(None, "dp"),
    )
    in_specs = (
        (P("dp", None), P("dp", None), P("dp"), P("dp"), P()) + matrices + matrices + matrices
    )
    out_specs = (P("dp", None), P("dp", None)) + tuple(
        spec for spec in matrices for _ in range(3)
    )
    return jax.shard_map(
        per_device, mesh=mesh, in_specs=in_specs, out_specs=out_specs, check_vma=False
    )
```

```python
from functools import partial
import math

import jax
import jax.numpy as jnp
from jax import lax
from jax.experimental import pallas as pl
from jax.experimental.pallas import tpu as pltpu
from jax.sharding import PartitionSpec as P

D = 768
HEAD_DIM = 64
FF = 3072
LEN = 512
LANES = 128
ROWS = 384
COST_SHARE = 1
ATTEND, BACK, EXPAND, CONTRACT, GRADS = 12, 16, 22, 26, 16

norm_epsilon = 1e-12
low = jnp.bfloat16
full = jnp.float32


def dot_nn(left, right):
    return lax.dot_general(left, right, (((1,), (0,)), ((), ())), preferred_element_type=full)


def dot_nt(left, right):
    return lax.dot_general(left, right, (((1,), (1,)), ((), ())), preferred_element_type=full)


def column_sum(values):
    return jnp.sum(values, axis=0, keepdims=True)


def row_mean(values):
    return jnp.mean(values, axis=-1, keepdims=True)


def normalize(total_in):
    centred = total_in - row_mean(total_in)
    inverse = lax.rsqrt(row_mean(centred * centred) + norm_epsilon)
    return (centred * inverse, inverse)


def norm_back(incoming, normed, inverse, gain):
    scaled = incoming * gain
    return inverse * (scaled - row_mean(scaled) - normed * row_mean(scaled * normed))


def cost(flops, moved, exps=0):
    return pl.CostEstimate(
        flops=int(flops / COST_SHARE),
        bytes_accessed=int(moved / COST_SHARE),
        transcendentals=int(exps / COST_SHARE),
    )


def params(mebibytes=12):
    return pltpu.CompilerParams(vmem_limit_bytes=mebibytes * 1024 * 1024)


def shape(dims, kind):
    return jax.ShapeDtypeStruct(dims, kind)


def main(dims, kind):
    return pltpu.HBM(dims, kind)


def streamed(*arrays):
    return [pltpu.with_memory_space_constraint(array, pltpu.HBM) for array in arrays]


def after(value, *others):
    return lax.optimization_barrier((value,) + others)[0]


def after_all(values, *others):
    return lax.optimization_barrier(tuple(values) + others)[: len(values)]


def hop(value, offset, size):
    return lax.ppermute(value, "dp", [(d, d ^ offset) for d in range(size)])


def swap_cores(value):
    return lax.ppermute(value, "tensor", [(0, 1), (1, 0)])


def split_columns(width):
    return -(-width // (2 * LANES)) * LANES


def gather_planes(shard, size):
    found = [shard] + [hop(shard, 4 * k, size) for k in range(1, size // 4)]
    return found


def gather_doubled(shard, size):
    pair = jnp.stack([shard, hop(shard, 8, size)])
    return (pair, hop(pair, 4, size))


def doubled_planes(pair, near):
    return [pair[0], near[0], pair[1], near[1]]


def split_halves(found):
    stacked = jnp.stack(found)
    cut = split_columns(stacked.shape[2])
    return lax.optimization_barrier((stacked[..., :cut], stacked[..., cut:]))


def gather_near(own, size):
    return (hop(own[0], 2, size), hop(own[1], 1, size))


def gather_pairs(own, near):
    return lax.optimization_barrier(
        (jnp.concatenate([own[0], near[0]]), jnp.concatenate([own[1], near[1]]))
    )


def gather_far(pairs, size):
    return (hop(pairs[0], 1, size), hop(pairs[1], 2, size))


def place_kernel(me_ref, pair_a, far_a, pair_b, far_b, out_ref):
    layers, rows, cut = pair_a.shape
    layers //= 2
    sources = (
        (pair_a, 0, pair_b, 0),
        (far_a, 0, pair_b, layers),
        (pair_a, layers, far_b, 0),
        (far_a, layers, far_b, layers),
    )
    for plane, (left, left_at, right, right_at) in enumerate(sources):
        for k in range(layers):
            start = pl.multiple_of((me_ref[0] ^ (4 * k + plane)) * rows, 16)
            out_ref[pl.ds(start, rows), :cut] = left[left_at + k]
            out_ref[pl.ds(start, rows), cut:] = right[right_at + k]


def place(pairs, far, me):
    flat = (pairs[0], far[0], pairs[1], far[1])
    layers, rows, cut = pairs[0].shape
    width = cut + pairs[1].shape[2]
    total = 2 * layers * rows
    return pl.pallas_call(
        place_kernel,
        out_shape=shape((total, width), low),
        grid_spec=pltpu.PrefetchScalarGridSpec(
            num_scalar_prefetch=1,
            grid=(1,),
            in_specs=[pl.BlockSpec(piece.shape, lambda i, m: (0, 0, 0)) for piece in flat],
            out_specs=pl.BlockSpec((total, width), lambda i, m: (0, 0)),
        ),
        compiler_params=params(12),
        cost_estimate=cost(0, 4 * total * width),
        name="place",
    )(me, *flat)


def turn_kernel(source_ref, out_ref):
    out_ref[...] = source_ref[...].astype(full).T.astype(low)


def turn(source):
    rows, width = source.shape
    return pl.pallas_call(
        turn_kernel,
        out_shape=shape((width, rows), low),
        grid=(rows // LEN,),
        in_specs=[pl.BlockSpec((LEN, width), lambda i: (i, 0))],
        out_specs=pl.BlockSpec((width, LEN), lambda i: (0, i)),
        compiler_params=params(16),
        cost_estimate=cost(0, 4 * rows * width),
        name="turn",
    )(source)


def combine_kernel(count, *refs):
    own_ref, out_ref = refs[-2:]
    start = 0
    for at in range(count):
        kept, got, more = refs[3 * at : 3 * at + 3]
        total = kept[0].astype(full) + got[0].astype(full) + more[...].astype(full)
        width = total.shape[2]
        for k in range(total.shape[0]):
            if k % 2:
                out_ref[k // 2, :, start : start + width] = total[k].astype(low)
            else:
                own_ref[k // 2, :, start : start + width] = total[k]
        start += width


def combine(halves):
    layers, rows = halves[0][2].shape[:2]
    width = sum(more.shape[2] for _, _, more in halves)
    flat, specs = [], []
    for kept, got, more in halves:
        part = (1,) + more.shape
        flat += [kept, got, more]
        specs += [pl.BlockSpec(part, lambda i: (0, 0, 0, 0))] * 2
        specs += [pl.BlockSpec(more.shape, lambda i: (0, 0, 0))]
    piece = (layers // 2, rows, width)
    return pl.pallas_call(
        partial(combine_kernel, len(halves)),
        out_shape=(shape(piece, full), shape(piece, low)),
        grid=(1,),
        in_specs=specs,
        out_specs=(pl.BlockSpec(piece, lambda i: (0, 0, 0)),) * 2,
        compiler_params=params(16),
        cost_estimate=cost(3 * layers * rows * width, 8 * layers * rows * width),
        name="combine",
    )(*flat)


def far_half(own, near):
    return (own[1] + near[1].astype(full)).astype(low)


def reduce_sum(own, near, far):
    return own[0] + near[0].astype(full) + far.astype(full)


def attend_kernel(length_ref, x_ref, w_ref, bias_ref, qkv_ref, weight_ref, context_ref):
    length = length_ref[pl.program_id(1)]
    mixed = dot_nn(x_ref[...], w_ref[...])
    queries = (mixed[:, :LANES] + bias_ref[0:1, :]).astype(low)
    key_rows = mixed[:, LANES : 2 * LANES].astype(low)
    values_full = mixed[:, 2 * LANES :] + bias_ref[1:2, :]
    values = values_full.astype(low)
    qkv_ref[:, :LANES] = queries
    qkv_ref[:, LANES : 2 * LANES] = key_rows
    qkv_ref[:, 2 * LANES :] = values
    values_t = values_full.T.astype(low)
    rows = queries.shape[0]
    lane = lax.broadcasted_iota(jnp.int32, (rows, LANES), 1)
    live = lax.broadcasted_iota(jnp.int32, (rows, 1), 0) < length
    scaled = queries * (1.0 / math.sqrt(HEAD_DIM))
    parts = []
    for head in range(2):
        picked = jnp.where((lane >= HEAD_DIM) == bool(head), scaled, jnp.zeros_like(scaled))
        scores = jnp.where(live, dot_nt(key_rows, picked), -jnp.inf)
        grown = jnp.exp(scores - jnp.max(scores, axis=0, keepdims=True))
        weights = (grown * (1.0 / jnp.sum(grown, axis=0, keepdims=True))).astype(low)
        weight_ref[0, head] = weights
        parts.append(dot_nn(values_t[head * HEAD_DIM : (head + 1) * HEAD_DIM, :], weights))
    context_ref[...] = jnp.concatenate(parts, axis=0).T.astype(low)


def attend(lengths, source, inward, biases, first, groups):
    rows = source.shape[0]
    count = rows // LEN
    width = 3 * LANES
    return pl.pallas_call(
        attend_kernel,
        out_shape=(
            main((rows, groups * width), low),
            main((groups * count, 2, LEN, LEN), low),
            main((rows, groups * LANES), low),
        ),
        grid_spec=pltpu.PrefetchScalarGridSpec(
            num_scalar_prefetch=1,
            grid=(groups, count),
            in_specs=[
                pl.BlockSpec((LEN, D), lambda g, s, n: (s, 0)),
                pl.BlockSpec((D, width), lambda g, s, n: (0, first + g)),
                pl.BlockSpec((2, LANES), lambda g, s, n: (0, first + g)),
            ],
            out_specs=(
                pl.BlockSpec((LEN, width), lambda g, s, n: (s, g)),
                pl.BlockSpec((1, 2, LEN, LEN), lambda g, s, n: (g * count + s, 0, 0, 0)),
                pl.BlockSpec((LEN, LANES), lambda g, s, n: (s, g)),
            ),
        ),
        compiler_params=params(ATTEND),
        cost_estimate=cost(
            groups * (2 * rows * D * width + 8 * count * LEN * LEN * LANES),
            groups * count * 2 * LEN * LEN * 2,
            groups * count * 2 * LEN * LEN,
        ),
        name="attend",
    )(lengths, *streamed(source), inward, biases)


def attend_back_kernel(qkv_ref, weight_ref, grad_ref, out_ref, sum_ref):
    @pl.when(pl.program_id(0) == 0)
    def _():
        sum_ref[...] = jnp.zeros_like(sum_ref)

    queries = qkv_ref[:, :LANES]
    key_rows = qkv_ref[:, LANES : 2 * LANES]
    values = qkv_ref[:, 2 * LANES :]
    grads = grad_ref[...]
    keys_t = key_rows.astype(full).T.astype(low)
    rows = queries.shape[0]
    lane = lax.broadcasted_iota(jnp.int32, (rows, LANES), 1)
    score_scale = 1.0 / math.sqrt(HEAD_DIM)
    query_parts, key_parts, value_parts = [], [], []
    for head in range(2):
        picked = jnp.where((lane >= HEAD_DIM) == bool(head), grads, jnp.zeros_like(grads))
        weights = weight_ref[0, head]
        wide = weights.astype(full)
        mixed = wide * dot_nt(values, picked)
        score_grads = (mixed - wide * jnp.sum(mixed, axis=0, keepdims=True)).astype(low)
        value_parts.append(dot_nn(weights, grads))
        key_parts.append(dot_nn(score_grads, queries))
        query_parts.append(
            dot_nn(keys_t[head * HEAD_DIM : (head + 1) * HEAD_DIM, :], score_grads)
        )
    first = lane < HEAD_DIM
    query_grads = (jnp.concatenate(query_parts, axis=0).T * score_scale).astype(low)
    key_grads = (jnp.where(first, key_parts[0], key_parts[1]) * score_scale).astype(low)
    value_grads = jnp.where(first, value_parts[0], value_parts[1]).astype(low)
    out_ref[:, :LANES] = query_grads
    out_ref[:, LANES : 2 * LANES] = key_grads
    out_ref[:, 2 * LANES :] = value_grads
    sum_ref[0:1, :] += column_sum(query_grads.astype(full))
    sum_ref[1:2, :] += column_sum(value_grads.astype(full))


def attend_back(qkv, weights, at, grads, group):
    rows = qkv.shape[0]
    count = rows // LEN
    width = 3 * LANES
    return pl.pallas_call(
        attend_back_kernel,
        out_shape=(main((rows, width), low), shape((2, LANES), full)),
        grid=(count,),
        in_specs=[
            pl.BlockSpec((LEN, width), lambda s: (s, at)),
            pl.BlockSpec((1, 2, LEN, LEN), lambda s: (at * count + s, 0, 0, 0)),
            pl.BlockSpec((LEN, LANES), lambda s: (s, group)),
        ],
        out_specs=(
            pl.BlockSpec((LEN, width), lambda s: (s, 0)),
            pl.BlockSpec((2, LANES), lambda s: (0, 0)),
        ),
        compiler_params=params(BACK),
        cost_estimate=cost(
            16 * count * LEN * LEN * LANES, count * 2 * LEN * LEN * 2 + 4 * rows * width
        ),
        name="attend_back",
    )(*streamed(qkv, weights, grads))


def outward_kernel(*refs):
    contexts, w_ref, out_ref = refs[:-2], refs[-2], refs[-1]
    context = jnp.concatenate([ref[...] for ref in contexts], axis=1)
    out_ref[...] = dot_nt(context, w_ref[...]).astype(low)


def row_block(width):
    return pl.BlockSpec((ROWS, width), lambda i: (i, 0))


def fixed_block(dims, at=0):
    return pl.BlockSpec(dims, lambda i: (0, at))


def outward_part(contexts, mid, outward_at):
    rows = contexts[0].shape[0]
    width = sum(context.shape[1] for context in contexts)
    return pl.pallas_call(
        outward_kernel,
        out_shape=shape((rows, D), low),
        grid=(rows // ROWS,),
        in_specs=[row_block(context.shape[1]) for context in contexts]
        + [fixed_block((D, width), outward_at // width)],
        out_specs=row_block(D),
        compiler_params=params(),
        cost_estimate=cost(2 * rows * D * width, 2 * (rows * D + rows * width + D * width)),
        name="outward",
    )(*streamed(*contexts), mid)


def gelu_parts(hidden):
    half = 0.5 + 0.5 * lax.erf(hidden * 0.7071067811865476)
    slope = half + hidden * 0.3989422804014327 * jnp.exp(-0.5 * hidden * hidden)
    return ((hidden * half).astype(low), slope.astype(low))


def expand_first_kernel(
    mine_ref, other_ref, x_ref, vector_ref, bias_ref, up_ref, down_ref,
    total_ref, active_ref, slope_ref, middle_ref, normed_ref, inverse_ref,
):
    summed = (
        mine_ref[...].astype(full)
        + other_ref[...].astype(full)
        + vector_ref[0:1, :]
        + x_ref[...].astype(full)
    )
    normed, inverse = normalize(summed)
    normed_ref[...] = normed
    inverse_ref[...] = inverse
    held = (normed * vector_ref[1:2, :] + vector_ref[2:3, :]).astype(low)
    middle_ref[...] = held
    active, slope = gelu_parts(dot_nn(held, up_ref[...]) + bias_ref[...])
    active_ref[...] = active
    slope_ref[...] = slope
    total_ref[...] = dot_nt(active, down_ref[...])


def expand_first(mine, other, source, vectors, hidden_bias, mid):
    rows, hidden = source.shape[0], hidden_bias.shape[1]
    block = hidden // 2
    return pl.pallas_call(
        expand_first_kernel,
        out_shape=(
            main((rows, D), full),
            main((rows, block), low),
            main((rows, block), low),
            main((rows, D), low),
            main((rows, D), full),
            main((rows, 1), full),
        ),
        grid=(rows // ROWS,),
        in_specs=[
            row_block(D),
            row_block(D),
            row_block(D),
            fixed_block(vectors.shape),
            fixed_block((1, block)),
            fixed_block((D, block)),
            fixed_block((D, block), 1),
        ],
        out_specs=(
            row_block(D), row_block(block), row_block(block), row_block(D), row_block(D),
            row_block(1),
        ),
        compiler_params=params(EXPAND),
        cost_estimate=cost(4 * rows * D * block, 4 * D * block + 16 * rows * D, 2 * rows * block),
        name="expand_first",
    )(mine, other, *streamed(source), vectors, hidden_bias, mid, mid)


def expand_last_kernel(
    total_ref, middle_ref, bias_ref, up_ref, down_ref, part_ref, active_ref, slope_ref
):
    active, slope = gelu_parts(dot_nn(middle_ref[...], up_ref[...]) + bias_ref[...])
    active_ref[...] = active
    slope_ref[...] = slope
    part_ref[...] = (total_ref[...] + dot_nt(active, down_ref[...])).astype(low)


def expand_last(total, middle, hidden_bias, mid):
    rows, hidden = total.shape[0], hidden_bias.shape[1]
    block = hidden // 2
    return pl.pallas_call(
        expand_last_kernel,
        out_shape=(shape((rows, D), low), main((rows, block), low), main((rows, block), low)),
        grid=(rows // ROWS,),
        in_specs=[
            row_block(D),
            row_block(D),
            fixed_block((1, block), 1),
            fixed_block((D, block)),
            fixed_block((D, block), 1),
        ],
        out_specs=(row_block(D), row_block(block), row_block(block)),
        compiler_params=params(EXPAND),
        cost_estimate=cost(4 * rows * D * block, 4 * D * block + 10 * rows * D, 2 * rows * block),
        name="expand_last",
    )(*streamed(total, middle), hidden_bias, mid, mid)


def contract_kernel(
    mine_ref, other_ref, normed_ref, cotangent_ref, scale_ref, vector_ref,
    slope_first, slope_last, up_first, down_first, up_last, down_last,
    part_ref, sum_ref, hidden_sum_ref, out_ref, wide_ref, low_ref, hidden_first, hidden_last,
):
    @pl.when(pl.program_id(0) == 0)
    def _():
        sum_ref[...] = jnp.zeros_like(sum_ref)
        hidden_sum_ref[...] = jnp.zeros_like(hidden_sum_ref)

    middle = normed_ref[...] * vector_ref[1:2, :] + vector_ref[2:3, :]
    summed = (
        mine_ref[...].astype(full) + other_ref[...].astype(full) + vector_ref[3:4, :] + middle
    )
    normed, inverse = normalize(summed)
    out_ref[...] = (normed * vector_ref[4:5, :] + vector_ref[5:6, :]).astype(low)
    incoming = cotangent_ref[...].astype(full) * scale_ref[...]
    second = norm_back(incoming, normed, inverse, vector_ref[4:5, :])
    sum_ref[0:1, :] += column_sum(second)
    sum_ref[1:2, :] += column_sum(incoming * normed)
    sum_ref[2:3, :] += column_sum(incoming)
    wide_ref[...] = second
    held = second.astype(low)
    low_ref[...] = held
    block = up_first.shape[1]
    total = None
    for at, slope_ref, up_ref, down_ref, hidden_ref in (
        (0, slope_first, up_first, down_first, hidden_first),
        (block, slope_last, up_last, down_last, hidden_last),
    ):
        hidden_grad = (dot_nn(held, down_ref[...]) * slope_ref[...].astype(full)).astype(low)
        hidden_ref[...] = hidden_grad
        hidden_sum_ref[:, at : at + block] += column_sum(hidden_grad.astype(full))
        part = dot_nt(hidden_grad, up_ref[...])
        total = part if total is None else total + part
    part_ref[...] = total.astype(low)


def contract(mine, other, normed, cotangent, scale, vectors, slopes, mids):
    rows, block = slopes[0].shape
    hidden = 2 * block
    weights = [fixed_block((D, block)), fixed_block((D, block), 1)]
    return pl.pallas_call(
        contract_kernel,
        out_shape=(
            shape((rows, D), low),
            shape((3, D), full),
            shape((1, hidden), full),
            main((rows, D), low),
            main((rows, D), full),
            main((rows, D), low),
            main((rows, block), low),
            main((rows, block), low),
        ),
        grid=(rows // ROWS,),
        in_specs=[
            row_block(D),
            row_block(D),
            row_block(D),
            row_block(D),
            row_block(1),
            fixed_block(vectors.shape),
            row_block(block),
            row_block(block),
        ]
        + weights
        + weights,
        out_specs=(
            row_block(D),
            fixed_block((3, D)),
            fixed_block((1, hidden)),
            row_block(D),
            row_block(D),
            row_block(D),
            row_block(block),
            row_block(block),
        ),
        compiler_params=params(CONTRACT),
        cost_estimate=cost(4 * rows * D * hidden, 4 * D * hidden + 4 * rows * hidden),
        name="contract",
    )(
        mine, other, *streamed(normed, cotangent), scale, vectors, *streamed(*slopes),
        mids[0], mids[0], mids[1], mids[1],
    )


def first_back_kernel(
    mine_ref, other_ref, second_ref, normed_ref, inverse_ref, vector_ref, w_ref,
    sum_ref, wide_ref, low_ref, grad_ref,
):
    @pl.when(pl.program_id(0) == 0)
    def _():
        sum_ref[...] = jnp.zeros_like(sum_ref)

    incoming = mine_ref[...].astype(full) + other_ref[...].astype(full) + second_ref[...]
    normed = normed_ref[...]
    first = norm_back(incoming, normed, inverse_ref[...], vector_ref[1:2, :])
    sum_ref[0:1, :] += column_sum(first)
    sum_ref[1:2, :] += column_sum(incoming * normed)
    sum_ref[2:3, :] += column_sum(incoming)
    wide_ref[...] = first
    held = first.astype(low)
    low_ref[...] = held
    grad_ref[...] = dot_nn(held, w_ref[...]).astype(low)


def first_back(mine, other, second, normed, inverse, vectors, mid, outward_at, width):
    rows = second.shape[0]
    return pl.pallas_call(
        first_back_kernel,
        out_shape=(
            shape((3, D), full),
            main((rows, D), full),
            main((rows, D), low),
            main((rows, width), low),
        ),
        grid=(rows // ROWS,),
        in_specs=[row_block(D)] * 4
        + [
            row_block(1),
            fixed_block(vectors.shape),
            fixed_block((D, width), outward_at // width),
        ],
        out_specs=(fixed_block((3, D)), row_block(D), row_block(D), row_block(width)),
        compiler_params=params(BACK),
        cost_estimate=cost(2 * rows * D * width, 20 * rows * D),
        name="first_back",
    )(mine, other, *streamed(second, normed, inverse), vectors, mid)


def source_kernel(*refs):
    grads, weights, out_ref = refs[:-2], refs[-2], refs[-1]
    width = 3 * LANES
    total = None
    for group, grad_ref in enumerate(grads):
        part = dot_nt(grad_ref[...], weights[:, group * width : (group + 1) * width])
        total = part if total is None else total + part
    out_ref[...] = total.astype(low)


def source_part(grads, inward):
    rows, width = grads[0].shape
    groups = len(grads)
    return pl.pallas_call(
        source_kernel,
        out_shape=shape((rows, D), low),
        grid=(rows // ROWS,),
        in_specs=[row_block(width) for _ in grads] + [fixed_block((D, groups * width))],
        out_specs=row_block(D),
        compiler_params=params(),
        cost_estimate=cost(2 * rows * D * width * groups, 2 * (rows + D) * width * groups),
        name="source",
    )(*streamed(*grads), inward)


def finish_kernel(mine_ref, other_ref, first_ref, out_ref):
    out_ref[...] = mine_ref[...].astype(full) + other_ref[...].astype(full) + first_ref[...]


def finish(mine, other, first):
    rows = first.shape[0]
    return pl.pallas_call(
        finish_kernel,
        out_shape=main((rows, D), full),
        grid=(rows // ROWS,),
        in_specs=[row_block(D)] * 3,
        out_specs=row_block(D),
        compiler_params=params(),
        cost_estimate=cost(2 * rows * D, 12 * rows * D),
        name="finish",
    )(mine, other, *streamed(first))


def weight_grad_kernel(bit, count, turned, extra, me_ref, left_ref, *refs):
    rights, refs = refs[:count], refs[count:]
    if extra:
        small_refs, refs = refs[:extra], refs[extra:]
        small, refs = refs[-1], refs[:-1]
        small[...] = jnp.zeros_like(small)
        at = 0
        for small_ref in small_refs:
            small[at : at + small_ref.shape[0], :] = small_ref[...]
            at += small_ref.shape[0]
    left = left_ref
    if not turned:
        left, refs = refs[-1], refs[:-1]

        def turn_block(i, carry):
            start = pl.multiple_of(i * ROWS, ROWS)
            block = left_ref[pl.ds(start, ROWS), :].astype(full)
            left[:, pl.ds(start, ROWS)] = block.T.astype(low)
            return carry

        lax.fori_loop(0, left_ref.shape[0] // ROWS, turn_block, 0, unroll=True)
    total_ref = refs[-1] if bit is not None else refs[0]
    if extra:
        total_ref[:, total_ref.shape[1] - LANES :] = small[...].T
    block = 2 * ROWS if rights[0].shape[1] % D else D
    if rights[0].shape[1] % block:
        right = jnp.concatenate([piece[...] for piece in rights], axis=1)
        total_ref[:, : right.shape[1]] = dot_nn(left[...], right)
    else:
        for at, piece in enumerate(rights):
            steps = piece.shape[1] // block

            def multiply(j, carry, at=at, piece=piece, steps=steps):
                start = pl.multiple_of(j * block, LANES)
                into = pl.multiple_of((at * steps + j) * block, LANES)
                total_ref[:, pl.ds(into, block)] = dot_nn(
                    left[...], piece[:, pl.ds(start, block)]
                )
                return carry

            if steps == 1:
                multiply(0, 0)
            else:
                lax.fori_loop(0, steps, multiply, 0)
    if bit is None:
        return
    layers, rows = refs[0].shape[1:3]
    for target, far in ((refs[0], 1), (refs[1], 0)):

        def spread(i, carry, target=target, far=far):
            other, k = i // layers, i % layers
            plane = 2 * other + far if bit == 0 else other + 2 * far
            owner = me_ref[0] ^ (4 * k + plane)
            start = pl.multiple_of(owner * rows, 8)
            target[other, k] = total_ref[pl.ds(start, rows), :].astype(low)
            return carry

        lax.fori_loop(0, 2 * layers, spread, 0)


def weight_grad(left, rights, me, size, bit, turned=False, extras=()):
    tokens = rights[0].shape[0]
    width = sum(right.shape[1] for right in rights)
    layers, rows = size // 4, D // size
    if me is not None:
        total = width + (LANES if extras else 0)
        outs = (shape((2, layers, rows, total), low),) * 2
        scratch = [pltpu.VMEM((D, total), full)]
    else:
        outs = (shape((D, width), full),)
        scratch = []
        me = jnp.zeros((1,), jnp.int32)
        bit = None
    if not turned:
        scratch.append(pltpu.VMEM((D, tokens), low))
    if extras:
        scratch.append(pltpu.VMEM((LANES, D), full))

    def whole(array):
        return pl.BlockSpec(array.shape, lambda j, m: (0,) * len(array.shape))

    flat = (left, *rights, *extras)
    return pl.pallas_call(
        partial(weight_grad_kernel, bit, len(rights), turned, len(extras)),
        out_shape=outs,
        grid_spec=pltpu.PrefetchScalarGridSpec(
            num_scalar_prefetch=1,
            grid=(1,),
            in_specs=[whole(array) for array in flat],
            out_specs=tuple(whole(array) for array in outs),
            scratch_shapes=scratch,
        ),
        compiler_params=params(GRADS),
        cost_estimate=cost(2 * tokens * D * width, 2 * tokens * (D + width)),
        name="weight_grad",
    )(me, *flat)


def adamw(master, gradient, first_moment, second_moment, step_rate, decay_rate, correct):
    first_new = 0.5 * first_moment + 0.5 * gradient
    second_new = 0.5 * second_moment + 0.5 * gradient * gradient
    moved = first_new / correct / (jnp.sqrt(second_new / correct) + 1e-08)
    return (master - step_rate * (moved + decay_rate * master), first_new, second_new)


def per_device(
    activations,
    cotangent,
    token_weight,
    lengths,
    step_count,
    inward_weight,
    output_weight,
    up_weight,
    down_weight,
    heads_bias,
    hidden_bias,
    norm_vectors,
    *moments,
):
    size = lax.axis_size("dp")
    rows, width = inward_weight.shape[1], inward_weight.shape[2]
    hidden_width = up_weight.shape[1]
    groups = width // LANES
    tokens = activations.shape[0]
    count = tokens // LEN
    fast = size == 16 and rows % 16 == 0
    me = lax.axis_index("dp").astype(jnp.int32).reshape(1) if fast else None

    small = jnp.concatenate(
        [heads_bias.reshape(-1), hidden_bias.reshape(-1), norm_vectors.reshape(-1)]
    )
    per_row = small.shape[0] // rows
    small_block = jnp.pad(small.reshape(rows, per_row), ((0, 0), (0, LANES - per_row)))
    inward_shard = jnp.concatenate(
        [
            inward_weight.reshape(3, rows, groups, LANES)
            .transpose(1, 2, 0, 3)
            .reshape(rows, 3 * width),
            small_block,
        ],
        axis=1,
    ).astype(low)
    block = hidden_width // 2
    outward_at = 2 * block
    up_shard, down_shard = up_weight.astype(low), down_weight.T.astype(low)
    first_shard = jnp.concatenate(
        [up_shard[:, :block], down_shard[:, :block], output_weight.T.astype(low)], axis=1
    )
    last_shard = jnp.concatenate([up_shard[:, block:], down_shard[:, block:]], axis=1)

    if fast:
        found = gather_planes(inward_shard, size)
        found_first = gather_doubled(after(first_shard, *found[1:]), size)
        found_last = gather_doubled(after(last_shard, found_first[1]), size)
        turned = turn(activations)
        found[0] = after(found[0], turned)
        own = split_halves(found)
        pairs = gather_pairs(own, gather_near(own, size))
        far = gather_far(pairs, size)
        own_first = split_halves(doubled_planes(*found_first))
        far = after_all(far, *own_first)
        own_first = after_all(own_first, *far)
        inward = place(pairs, far, me)
        near_first = gather_near(own_first, size)
        inward = after(inward, *own_first)
    else:
        inward, mid_first, mid_last = [
            lax.all_gather(shard, "dp", axis=0, tiled=True)
            for shard in (inward_shard, first_shard, last_shard)
        ]
        turned = turn(activations)

    smalls = inward[:, 3 * width : 3 * width + per_row].astype(full).reshape(size, -1)
    heads_size, hidden_size = heads_bias.size, hidden_bias.size
    head_biases = (
        smalls[:, :heads_size].reshape(size, 2, -1).transpose(1, 2, 0).reshape(2, width)
    )
    hidden_biases = smalls[:, heads_size : heads_size + hidden_size].T.reshape(1, hidden_width)
    vectors = (
        smalls[:, heads_size + hidden_size :].reshape(size, 6, rows).transpose(1, 0, 2)
    ).reshape(6, D)

    live = lax.broadcasted_iota(jnp.int32, (count, LEN), 1) < lengths[:, None]
    scale = (token_weight.reshape(count, LEN) * live.astype(jnp.int32)).astype(full)
    scale = scale.reshape(tokens, 1)

    first_pair = attend(lengths, activations, inward, head_biases, 0, 1)
    if fast:
        near_first = after_all(near_first, first_pair[2])
        pairs_first = gather_pairs(own_first, near_first)
        far_first = gather_far(pairs_first, size)
        own_last = split_halves(doubled_planes(*after_all(found_last, *pairs_first)))
        near_last = gather_near(own_last, size)
        gated = after(activations, *pairs_first, *own_last, vectors, hidden_biases)
    else:
        gated = after(activations, first_pair[2])
    later_pairs = attend(lengths, gated, inward, head_biases, 1, groups - 1)
    contexts = [first_pair[2], later_pairs[2]]
    if fast:
        pairs_last = gather_pairs(own_last, after_all(near_last, later_pairs[2]))
        far_last = gather_far(pairs_last, size)
        mid_first = place(pairs_first, after_all(far_first, *pairs_last), me)

    mine = outward_part(contexts, mid_first, outward_at)
    total, active_first, slope_first, middle, normed, inverse = expand_first(
        mine, swap_cores(mine), activations, vectors, hidden_biases, mid_first
    )
    if fast:
        mid_last = place(pairs_last, after_all(far_last, total), me)
    mine_down, active_last, slope_last = expand_last(total, middle, hidden_biases, mid_last)
    (
        mine_middle, second_sums, hidden_sums, output_rows,
        second_grad, second_low, hidden_first, hidden_last,
    ) = contract(
        mine_down, swap_cores(mine_down), normed, cotangent, scale, vectors,
        (slope_first, slope_last), (mid_first, mid_last),
    )
    other_middle = swap_cores(mine_middle)
    actives, hiddens = (active_first, active_last), (hidden_first, hidden_last)

    def back_first(*gates):
        return first_back(
            after(mine_middle, *gates), other_middle, second_grad, normed, inverse, vectors,
            mid_first, outward_at, width,
        )

    def attention_grads(group, *gates):
        at = max(group - 1, 0)
        qkv, weights, _ = later_pairs if group else first_pair
        return attend_back(after(qkv, *gates), weights, at, context_grad, group)

    def heads_outgoing(sums):
        return jnp.concatenate(sums, axis=1).reshape(2, -1, size).transpose(2, 0, 1)

    def small_outgoing(first_sums, head_sums):
        norm_grad = jnp.concatenate([first_sums, second_sums])
        return jnp.concatenate(
            [
                heads_outgoing(head_sums).reshape(size, -1),
                hidden_sums.reshape(-1, size).T,
                norm_grad.reshape(6, size, rows).transpose(1, 0, 2).reshape(size, -1),
            ],
            axis=1,
        )

    stacked, head_sums = [], []
    if fast:
        sent_down, kept_down = weight_grad(second_low, actives, me, size, 0)
        got_down = hop(sent_down, 1, size)
        sent_up, kept_up = weight_grad(after(middle, sent_down), hiddens, me, size, 1)
        got_up = hop(sent_up, 2, size)
        first_sums, first_grad, first_low, context_grad = back_first(sent_up)

        sent_out, kept_out = weight_grad(first_low, contexts, me, size, 0)
        got_out = hop(sent_out, 1, size)

        def attention(group, *gates):
            grads, sums = attention_grads(group, *gates)
            stacked.append(grads)
            head_sums.append(sums)

        attention(0, sent_out)
        got_down = after(got_down, stacked[0])
        next_down = kept_down[1] + got_down[1]
        more_down = hop(next_down, 2, size)
        gated = after(turned, next_down)
        sent_0, kept_0 = weight_grad(gated, [stacked[0]], me, size, 1, True)
        got_0 = hop(sent_0, 2, size)
        got_up = after(got_up, sent_0)
        next_up = kept_up[1] + got_up[1]
        more_up = hop(next_up, 1, size)

        attention(1, next_up)
        more_down = after(more_down, stacked[1])
        own_down, out_down = combine([(kept_down, got_down, more_down)])
        near_down = hop(out_down, 4, size)
        gated = after(turned, out_down)
        sent_1, kept_1 = weight_grad(gated, [stacked[1]], me, size, 0, True)
        got_1 = hop(sent_1, 1, size)

        attention(2, sent_1)
        extras = (
            first_sums,
            second_sums,
            hidden_sums.reshape(2, rows, size).transpose(0, 2, 1).reshape(2, D),
            jnp.concatenate(head_sums, axis=1).reshape(rows, size).T.reshape(1, D),
        )
        got_out, got_0, more_up = after_all((got_out, got_0, more_up), stacked[2])
        next_out, next_0 = after_all((kept_out[1] + got_out[1], kept_0[1] + got_0[1]))
        more_out, more_0 = hop(next_out, 2, size), hop(next_0, 1, size)
        own_up, out_up = combine([(kept_up, got_up, after(more_up, next_out, next_0))])
        near_up = hop(out_up, 4, size)
        near_down = after(near_down, out_up)
        next_far = far_half(own_down, near_down)
        gated = after(turned, out_up, next_far)
        sent_2, kept_2 = weight_grad(gated, [stacked[2]], me, size, 1, True, extras)
        got_2 = hop(sent_2, 2, size)

        mine_source = source_part([after(stacked[0], sent_2)] + stacked[1:], inward)
        other_source = swap_cores(mine_source)
        far_down = hop(after(next_far, mine_source), 8, size)
        near_up, more_out, more_0, got_1, got_2 = after_all(
            (near_up, more_out, more_0, got_1, got_2), mine_source
        )
        own_near, out_near = combine([(kept_out, got_out, more_out), (kept_0, got_0, more_0)])
        near_near = hop(out_near, 4, size)
        next_far = far_half(own_up, after(near_up, out_near))
        far_up = hop(next_far, 8, size)
        got_1, got_2 = after_all((got_1, got_2), next_far)
        next_1, next_2 = after_all((kept_1[1] + got_1[1], kept_2[1] + got_2[1]))
        more_1, more_2 = hop(next_1, 2, size), hop(next_2, 1, size)
        near_near, far_down = after_all((near_near, far_down), next_1, next_2)
        next_far = far_half(own_near, near_near)
        far_near = hop(next_far, 8, size)
        more_1, more_2 = after_all((more_1, more_2), next_far)
        own_last, out_last = combine([(kept_1, got_1, more_1), (kept_2, got_2, more_2)])
        near_last = hop(out_last, 4, size)
        input_grad = finish(mine_source, after(other_source, out_last), first_grad)
        near_last = after(near_last, input_grad)
        far_last = hop(far_half(own_last, near_last), 8, size)
        downward_grad = reduce_sum(own_down, near_down, far_down)
        upward_grad = reduce_sum(own_up, near_up, far_up)
        near_grad = reduce_sum(own_near, near_near, far_near)
        far_grad = reduce_sum(own_last, near_last, far_last)
        outward_grad = near_grad[:, :width]
        cut = 3 * LANES
        inward_grads = [near_grad[:, width:], far_grad[:, :cut], far_grad[:, cut : 2 * cut]]
        small_grad = far_grad[:, 2 * cut :]
        small_grads = (
            small_grad[:, 8].reshape(heads_bias.shape),
            small_grad[:, 6:8].T.reshape(hidden_bias.shape),
            small_grad[:, :6].T,
        )
    else:

        def reduced(left, rights, turned=False):
            (value,) = weight_grad(left, rights, None, size, None, turned)
            return lax.psum_scatter(value, "dp", scatter_dimension=0, tiled=True)

        first_sums, first_grad, first_low, context_grad = back_first()
        downward_grad = reduced(second_low, actives)
        upward_grad = reduced(middle, hiddens)
        outward_grad = reduced(first_low, contexts)
        inward_grads = []
        for group in range(groups):
            grads, sums = attention_grads(group)
            stacked.append(grads)
            head_sums.append(sums)
            inward_grads.append(reduced(turned, [grads], True))
        mine_source = source_part(stacked, inward)
        small_grad = lax.psum_scatter(
            small_outgoing(first_sums, head_sums), "dp", scatter_dimension=0, tiled=True
        ).reshape(-1)
        small_grads = (
            small_grad[:heads_size].reshape(heads_bias.shape),
            small_grad[heads_size : heads_size + hidden_size].reshape(hidden_bias.shape),
            small_grad[heads_size + hidden_size :].reshape(norm_vectors.shape),
        )
        input_grad = finish(mine_source, swap_cores(mine_source), first_grad)

    inward_grad = jnp.stack(
        [
            jnp.concatenate(
                [grad[:, kind * LANES : (kind + 1) * LANES] for grad in inward_grads], axis=1
            )
            for kind in range(3)
        ]
    )
    grads = (
        inward_grad,
        outward_grad.T,
        upward_grad,
        downward_grad.T,
        *small_grads,
    )

    step_value = step_count[0].astype(full)
    correct = 1.0 - jnp.power(0.5, step_value)
    plan = (step_value + 4.0) / 12.0
    rates = (D ** (-0.5), (6 * D // LEN) ** (-0.5), D ** (-0.5), FF ** (-0.5), 0.5, 0.5, 0.3)
    decays = (0.01, 0.01, 0.01, 0.01, 0.0, 0.0, 0.0)
    masters = (
        inward_weight,
        output_weight,
        up_weight,
        down_weight,
        heads_bias,
        hidden_bias,
        norm_vectors,
    )
    results = [output_rows, input_grad]
    for at in range(7):
        results.extend(
            adamw(
                masters[at],
                grads[at],
                moments[at],
                moments[7 + at],
                rates[at] * plan,
                decays[at],
                correct,
            )
        )
    return tuple(results)


def solution(mesh):
    matrices = (
        P(None, "dp", "tensor"),
        P("tensor", "dp"),
        P("dp", "tensor"),
        P("tensor", "dp"),
        P(None, "tensor", "dp"),
        P("tensor", "dp"),
        P(None, "dp"),
    )
    in_specs = (
        (P("dp", None), P("dp", None), P("dp"), P("dp"), P()) + matrices + matrices + matrices
    )
    out_specs = (P("dp", None), P("dp", None)) + tuple(
        spec for spec in matrices for _ in range(3)
    )
    return jax.shard_map(
        per_device, mesh=mesh, in_specs=in_specs, out_specs=out_specs, check_vma=False
    )
```

```python
from functools import partial
import math

import jax
import jax.numpy as jnp
from jax import lax
from jax.experimental import pallas as pl
from jax.experimental.pallas import tpu as pltpu
from jax.sharding import PartitionSpec as P

D = 768
HEAD_DIM = 64
FF = 3072
LEN = 512
LANES = 128
ROWS = 384
COST_SHARE = 1
ATTEND, BACK, EXPAND, CONTRACT, GRADS = 12, 16, 22, 26, 16

norm_epsilon = 1e-12
low = jnp.bfloat16
full = jnp.float32


def dot_nn(left, right):
    return lax.dot_general(left, right, (((1,), (0,)), ((), ())), preferred_element_type=full)


def dot_nt(left, right):
    return lax.dot_general(left, right, (((1,), (1,)), ((), ())), preferred_element_type=full)


def column_sum(values):
    return jnp.sum(values, axis=0, keepdims=True)


def row_mean(values):
    return jnp.mean(values, axis=-1, keepdims=True)


def normalize(total_in):
    centred = total_in - row_mean(total_in)
    inverse = lax.rsqrt(row_mean(centred * centred) + norm_epsilon)
    return (centred * inverse, inverse)


def norm_back(incoming, normed, inverse, gain):
    scaled = incoming * gain
    return inverse * (scaled - row_mean(scaled) - normed * row_mean(scaled * normed))


def cost(flops, moved, exps=0):
    return pl.CostEstimate(
        flops=int(flops / COST_SHARE),
        bytes_accessed=int(moved / COST_SHARE),
        transcendentals=int(exps / COST_SHARE),
    )


def params(mebibytes=12):
    return pltpu.CompilerParams(vmem_limit_bytes=mebibytes * 1024 * 1024)


def shape(dims, kind):
    return jax.ShapeDtypeStruct(dims, kind)


def main(dims, kind):
    return pltpu.HBM(dims, kind)


def streamed(*arrays):
    return [pltpu.with_memory_space_constraint(array, pltpu.HBM) for array in arrays]


def after(value, *others):
    return lax.optimization_barrier((value,) + others)[0]


def after_all(values, *others):
    return lax.optimization_barrier(tuple(values) + others)[: len(values)]


def hop(value, offset, size):
    return lax.ppermute(value, "dp", [(d, d ^ offset) for d in range(size)])


def swap_cores(value):
    return lax.ppermute(value, "tensor", [(0, 1), (1, 0)])


def split_columns(width):
    return -(-width // (2 * LANES)) * LANES


def gather_planes(shard, size):
    found = [shard] + [hop(shard, 4 * k, size) for k in range(1, size // 4)]
    return found


def gather_doubled(shard, size):
    pair = jnp.stack([shard, hop(shard, 8, size)])
    return (pair, hop(pair, 4, size))


def doubled_planes(pair, near):
    return [pair[0], near[0], pair[1], near[1]]


def split_halves(found):
    stacked = jnp.stack(found)
    cut = split_columns(stacked.shape[2])
    return lax.optimization_barrier((stacked[..., :cut], stacked[..., cut:]))


def gather_near(own, size):
    return (hop(own[0], 2, size), hop(own[1], 1, size))


def gather_pairs(own, near):
    return lax.optimization_barrier(
        (jnp.concatenate([own[0], near[0]]), jnp.concatenate([own[1], near[1]]))
    )


def gather_far(pairs, size):
    return (hop(pairs[0], 1, size), hop(pairs[1], 2, size))


def place_kernel(me_ref, pair_a, far_a, pair_b, far_b, out_ref):
    layers, rows, cut = pair_a.shape
    layers //= 2
    sources = (
        (pair_a, 0, pair_b, 0),
        (far_a, 0, pair_b, layers),
        (pair_a, layers, far_b, 0),
        (far_a, layers, far_b, layers),
    )
    for plane, (left, left_at, right, right_at) in enumerate(sources):
        for k in range(layers):
            start = pl.multiple_of((me_ref[0] ^ (4 * k + plane)) * rows, 16)
            out_ref[pl.ds(start, rows), :cut] = left[left_at + k]
            out_ref[pl.ds(start, rows), cut:] = right[right_at + k]


def place(pairs, far, me):
    flat = (pairs[0], far[0], pairs[1], far[1])
    layers, rows, cut = pairs[0].shape
    width = cut + pairs[1].shape[2]
    total = 2 * layers * rows
    return pl.pallas_call(
        place_kernel,
        out_shape=shape((total, width), low),
        grid_spec=pltpu.PrefetchScalarGridSpec(
            num_scalar_prefetch=1,
            grid=(1,),
            in_specs=[pl.BlockSpec(piece.shape, lambda i, m: (0, 0, 0)) for piece in flat],
            out_specs=pl.BlockSpec((total, width), lambda i, m: (0, 0)),
        ),
        compiler_params=params(12),
        cost_estimate=cost(0, 4 * total * width),
        name="place",
    )(me, *flat)


def turn_kernel(source_ref, out_ref):
    out_ref[...] = source_ref[...].astype(full).T.astype(low)


def turn(source):
    rows, width = source.shape
    return pl.pallas_call(
        turn_kernel,
        out_shape=shape((width, rows), low),
        grid=(rows // LEN,),
        in_specs=[pl.BlockSpec((LEN, width), lambda i: (i, 0))],
        out_specs=pl.BlockSpec((width, LEN), lambda i: (0, i)),
        compiler_params=params(16),
        cost_estimate=cost(0, 4 * rows * width),
        name="turn",
    )(source)


def combine_kernel(count, *refs):
    own_ref, out_ref = refs[-2:]
    start = 0
    for at in range(count):
        kept, got, more = refs[3 * at : 3 * at + 3]
        total = kept[0].astype(full) + got[0].astype(full) + more[...].astype(full)
        width = total.shape[2]
        for k in range(total.shape[0]):
            if k % 2:
                out_ref[k // 2, :, start : start + width] = total[k].astype(low)
            else:
                own_ref[k // 2, :, start : start + width] = total[k]
        start += width


def combine(halves):
    layers, rows = halves[0][2].shape[:2]
    width = sum(more.shape[2] for _, _, more in halves)
    flat, specs = [], []
    for kept, got, more in halves:
        part = (1,) + more.shape
        flat += [kept, got, more]
        specs += [pl.BlockSpec(part, lambda i: (0, 0, 0, 0))] * 2
        specs += [pl.BlockSpec(more.shape, lambda i: (0, 0, 0))]
    piece = (layers // 2, rows, width)
    return pl.pallas_call(
        partial(combine_kernel, len(halves)),
        out_shape=(shape(piece, full), shape(piece, low)),
        grid=(1,),
        in_specs=specs,
        out_specs=(pl.BlockSpec(piece, lambda i: (0, 0, 0)),) * 2,
        compiler_params=params(16),
        cost_estimate=cost(3 * layers * rows * width, 8 * layers * rows * width),
        name="combine",
    )(*flat)


def advance_kernel(kept_a, got_a, kept_b, got_b, out_a, out_b):
    out_a[...] = (kept_a[0].astype(full) + got_a[0].astype(full)).astype(low)
    out_b[...] = (kept_b[0].astype(full) + got_b[0].astype(full)).astype(low)


def advance(kept_a, got_a, kept_b, got_b):
    flat = (kept_a, got_a, kept_b, got_b)
    pieces = (kept_a.shape[1:], kept_b.shape[1:])
    return pl.pallas_call(
        advance_kernel,
        out_shape=tuple(shape(piece, low) for piece in pieces),
        grid=(1,),
        in_specs=[pl.BlockSpec((1,) + part.shape[1:], lambda i: (1, 0, 0, 0)) for part in flat],
        out_specs=tuple(pl.BlockSpec(piece, lambda i: (0, 0, 0)) for piece in pieces),
        compiler_params=params(),
        cost_estimate=cost(kept_a.size + kept_b.size, 3 * (kept_a.size + kept_b.size)),
        name="advance",
    )(*flat)


def far_half(own, near):
    return (own[1] + near[1].astype(full)).astype(low)


def reduce_sum(own, near, far):
    return own[0] + near[0].astype(full) + far.astype(full)


def attend_kernel(length_ref, x_ref, w_ref, bias_ref, qkv_ref, weight_ref, context_ref):
    length = length_ref[pl.program_id(1)]
    mixed = dot_nn(x_ref[...], w_ref[...])
    queries = (mixed[:, :LANES] + bias_ref[0:1, :]).astype(low)
    key_rows = mixed[:, LANES : 2 * LANES].astype(low)
    values_full = mixed[:, 2 * LANES :] + bias_ref[1:2, :]
    values = values_full.astype(low)
    qkv_ref[:, :LANES] = queries
    qkv_ref[:, LANES : 2 * LANES] = key_rows
    qkv_ref[:, 2 * LANES :] = values
    values_t = values_full.T.astype(low)
    rows = queries.shape[0]
    lane = lax.broadcasted_iota(jnp.int32, (rows, LANES), 1)
    live = lax.broadcasted_iota(jnp.int32, (rows, 1), 0) < length
    scaled = queries * (1.0 / math.sqrt(HEAD_DIM))
    parts = []
    for head in range(2):
        picked = jnp.where((lane >= HEAD_DIM) == bool(head), scaled, jnp.zeros_like(scaled))
        scores = jnp.where(live, dot_nt(key_rows, picked), -jnp.inf)
        grown = jnp.exp(scores - jnp.max(scores, axis=0, keepdims=True))
        weights = (grown * (1.0 / jnp.sum(grown, axis=0, keepdims=True))).astype(low)
        weight_ref[0, head] = weights
        parts.append(dot_nn(values_t[head * HEAD_DIM : (head + 1) * HEAD_DIM, :], weights))
    context_ref[...] = jnp.concatenate(parts, axis=0).T.astype(low)


def attend(lengths, source, inward, biases, first, groups):
    rows = source.shape[0]
    count = rows // LEN
    width = 3 * LANES
    return pl.pallas_call(
        attend_kernel,
        out_shape=(
            main((rows, groups * width), low),
            main((groups * count, 2, LEN, LEN), low),
            main((rows, groups * LANES), low),
        ),
        grid_spec=pltpu.PrefetchScalarGridSpec(
            num_scalar_prefetch=1,
            grid=(groups, count),
            in_specs=[
                pl.BlockSpec((LEN, D), lambda g, s, n: (s, 0)),
                pl.BlockSpec((D, width), lambda g, s, n: (0, first + g)),
                pl.BlockSpec((2, LANES), lambda g, s, n: (0, first + g)),
            ],
            out_specs=(
                pl.BlockSpec((LEN, width), lambda g, s, n: (s, g)),
                pl.BlockSpec((1, 2, LEN, LEN), lambda g, s, n: (g * count + s, 0, 0, 0)),
                pl.BlockSpec((LEN, LANES), lambda g, s, n: (s, g)),
            ),
        ),
        compiler_params=params(ATTEND),
        cost_estimate=cost(
            groups * (2 * rows * D * width + 8 * count * LEN * LEN * LANES),
            groups * count * 2 * LEN * LEN * 2,
            groups * count * 2 * LEN * LEN,
        ),
        name="attend",
    )(lengths, *streamed(source), inward, biases)


def attend_back_kernel(qkv_ref, weight_ref, grad_ref, out_ref, sum_ref):
    @pl.when(pl.program_id(0) == 0)
    def _():
        sum_ref[...] = jnp.zeros_like(sum_ref)

    queries = qkv_ref[:, :LANES]
    key_rows = qkv_ref[:, LANES : 2 * LANES]
    values = qkv_ref[:, 2 * LANES :]
    grads = grad_ref[...]
    keys_t = key_rows.astype(full).T.astype(low)
    rows = queries.shape[0]
    lane = lax.broadcasted_iota(jnp.int32, (rows, LANES), 1)
    score_scale = 1.0 / math.sqrt(HEAD_DIM)
    query_parts, key_parts, value_parts = [], [], []
    for head in range(2):
        picked = jnp.where((lane >= HEAD_DIM) == bool(head), grads, jnp.zeros_like(grads))
        weights = weight_ref[0, head]
        wide = weights.astype(full)
        mixed = wide * dot_nt(values, picked)
        score_grads = (mixed - wide * jnp.sum(mixed, axis=0, keepdims=True)).astype(low)
        value_parts.append(dot_nn(weights, grads))
        key_parts.append(dot_nn(score_grads, queries))
        query_parts.append(
            dot_nn(keys_t[head * HEAD_DIM : (head + 1) * HEAD_DIM, :], score_grads)
        )
    first = lane < HEAD_DIM
    query_grads = (jnp.concatenate(query_parts, axis=0).T * score_scale).astype(low)
    key_grads = (jnp.where(first, key_parts[0], key_parts[1]) * score_scale).astype(low)
    value_grads = jnp.where(first, value_parts[0], value_parts[1]).astype(low)
    out_ref[:, :LANES] = query_grads
    out_ref[:, LANES : 2 * LANES] = key_grads
    out_ref[:, 2 * LANES :] = value_grads
    sum_ref[0:1, :] += column_sum(query_grads.astype(full))
    sum_ref[1:2, :] += column_sum(value_grads.astype(full))


def attend_back(qkv, weights, at, grads, group):
    rows = qkv.shape[0]
    count = rows // LEN
    width = 3 * LANES
    return pl.pallas_call(
        attend_back_kernel,
        out_shape=(main((rows, width), low), shape((2, LANES), full)),
        grid=(count,),
        in_specs=[
            pl.BlockSpec((LEN, width), lambda s: (s, at)),
            pl.BlockSpec((1, 2, LEN, LEN), lambda s: (at * count + s, 0, 0, 0)),
            pl.BlockSpec((LEN, LANES), lambda s: (s, group)),
        ],
        out_specs=(
            pl.BlockSpec((LEN, width), lambda s: (s, 0)),
            pl.BlockSpec((2, LANES), lambda s: (0, 0)),
        ),
        compiler_params=params(BACK),
        cost_estimate=cost(
            16 * count * LEN * LEN * LANES, count * 2 * LEN * LEN * 2 + 4 * rows * width
        ),
        name="attend_back",
    )(*streamed(qkv, weights, grads))


def outward_kernel(*refs):
    contexts, w_ref, out_ref = refs[:-2], refs[-2], refs[-1]
    context = jnp.concatenate([ref[...] for ref in contexts], axis=1)
    out_ref[...] = dot_nt(context, w_ref[...]).astype(low)


def row_block(width):
    return pl.BlockSpec((ROWS, width), lambda i: (i, 0))


def fixed_block(dims, at=0):
    return pl.BlockSpec(dims, lambda i: (0, at))


def outward_part(contexts, mid, outward_at):
    rows = contexts[0].shape[0]
    width = sum(context.shape[1] for context in contexts)
    return pl.pallas_call(
        outward_kernel,
        out_shape=shape((rows, D), low),
        grid=(rows // ROWS,),
        in_specs=[row_block(context.shape[1]) for context in contexts]
        + [fixed_block((D, width), outward_at // width)],
        out_specs=row_block(D),
        compiler_params=params(),
        cost_estimate=cost(2 * rows * D * width, 2 * (rows * D + rows * width + D * width)),
        name="outward",
    )(*streamed(*contexts), mid)


def gelu_parts(hidden):
    half = 0.5 + 0.5 * lax.erf(hidden * 0.7071067811865476)
    slope = half + hidden * 0.3989422804014327 * jnp.exp(-0.5 * hidden * hidden)
    return ((hidden * half).astype(low), slope.astype(low))


def expand_first_kernel(
    mine_ref, other_ref, x_ref, vector_ref, bias_ref, up_ref, down_ref,
    total_ref, active_ref, slope_ref, middle_ref, normed_ref, inverse_ref,
):
    summed = (
        mine_ref[...].astype(full)
        + other_ref[...].astype(full)
        + vector_ref[0:1, :]
        + x_ref[...].astype(full)
    )
    normed, inverse = normalize(summed)
    normed_ref[...] = normed
    inverse_ref[...] = inverse
    held = (normed * vector_ref[1:2, :] + vector_ref[2:3, :]).astype(low)
    middle_ref[...] = held
    active, slope = gelu_parts(dot_nn(held, up_ref[...]) + bias_ref[...])
    active_ref[...] = active
    slope_ref[...] = slope
    total_ref[...] = dot_nt(active, down_ref[...])


def expand_first(mine, other, source, vectors, hidden_bias, mid):
    rows, hidden = source.shape[0], hidden_bias.shape[1]
    block = hidden // 2
    return pl.pallas_call(
        expand_first_kernel,
        out_shape=(
            main((rows, D), full),
            main((rows, block), low),
            main((rows, block), low),
            main((rows, D), low),
            main((rows, D), full),
            main((rows, 1), full),
        ),
        grid=(rows // ROWS,),
        in_specs=[
            row_block(D),
            row_block(D),
            row_block(D),
            fixed_block(vectors.shape),
            fixed_block((1, block)),
            fixed_block((D, block)),
            fixed_block((D, block), 1),
        ],
        out_specs=(
            row_block(D), row_block(block), row_block(block), row_block(D), row_block(D),
            row_block(1),
        ),
        compiler_params=params(EXPAND),
        cost_estimate=cost(4 * rows * D * block, 4 * D * block + 16 * rows * D, 2 * rows * block),
        name="expand_first",
    )(mine, other, *streamed(source), vectors, hidden_bias, mid, mid)


def expand_last_kernel(
    total_ref, middle_ref, bias_ref, up_ref, down_ref, part_ref, active_ref, slope_ref
):
    active, slope = gelu_parts(dot_nn(middle_ref[...], up_ref[...]) + bias_ref[...])
    active_ref[...] = active
    slope_ref[...] = slope
    part_ref[...] = (total_ref[...] + dot_nt(active, down_ref[...])).astype(low)


def expand_last(total, middle, hidden_bias, mid):
    rows, hidden = total.shape[0], hidden_bias.shape[1]
    block = hidden // 2
    return pl.pallas_call(
        expand_last_kernel,
        out_shape=(shape((rows, D), low), main((rows, block), low), main((rows, block), low)),
        grid=(rows // ROWS,),
        in_specs=[
            row_block(D),
            row_block(D),
            fixed_block((1, block), 1),
            fixed_block((D, block)),
            fixed_block((D, block), 1),
        ],
        out_specs=(row_block(D), row_block(block), row_block(block)),
        compiler_params=params(EXPAND),
        cost_estimate=cost(4 * rows * D * block, 4 * D * block + 10 * rows * D, 2 * rows * block),
        name="expand_last",
    )(*streamed(total, middle), hidden_bias, mid, mid)


def contract_kernel(
    mine_ref, other_ref, normed_ref, cotangent_ref, scale_ref, vector_ref,
    slope_first, slope_last, up_first, down_first, up_last, down_last,
    part_ref, sum_ref, hidden_sum_ref, out_ref, wide_ref, low_ref, hidden_first, hidden_last,
):
    @pl.when(pl.program_id(0) == 0)
    def _():
        sum_ref[...] = jnp.zeros_like(sum_ref)
        hidden_sum_ref[...] = jnp.zeros_like(hidden_sum_ref)

    middle = normed_ref[...] * vector_ref[1:2, :] + vector_ref[2:3, :]
    summed = (
        mine_ref[...].astype(full) + other_ref[...].astype(full) + vector_ref[3:4, :] + middle
    )
    normed, inverse = normalize(summed)
    out_ref[...] = (normed * vector_ref[4:5, :] + vector_ref[5:6, :]).astype(low)
    incoming = cotangent_ref[...].astype(full) * scale_ref[...]
    second = norm_back(incoming, normed, inverse, vector_ref[4:5, :])
    sum_ref[0:1, :] += column_sum(second)
    sum_ref[1:2, :] += column_sum(incoming * normed)
    sum_ref[2:3, :] += column_sum(incoming)
    wide_ref[...] = second
    held = second.astype(low)
    low_ref[...] = held
    block = up_first.shape[1]
    total = None
    for at, slope_ref, up_ref, down_ref, hidden_ref in (
        (0, slope_first, up_first, down_first, hidden_first),
        (block, slope_last, up_last, down_last, hidden_last),
    ):
        hidden_grad = (dot_nn(held, down_ref[...]) * slope_ref[...].astype(full)).astype(low)
        hidden_ref[...] = hidden_grad
        hidden_sum_ref[:, at : at + block] += column_sum(hidden_grad.astype(full))
        part = dot_nt(hidden_grad, up_ref[...])
        total = part if total is None else total + part
    part_ref[...] = total.astype(low)


def contract(mine, other, normed, cotangent, scale, vectors, slopes, mids):
    rows, block = slopes[0].shape
    hidden = 2 * block
    weights = [fixed_block((D, block)), fixed_block((D, block), 1)]
    return pl.pallas_call(
        contract_kernel,
        out_shape=(
            shape((rows, D), low),
            shape((3, D), full),
            shape((1, hidden), full),
            main((rows, D), low),
            main((rows, D), full),
            main((rows, D), low),
            main((rows, block), low),
            main((rows, block), low),
        ),
        grid=(rows // ROWS,),
        in_specs=[
            row_block(D),
            row_block(D),
            row_block(D),
            row_block(D),
            row_block(1),
            fixed_block(vectors.shape),
            row_block(block),
            row_block(block),
        ]
        + weights
        + weights,
        out_specs=(
            row_block(D),
            fixed_block((3, D)),
            fixed_block((1, hidden)),
            row_block(D),
            row_block(D),
            row_block(D),
            row_block(block),
            row_block(block),
        ),
        compiler_params=params(CONTRACT),
        cost_estimate=cost(4 * rows * D * hidden, 4 * D * hidden + 4 * rows * hidden),
        name="contract",
    )(
        mine, other, *streamed(normed, cotangent), scale, vectors, *streamed(*slopes),
        mids[0], mids[0], mids[1], mids[1],
    )


def first_back_kernel(
    mine_ref, other_ref, second_ref, normed_ref, inverse_ref, vector_ref, w_ref,
    sum_ref, wide_ref, low_ref, grad_ref,
):
    @pl.when(pl.program_id(0) == 0)
    def _():
        sum_ref[...] = jnp.zeros_like(sum_ref)

    incoming = mine_ref[...].astype(full) + other_ref[...].astype(full) + second_ref[...]
    normed = normed_ref[...]
    first = norm_back(incoming, normed, inverse_ref[...], vector_ref[1:2, :])
    sum_ref[0:1, :] += column_sum(first)
    sum_ref[1:2, :] += column_sum(incoming * normed)
    sum_ref[2:3, :] += column_sum(incoming)
    wide_ref[...] = first
    held = first.astype(low)
    low_ref[...] = held
    grad_ref[...] = dot_nn(held, w_ref[...]).astype(low)


def first_back(mine, other, second, normed, inverse, vectors, mid, outward_at, width):
    rows = second.shape[0]
    return pl.pallas_call(
        first_back_kernel,
        out_shape=(
            shape((3, D), full),
            main((rows, D), full),
            main((rows, D), low),
            main((rows, width), low),
        ),
        grid=(rows // ROWS,),
        in_specs=[row_block(D)] * 4
        + [
            row_block(1),
            fixed_block(vectors.shape),
            fixed_block((D, width), outward_at // width),
        ],
        out_specs=(fixed_block((3, D)), row_block(D), row_block(D), row_block(width)),
        compiler_params=params(BACK),
        cost_estimate=cost(2 * rows * D * width, 20 * rows * D),
        name="first_back",
    )(mine, other, *streamed(second, normed, inverse), vectors, mid)


def source_kernel(*refs):
    grads, weights, out_ref = refs[:-2], refs[-2], refs[-1]
    width = 3 * LANES
    total = None
    for group, grad_ref in enumerate(grads):
        part = dot_nt(grad_ref[...], weights[:, group * width : (group + 1) * width])
        total = part if total is None else total + part
    out_ref[...] = total.astype(low)


def source_part(grads, inward):
    rows, width = grads[0].shape
    groups = len(grads)
    return pl.pallas_call(
        source_kernel,
        out_shape=shape((rows, D), low),
        grid=(rows // ROWS,),
        in_specs=[row_block(width) for _ in grads] + [fixed_block((D, groups * width))],
        out_specs=row_block(D),
        compiler_params=params(),
        cost_estimate=cost(2 * rows * D * width * groups, 2 * (rows + D) * width * groups),
        name="source",
    )(*streamed(*grads), inward)


def finish_kernel(mine_ref, other_ref, first_ref, out_ref):
    out_ref[...] = mine_ref[...].astype(full) + other_ref[...].astype(full) + first_ref[...]


def finish(mine, other, first):
    rows = first.shape[0]
    return pl.pallas_call(
        finish_kernel,
        out_shape=main((rows, D), full),
        grid=(rows // ROWS,),
        in_specs=[row_block(D)] * 3,
        out_specs=row_block(D),
        compiler_params=params(),
        cost_estimate=cost(2 * rows * D, 12 * rows * D),
        name="finish",
    )(mine, other, *streamed(first))


def weight_grad_kernel(bit, count, turned, extra, me_ref, left_ref, *refs):
    rights, refs = refs[:count], refs[count:]
    if extra:
        small_refs, refs = refs[:extra], refs[extra:]
        small, refs = refs[-1], refs[:-1]
        small[...] = jnp.zeros_like(small)
        at = 0
        for small_ref in small_refs:
            small[at : at + small_ref.shape[0], :] = small_ref[...]
            at += small_ref.shape[0]
    left = left_ref
    if not turned:
        left, refs = refs[-1], refs[:-1]

        def turn_block(i, carry):
            start = pl.multiple_of(i * ROWS, ROWS)
            block = left_ref[pl.ds(start, ROWS), :].astype(full)
            left[:, pl.ds(start, ROWS)] = block.T.astype(low)
            return carry

        lax.fori_loop(0, left_ref.shape[0] // ROWS, turn_block, 0, unroll=True)
    total_ref = refs[-1] if bit is not None else refs[0]
    if extra:
        total_ref[:, total_ref.shape[1] - LANES :] = small[...].T
    block = 2 * ROWS if rights[0].shape[1] % D else D
    if rights[0].shape[1] % block:
        right = jnp.concatenate([piece[...] for piece in rights], axis=1)
        total_ref[:, : right.shape[1]] = dot_nn(left[...], right)
    else:
        for at, piece in enumerate(rights):
            steps = piece.shape[1] // block

            def multiply(j, carry, at=at, piece=piece, steps=steps):
                start = pl.multiple_of(j * block, LANES)
                into = pl.multiple_of((at * steps + j) * block, LANES)
                total_ref[:, pl.ds(into, block)] = dot_nn(
                    left[...], piece[:, pl.ds(start, block)]
                )
                return carry

            if steps == 1:
                multiply(0, 0)
            else:
                lax.fori_loop(0, steps, multiply, 0)
    if bit is None:
        return
    layers, rows = refs[0].shape[1:3]
    for target, far in ((refs[0], 1), (refs[1], 0)):

        def spread(i, carry, target=target, far=far):
            other, k = i // layers, i % layers
            plane = 2 * other + far if bit == 0 else other + 2 * far
            owner = me_ref[0] ^ (4 * k + plane)
            start = pl.multiple_of(owner * rows, 8)
            target[other, k] = total_ref[pl.ds(start, rows), :].astype(low)
            return carry

        lax.fori_loop(0, 2 * layers, spread, 0)


def weight_grad(left, rights, me, size, bit, turned=False, extras=()):
    tokens = rights[0].shape[0]
    width = sum(right.shape[1] for right in rights)
    layers, rows = size // 4, D // size
    if me is not None:
        total = width + (LANES if extras else 0)
        outs = (shape((2, layers, rows, total), low),) * 2
        scratch = [pltpu.VMEM((D, total), full)]
    else:
        outs = (shape((D, width), full),)
        scratch = []
        me = jnp.zeros((1,), jnp.int32)
        bit = None
    if not turned:
        scratch.append(pltpu.VMEM((D, tokens), low))
    if extras:
        scratch.append(pltpu.VMEM((LANES, D), full))

    def whole(array):
        return pl.BlockSpec(array.shape, lambda j, m: (0,) * len(array.shape))

    flat = (left, *rights, *extras)
    return pl.pallas_call(
        partial(weight_grad_kernel, bit, len(rights), turned, len(extras)),
        out_shape=outs,
        grid_spec=pltpu.PrefetchScalarGridSpec(
            num_scalar_prefetch=1,
            grid=(1,),
            in_specs=[whole(array) for array in flat],
            out_specs=tuple(whole(array) for array in outs),
            scratch_shapes=scratch,
        ),
        compiler_params=params(GRADS),
        cost_estimate=cost(2 * tokens * D * width, 2 * tokens * (D + width)),
        name="weight_grad",
    )(me, *flat)


def adamw(master, gradient, first_moment, second_moment, step_rate, decay_rate, correct):
    first_new = 0.5 * first_moment + 0.5 * gradient
    second_new = 0.5 * second_moment + 0.5 * gradient * gradient
    moved = first_new / correct / (jnp.sqrt(second_new / correct) + 1e-08)
    return (master - step_rate * (moved + decay_rate * master), first_new, second_new)


def per_device(
    activations,
    cotangent,
    token_weight,
    lengths,
    step_count,
    inward_weight,
    output_weight,
    up_weight,
    down_weight,
    heads_bias,
    hidden_bias,
    norm_vectors,
    *moments,
):
    size = lax.axis_size("dp")
    rows, width = inward_weight.shape[1], inward_weight.shape[2]
    hidden_width = up_weight.shape[1]
    groups = width // LANES
    tokens = activations.shape[0]
    count = tokens // LEN
    fast = size == 16 and rows % 16 == 0
    me = lax.axis_index("dp").astype(jnp.int32).reshape(1) if fast else None

    small = jnp.concatenate(
        [heads_bias.reshape(-1), hidden_bias.reshape(-1), norm_vectors.reshape(-1)]
    )
    per_row = small.shape[0] // rows
    small_block = jnp.pad(small.reshape(rows, per_row), ((0, 0), (0, LANES - per_row)))
    inward_shard = jnp.concatenate(
        [
            inward_weight.reshape(3, rows, groups, LANES)
            .transpose(1, 2, 0, 3)
            .reshape(rows, 3 * width),
            small_block,
        ],
        axis=1,
    ).astype(low)
    block = hidden_width // 2
    outward_at = 2 * block
    up_shard, down_shard = up_weight.astype(low), down_weight.T.astype(low)
    first_shard = jnp.concatenate(
        [up_shard[:, :block], down_shard[:, :block], output_weight.T.astype(low)], axis=1
    )
    last_shard = jnp.concatenate([up_shard[:, block:], down_shard[:, block:]], axis=1)

    if fast:
        found = gather_planes(inward_shard, size)
        found_first = gather_doubled(after(first_shard, *found[1:]), size)
        found_last = gather_doubled(after(last_shard, found_first[1]), size)
        turned = turn(activations)
        found[0] = after(found[0], turned)
        own = split_halves(found)
        pairs = gather_pairs(own, gather_near(own, size))
        far = gather_far(pairs, size)
        own_first = split_halves(doubled_planes(*found_first))
        far = after_all(far, *own_first)
        own_first = after_all(own_first, *far)
        inward = place(pairs, far, me)
        near_first = gather_near(own_first, size)
        inward = after(inward, *own_first)
    else:
        inward, mid_first, mid_last = [
            lax.all_gather(shard, "dp", axis=0, tiled=True)
            for shard in (inward_shard, first_shard, last_shard)
        ]
        turned = turn(activations)

    smalls = inward[:, 3 * width : 3 * width + per_row].astype(full).reshape(size, -1)
    heads_size, hidden_size = heads_bias.size, hidden_bias.size
    head_biases = (
        smalls[:, :heads_size].reshape(size, 2, -1).transpose(1, 2, 0).reshape(2, width)
    )
    hidden_biases = smalls[:, heads_size : heads_size + hidden_size].T.reshape(1, hidden_width)
    vectors = (
        smalls[:, heads_size + hidden_size :].reshape(size, 6, rows).transpose(1, 0, 2)
    ).reshape(6, D)

    live = lax.broadcasted_iota(jnp.int32, (count, LEN), 1) < lengths[:, None]
    scale = (token_weight.reshape(count, LEN) * live.astype(jnp.int32)).astype(full)
    scale = scale.reshape(tokens, 1)

    first_pair = attend(lengths, activations, inward, head_biases, 0, 1)
    if fast:
        near_first = after_all(near_first, first_pair[2])
        pairs_first = gather_pairs(own_first, near_first)
        far_first = gather_far(pairs_first, size)
        own_last = split_halves(doubled_planes(*after_all(found_last, *pairs_first)))
        near_last = gather_near(own_last, size)
        gated = after(activations, *pairs_first, *own_last, vectors, hidden_biases)
    else:
        gated = after(activations, first_pair[2])
    later_pairs = attend(lengths, gated, inward, head_biases, 1, groups - 1)
    contexts = [first_pair[2], later_pairs[2]]
    if fast:
        pairs_last = gather_pairs(own_last, after_all(near_last, later_pairs[2]))
        far_last = gather_far(pairs_last, size)
        mid_first = place(pairs_first, after_all(far_first, *pairs_last), me)

    mine = outward_part(contexts, mid_first, outward_at)
    total, active_first, slope_first, middle, normed, inverse = expand_first(
        mine, swap_cores(mine), activations, vectors, hidden_biases, mid_first
    )
    if fast:
        mid_last = place(pairs_last, after_all(far_last, total), me)
    mine_down, active_last, slope_last = expand_last(total, middle, hidden_biases, mid_last)
    (
        mine_middle, second_sums, hidden_sums, output_rows,
        second_grad, second_low, hidden_first, hidden_last,
    ) = contract(
        mine_down, swap_cores(mine_down), normed, cotangent, scale, vectors,
        (slope_first, slope_last), (mid_first, mid_last),
    )
    other_middle = swap_cores(mine_middle)
    actives, hiddens = (active_first, active_last), (hidden_first, hidden_last)

    def back_first(*gates):
        return first_back(
            after(mine_middle, *gates), other_middle, second_grad, normed, inverse, vectors,
            mid_first, outward_at, width,
        )

    def attention_grads(group, *gates):
        at = max(group - 1, 0)
        qkv, weights, _ = later_pairs if group else first_pair
        return attend_back(after(qkv, *gates), weights, at, context_grad, group)

    def heads_outgoing(sums):
        return jnp.concatenate(sums, axis=1).reshape(2, -1, size).transpose(2, 0, 1)

    def small_outgoing(first_sums, head_sums):
        norm_grad = jnp.concatenate([first_sums, second_sums])
        return jnp.concatenate(
            [
                heads_outgoing(head_sums).reshape(size, -1),
                hidden_sums.reshape(-1, size).T,
                norm_grad.reshape(6, size, rows).transpose(1, 0, 2).reshape(size, -1),
            ],
            axis=1,
        )

    stacked, head_sums = [], []
    if fast:
        sent_down, kept_down = weight_grad(second_low, actives, me, size, 0)
        got_down = hop(sent_down, 1, size)
        sent_up, kept_up = weight_grad(after(middle, sent_down), hiddens, me, size, 1)
        got_up = hop(sent_up, 2, size)
        first_sums, first_grad, first_low, context_grad = back_first(sent_up)

        sent_out, kept_out = weight_grad(first_low, contexts, me, size, 0)
        got_out = hop(sent_out, 1, size)

        def attention(group, *gates):
            grads, sums = attention_grads(group, *gates)
            stacked.append(grads)
            head_sums.append(sums)

        attention(0, sent_out)
        got_down = after(got_down, stacked[0])
        next_down = kept_down[1] + got_down[1]
        more_down = hop(next_down, 2, size)
        gated = after(turned, next_down)
        sent_0, kept_0 = weight_grad(gated, [stacked[0]], me, size, 1, True)
        got_0 = hop(sent_0, 2, size)
        got_up = after(got_up, sent_0)
        next_up = kept_up[1] + got_up[1]
        more_up = hop(next_up, 1, size)

        attention(1, next_up)
        more_down = after(more_down, stacked[1])
        own_down, out_down = combine([(kept_down, got_down, more_down)])
        near_down = hop(out_down, 4, size)
        gated = after(turned, out_down)
        sent_1, kept_1 = weight_grad(gated, [stacked[1]], me, size, 0, True)
        got_1 = hop(sent_1, 1, size)

        attention(2, sent_1)
        extras = (
            first_sums,
            second_sums,
            hidden_sums.reshape(2, rows, size).transpose(0, 2, 1).reshape(2, D),
            jnp.concatenate(head_sums, axis=1).reshape(rows, size).T.reshape(1, D),
        )
        got_out, got_0, more_up = after_all((got_out, got_0, more_up), stacked[2])
        next_out, next_0 = advance(kept_out, got_out, kept_0, got_0)
        more_out, more_0 = hop(next_out, 2, size), hop(next_0, 1, size)
        own_up, out_up = combine([(kept_up, got_up, after(more_up, next_out, next_0))])
        near_up = hop(out_up, 4, size)
        near_down = after(near_down, out_up)
        next_far = far_half(own_down, near_down)
        gated = after(turned, out_up, next_far)
        sent_2, kept_2 = weight_grad(gated, [stacked[2]], me, size, 1, True, extras)
        got_2 = hop(sent_2, 2, size)

        mine_source = source_part([after(stacked[0], sent_2)] + stacked[1:], inward)
        other_source = swap_cores(mine_source)
        far_down = hop(after(next_far, mine_source), 8, size)
        near_up, more_out, more_0, got_1, got_2 = after_all(
            (near_up, more_out, more_0, got_1, got_2), mine_source
        )
        own_near, out_near = combine([(kept_out, got_out, more_out), (kept_0, got_0, more_0)])
        near_near = hop(out_near, 4, size)
        next_far = far_half(own_up, after(near_up, out_near))
        far_up = hop(next_far, 8, size)
        got_1, got_2 = after_all((got_1, got_2), next_far)
        next_1, next_2 = advance(kept_1, got_1, kept_2, got_2)
        more_1, more_2 = hop(next_1, 2, size), hop(next_2, 1, size)
        near_near, far_down = after_all((near_near, far_down), next_1, next_2)
        next_far = far_half(own_near, near_near)
        far_near = hop(next_far, 8, size)
        more_1, more_2 = after_all((more_1, more_2), next_far)
        own_last, out_last = combine([(kept_1, got_1, more_1), (kept_2, got_2, more_2)])
        near_last = hop(out_last, 4, size)
        input_grad = finish(mine_source, after(other_source, out_last), first_grad)
        near_last = after(near_last, input_grad)
        far_last = hop(far_half(own_last, near_last), 8, size)
        downward_grad = reduce_sum(own_down, near_down, far_down)
        upward_grad = reduce_sum(own_up, near_up, far_up)
        near_grad = reduce_sum(own_near, near_near, far_near)
        far_grad = reduce_sum(own_last, near_last, far_last)
        outward_grad = near_grad[:, :width]
        cut = 3 * LANES
        inward_grads = [near_grad[:, width:], far_grad[:, :cut], far_grad[:, cut : 2 * cut]]
        small_grad = far_grad[:, 2 * cut :]
        small_grads = (
            small_grad[:, 8].reshape(heads_bias.shape),
            small_grad[:, 6:8].T.reshape(hidden_bias.shape),
            small_grad[:, :6].T,
        )
    else:

        def reduced(left, rights, turned=False):
            (value,) = weight_grad(left, rights, None, size, None, turned)
            return lax.psum_scatter(value, "dp", scatter_dimension=0, tiled=True)

        first_sums, first_grad, first_low, context_grad = back_first()
        downward_grad = reduced(second_low, actives)
        upward_grad = reduced(middle, hiddens)
        outward_grad = reduced(first_low, contexts)
        inward_grads = []
        for group in range(groups):
            grads, sums = attention_grads(group)
            stacked.append(grads)
            head_sums.append(sums)
            inward_grads.append(reduced(turned, [grads], True))
        mine_source = source_part(stacked, inward)
        small_grad = lax.psum_scatter(
            small_outgoing(first_sums, head_sums), "dp", scatter_dimension=0, tiled=True
        ).reshape(-1)
        small_grads = (
            small_grad[:heads_size].reshape(heads_bias.shape),
            small_grad[heads_size : heads_size + hidden_size].reshape(hidden_bias.shape),
            small_grad[heads_size + hidden_size :].reshape(norm_vectors.shape),
        )
        input_grad = finish(mine_source, swap_cores(mine_source), first_grad)

    inward_grad = jnp.stack(
        [
            jnp.concatenate(
                [grad[:, kind * LANES : (kind + 1) * LANES] for grad in inward_grads], axis=1
            )
            for kind in range(3)
        ]
    )
    grads = (
        inward_grad,
        outward_grad.T,
        upward_grad,
        downward_grad.T,
        *small_grads,
    )

    step_value = step_count[0].astype(full)
    correct = 1.0 - jnp.power(0.5, step_value)
    plan = (step_value + 4.0) / 12.0
    rates = (D ** (-0.5), (6 * D // LEN) ** (-0.5), D ** (-0.5), FF ** (-0.5), 0.5, 0.5, 0.3)
    decays = (0.01, 0.01, 0.01, 0.01, 0.0, 0.0, 0.0)
    masters = (
        inward_weight,
        output_weight,
        up_weight,
        down_weight,
        heads_bias,
        hidden_bias,
        norm_vectors,
    )
    results = [output_rows, input_grad]
    for at in range(7):
        results.extend(
            adamw(
                masters[at],
                grads[at],
                moments[at],
                moments[7 + at],
                rates[at] * plan,
                decays[at],
                correct,
            )
        )
    return tuple(results)


def solution(mesh):
    matrices = (
        P(None, "dp", "tensor"),
        P("tensor", "dp"),
        P("dp", "tensor"),
        P("tensor", "dp"),
        P(None, "tensor", "dp"),
        P("tensor", "dp"),
        P(None, "dp"),
    )
    in_specs = (
        (P("dp", None), P("dp", None), P("dp"), P("dp"), P()) + matrices + matrices + matrices
    )
    out_specs = (P("dp", None), P("dp", None)) + tuple(
        spec for spec in matrices for _ in range(3)
    )
    return jax.shard_map(
        per_device, mesh=mesh, in_specs=in_specs, out_specs=out_specs, check_vma=False
    )
```
